32 devices in a mesh: tm: 16 (over z, y, x), space: 2 (over core).
Axes of the slice: x: 2, y: 2, z: 4, core: 2. Of those that a mesh axis runs over, the one named last changes fastest.
Arguments:
- density: float32 [16, 256, 256], P('tm', 'space'), may hold values from 0.2 to 2
- flux_x: float32 [16, 256, 256], P('tm', 'space'), may hold values from -6 to 6
- flux_y: float32 [16, 256, 256], P('tm', 'space'), may hold values from -6 to 6
Outputs:
- density_out: float32 [16, 256, 256], P('tm', 'space')
- flux_x_out: float32 [16, 256, 256], P('tm', 'space')
- flux_y_out: float32 [16, 256, 256], P('tm', 'space')
The draws below stay inside these ranges and needn't reach their ends.
All inputs are finite; a program needn't handle non-finite values.
Results may differ from the reference program's by a relative error of at most 0.0004.
Values sent between devices are 32-bit elements; how exact they have to be, the bound alone decides.
A program may use at most 64 MiB of HBM per device.

```python
import math
import jax
import jax.numpy as jnp
from jax import lax

NS = 256
NEWTON = 4
NT = 16


def draw_density(key, part):
    logs = jax.random.uniform(key, (NT, NS, NS), jnp.float32, math.log(0.2), math.log(2.0))
    return jnp.clip(jnp.exp(logs), 0.2, 2.0).astype(jnp.float32)


def block_levels(own_key, dims, cuts, smallest, high):
    gain = 1.0
    for position, blocks in cuts:
        steps = jax.random.uniform(jax.random.fold_in(jax.random.fold_in(own_key, 6), position), (blocks,), jnp.float32, smallest / len(cuts), high / len(cuts))
        gain = gain * jnp.repeat(jnp.exp(steps), dims[position] // blocks).reshape((-1,) + (1,) * (len(dims) - 1 - position))
    return gain


def normal_values(own_key, shape, width, bound, cuts=(), kind=jnp.bfloat16):
    level = block_levels(own_key, shape, cuts, -0.22, 0.18) if cuts else 1.0
    drawn = jax.random.normal(own_key, shape, jnp.float32) * width * level
    return jnp.minimum(jnp.maximum(drawn, -bound), bound).astype(kind)


def setup_inputs(seed: int = 0) -> dict:
    seeds = jax.random.split(jax.random.key(seed), 4)
    density = draw_density(jax.random.fold_in(seeds[3], 71), 0)
    flux_x = normal_values(seeds[1], (NT, NS, NS), 1.0, 6.0, ((0, 16), (1, 2)), jnp.float32)
    flux_y = normal_values(seeds[2], (NT, NS, NS), 1.0, 6.0, ((0, 16), (1, 2)), jnp.float32)
    return dict(density=density, flux_x=flux_x, flux_y=flux_y)


prox_weight = 1.0
regular_shift = 0.0001
space_weight = 0.25
flux_weight = 0.5
highest = lax.Precision.HIGHEST

def kinetic_prox(density, flux_x, flux_y):
    square = flux_x * flux_x + flux_y * flux_y
    target = density + prox_weight + jnp.sqrt(square)
    for step in range(NEWTON):
        above = target + prox_weight
        value = (target - density) * above * above - 0.5 * prox_weight * square
        slope = above * (3.0 * target + prox_weight - 2.0 * density)
        target = target - value / slope
    shrink = target / (target + prox_weight)
    return (target, shrink * flux_x, shrink * flux_y)

def cosine_table(count):
    modes = jnp.arange(count).astype(jnp.float32)[:, None]
    points = jnp.arange(count).astype(jnp.float32)[None, :]
    table = jnp.cos(jnp.pi * modes * (2.0 * points + 1.0) / (2.0 * count))
    scales = jnp.where(modes == 0, jnp.sqrt(1.0 / count), jnp.sqrt(2.0 / count))
    return scales * table

def eigen_values(count):
    modes = jnp.arange(count).astype(jnp.float32)
    return 4.0 * jnp.sin(jnp.pi * modes / (2.0 * count)) ** 2

def divergence(field, axis):
    zeroed = jnp.moveaxis(field, axis, -1)
    zeroed = zeroed.at[..., -1].set(0.0)
    shifted = jnp.concatenate([jnp.zeros_like(zeroed[..., :1]), zeroed[..., :-1]], axis=-1)
    return jnp.moveaxis(zeroed - shifted, -1, axis)

def gradient(field, axis):
    moved = jnp.moveaxis(field, axis, -1)
    diffs = jnp.concatenate([moved[..., 1:] - moved[..., :-1], jnp.zeros_like(moved[..., :1])], axis=-1)
    return jnp.moveaxis(diffs, -1, axis)

def reference(density, flux_x, flux_y):
    rho, mom_x, mom_y = kinetic_prox(density, flux_x, flux_y)
    count = rho.shape[1]
    slices = rho.shape[0]
    before = jnp.concatenate([jnp.zeros_like(rho[:1]), rho[:-1]], axis=0)
    source = rho - before + flux_weight * (divergence(mom_x, 1) + divergence(mom_y, 2))
    table = cosine_table(count)
    halfway = jnp.einsum('ki,tij->tkj', table, source, precision=highest)
    modal = jnp.einsum('tkj,lj->tkl', halfway, table, precision=highest)
    lam = eigen_values(count)
    diag = 2.0 + regular_shift + space_weight * (lam[:, None] + lam[None, :])
    batch = modal.reshape(slices, count * count).T
    diag_full = jnp.broadcast_to(diag.reshape(count * count, 1), batch.shape)
    lower = -jnp.ones_like(batch)
    lower = lower.at[:, 0].set(0.0)
    upper = -jnp.ones_like(batch)
    upper = upper.at[:, -1].set(0.0)
    solved = lax.linalg.tridiagonal_solve(lower, diag_full, upper, batch[:, :, None])[:, :, 0]
    phihat = solved.T.reshape(slices, count, count)
    halfback = jnp.einsum('ki,tkl->til', table, phihat, precision=highest)
    potential = jnp.einsum('til,lj->tij', halfback, table, precision=highest)
    following = jnp.concatenate([potential[1:], jnp.zeros_like(potential[:1])], axis=0)
    density_out = rho - (potential - following)
    flux_x_out = mom_x - flux_weight * gradient(potential, 1)
    flux_y_out = mom_y - flux_weight * gradient(potential, 2)
    return (density_out, flux_x_out, flux_y_out)
```

```python
import jax
import jax.numpy as jnp
import numpy as np
from jax import lax
from jax.experimental import pallas as pl
from jax.experimental.pallas import tpu as pltpu
from jax.sharding import PartitionSpec as P

NEWTON = 4


prox_weight = 1.0
regular_shift = 0.0001
space_weight = 0.25
flux_weight = 0.5
highest = lax.Precision.HIGHEST


def swapped(block, axis, distance):
    count = lax.axis_size(axis)
    route = []
    for low in range(count):
        high = low | 1 << distance
        if high != low and high < count:
            route += [(low, high), (high, low)]
    return lax.ppermute(block, axis, route)


def shifted(array, axis, by):
    size = lax.axis_size(axis)
    pairs = [(i, i + by) for i in range(size) if 0 <= i + by < size]
    return lax.ppermute(array, axis, pairs)


def kinetic_prox(density, flux_x, flux_y):
    square = flux_x * flux_x + flux_y * flux_y
    target = density + prox_weight + jnp.sqrt(square)
    for step in range(NEWTON):
        above = target + prox_weight
        value = (target - density) * above * above - 0.5 * prox_weight * square
        slope = above * (3.0 * target + prox_weight - 2.0 * density)
        target = target - value / slope
    shrink = target / (target + prox_weight)
    return (target, shrink * flux_x, shrink * flux_y)


def cosine_table(count):
    modes = jnp.arange(count).astype(jnp.float32)[:, None]
    points = jnp.arange(count).astype(jnp.float32)[None, :]
    table = jnp.cos(jnp.pi * modes * (2.0 * points + 1.0) / (2.0 * count))
    scales = jnp.where(modes == 0, jnp.sqrt(1.0 / count), jnp.sqrt(2.0 / count))
    return scales * table


def eigen_values(count):
    modes = jnp.arange(count).astype(jnp.float32)
    return 4.0 * jnp.sin(jnp.pi * modes / (2.0 * count)) ** 2


def move_outward(stacked, bit):
    return swapped(stacked, "tm", bit)


def move_homeward(stacked, bit):
    return swapped(stacked, "tm", bit)


def butterfly(blocks, mover):
    total = lax.axis_size("tm")
    position = lax.axis_index("tm")
    bit_count = total.bit_length() - 1
    for bit in range(bit_count):
        higher = total >> bit + 1
        lowest = 1 << bit
        shaped = blocks.reshape((higher, 2, lowest) + blocks.shape[1:])
        own_bit = position >> bit & 1
        keeping = jnp.where(own_bit == 0, shaped[:, 0], shaped[:, 1])
        leaving = jnp.where(own_bit == 0, shaped[:, 1], shaped[:, 0])
        arrived = mover(leaving, bit)
        first_half = jnp.where(own_bit == 0, keeping, arrived)
        second_half = jnp.where(own_bit == 0, arrived, keeping)
        blocks = jnp.stack([first_half, second_half], axis=1).reshape(blocks.shape)
    return blocks


def per_device_xla(density, flux_x, flux_y):
    slabs = density.shape[0]
    rows_local = density.shape[1]
    count = density.shape[2]
    parts = lax.axis_size("space")
    modes_local = count // parts
    own_start = lax.axis_index("space") * rows_local
    mode_start = lax.axis_index("space") * modes_local
    rho, mom_x, mom_y = kinetic_prox(density, flux_x, flux_y)
    prior = shifted(rho[slabs - 1], "tm", 1)
    before = jnp.concatenate([prior[None], rho[:-1]], axis=0)
    zeroed = mom_y.at[:, :, count - 1].set(0.0)
    div_second = zeroed - jnp.concatenate(
        [jnp.zeros_like(zeroed[:, :, :1]), zeroed[:, :, :-1]], axis=2
    )
    partial_source = rho - before + flux_weight * div_second
    table = cosine_table(count)
    diff_table = jnp.concatenate(
        [table[:, :-1] - table[:, 1:], jnp.zeros_like(table[:, :1])], axis=1
    )
    stacked = jnp.concatenate([partial_source, flux_weight * mom_x], axis=1)
    column_modes = jnp.einsum("tij,kj->itk", stacked, table, precision=highest)
    left = lax.dynamic_slice(
        table, (0, own_start), (modes_local * lax.axis_size("space"), rows_local)
    )
    left_diff = lax.dynamic_slice(
        diff_table, (0, own_start), (modes_local * lax.axis_size("space"), rows_local)
    )
    both = jnp.concatenate([left, left_diff], axis=1)
    modal = lax.psum_scatter(
        jnp.einsum("ki,itj->ktj", both, column_modes, precision=highest),
        "space",
        scatter_dimension=0,
        tiled=True,
    )
    lam = eigen_values(count)
    lam_local = lax.dynamic_slice_in_dim(lam, mode_start, modes_local)
    coeff = 2.0 + regular_shift + space_weight * (lam_local[:, None] + lam[None, :])
    devices_tm = lax.axis_size("tm")
    position = lax.axis_index("tm")
    lines_local = modes_local * count
    line_group = lines_local // devices_tm
    steps_all = devices_tm * slabs
    outgoing = jnp.transpose(modal, (0, 2, 1)).reshape(devices_tm, line_group, slabs)
    incoming = butterfly(outgoing, move_outward)
    series = jnp.transpose(incoming, (1, 0, 2)).reshape(line_group, steps_all)
    line_coeff = lax.dynamic_slice_in_dim(
        coeff.reshape(lines_local), position * line_group, line_group
    )
    column = lax.broadcasted_iota(jnp.int32, (line_group, steps_all), 1)
    below_band = jnp.where(column == 0, 0.0, -1.0).astype(jnp.float32)
    above_band = jnp.where(column == steps_all - 1, 0.0, -1.0).astype(jnp.float32)
    middle_band = jnp.broadcast_to(line_coeff[:, None], (line_group, steps_all))
    solution = lax.linalg.tridiagonal_solve(
        below_band, middle_band, above_band, series[:, :, None]
    )[:, :, 0]
    blocked = solution.reshape(line_group, devices_tm, slabs)
    leading_next = jnp.concatenate(
        [solution[:, slabs::slabs], jnp.zeros((line_group, 1), jnp.float32)], axis=1
    )
    padded = jnp.concatenate([blocked, leading_next[:, :, None]], axis=2)
    returned = butterfly(jnp.transpose(padded, (1, 0, 2)), move_homeward)
    local_lines = returned.reshape(modes_local, count, slabs + 1)
    extended = jnp.transpose(local_lines, (0, 2, 1))
    phihat = extended[:, :slabs, :]
    left = lax.dynamic_slice(
        table, (mode_start, 0), (modes_local, rows_local * lax.axis_size("space"))
    )
    left_diff = lax.dynamic_slice(
        diff_table, (mode_start, 0), (modes_local, rows_local * lax.axis_size("space"))
    )
    values = jnp.einsum("ki,ktj->itj", left, extended, precision=highest)
    slopes = -jnp.einsum("ki,ktj->itj", left_diff, phihat, precision=highest)
    gathered = lax.psum_scatter(
        jnp.concatenate([values, slopes], axis=1), "space", scatter_dimension=0, tiled=True
    )
    physical = jnp.einsum("itk,kj->tij", gathered, table, precision=highest)
    potential = physical[: slabs + 1]
    grad_first = physical[slabs + 1 :]
    present = potential[:slabs]
    grad_second = jnp.concatenate(
        [present[:, :, 1:] - present[:, :, :-1], jnp.zeros_like(present[:, :, :1])], axis=2
    )
    density_out = rho - (present - potential[1:])
    flux_x_out = mom_x - flux_weight * grad_first
    flux_y_out = mom_y - flux_weight * grad_second
    return (density_out, flux_x_out, flux_y_out)


MESH = pl.DeviceIdType.MESH
CHUNKS = 1


def split_table(table):
    high = table.astype(jnp.bfloat16)
    low = (table - high.astype(np.float32)).astype(jnp.bfloat16)
    return np.stack([high, low], axis=-3)


def host_tables(count, solvers):
    modes = np.arange(count, dtype=np.float64)[:, None]
    points = np.arange(count, dtype=np.float64)[None, :]
    table = np.cos(np.pi * modes * (2.0 * points + 1.0) / (2.0 * count))
    table = table * np.where(modes == 0, np.sqrt(1.0 / count), np.sqrt(2.0 / count))
    lam = 4.0 * np.sin(np.pi * np.arange(count) / (2.0 * count)) ** 2
    coeff = 2.0 + regular_shift + space_weight * (lam[:, None] + lam[None, :])
    f32 = np.float32
    return (
        split_table(table.astype(f32)),
        split_table(table.T.astype(f32)),
        coeff.reshape(solvers, count // solvers, count).astype(f32),
    )


def parted(x):
    high = x.astype(jnp.bfloat16)
    return high, (x - high.astype(jnp.float32)).astype(jnp.bfloat16)


def mul(a, b):
    return jnp.dot(a, b, preferred_element_type=jnp.float32)


def mul_nt(a, b):
    return lax.dot_general(a, b, (((1,), (1,)), ((), ())), preferred_element_type=jnp.float32)


def by_table(x, table):
    high, low = parted(x)
    return mul(high, table[0]) + (mul(high, table[1]) + mul(low, table[0]))


def table_by(table, x):
    high, low = parted(x)
    return mul(table[0], high) + (mul(table[1], high) + mul(table[0], low))


def table_by_t(table, x):
    high, low = parted(x)
    return mul_nt(table[0], high) + (mul_nt(table[1], high) + mul_nt(table[0], low))


def step_kernel(
    total, density, flux_x, flux_y, cos, cos_t, coeff,
    rho, mx, my, fields, beyond_row,
    dv, xv, yv, cos_v, cos_t_v, coeff_v,
    halo, outgoing, incoming, pivots, steps, cut, phi, back, home, edge,
    load_sem, halo_sem, out_send, out_recv, cut_sem, back_send, back_recv, edge_sem,
):
    place = lax.axis_index("tm")
    half = place // total
    me = place - half * total
    base = half * total
    mirror = {"tm": lax.rem(place + total, 2 * total)}
    side = lax.axis_index("space")
    own = 2 * me + side
    rows, count = dv.shape
    group = coeff_v.shape[0]
    part = group // CHUNKS
    loads = [
        pltpu.make_async_copy(src, dst, load_sem.at[i])
        for i, (src, dst) in enumerate([
            (density.at[0], dv), (flux_x.at[0], xv), (flux_y.at[0], yv),
            (cos, cos_v), (coeff.at[own], coeff_v), (cos_t, cos_t_v),
        ])
    ]
    for load in loads:
        load.start()
    bits = [1 << i for i in range(total.bit_length() - 1)]
    flips = [bit * (1 - 2 * lax.rem(me // bit, 2)) for bit in bits]
    masks = sorted(range(total), key=lambda m: (-bin(m).count("1"), -m))
    peers = []
    for m in masks:
        chip = me + sum(f for f, bit in zip(flips, bits) if m & bit)
        for core in ([side] if m else []) + [1 - side]:
            peers.append((chip, core, 2 * chip + core))
    other = {"space": 1 - side}

    def device(peer):
        return {"tm": base + peer[0], "space": peer[1]}

    barrier = pltpu.get_barrier_semaphore()
    for peer in peers:
        pl.semaphore_signal(barrier, inc=1, device_id=device(peer), device_id_type=MESH)
    pl.semaphore_signal(barrier, inc=1, device_id=mirror, device_id_type=MESH)

    for load in loads[:3]:
        load.wait()
    tile = min(rows, 64)

    def prox(i, carry):
        span = pl.ds(pl.multiple_of(i * tile, tile), tile)
        r, fx, fy = dv[span], xv[span], yv[span]
        q, a, b = kinetic_prox(r, fx, fy)
        rho[span] = q
        mx[span] = a
        my[span] = b
        return carry

    lax.fori_loop(0, rows // tile, prox, 0)
    pl.semaphore_wait(barrier, 2 * total)
    row_halo = pltpu.make_async_remote_copy(
        src_ref=mx.at[pl.ds(rows - 8, 8)], dst_ref=halo, send_sem=halo_sem.at[0],
        recv_sem=halo_sem.at[1], device_id=other, device_id_type=MESH)
    row_halo.start()
    loads[3].wait()

    def outward(field, k, peer):
        return pltpu.make_async_remote_copy(
            src_ref=outgoing.at[field, peer[2], pl.ds(k * part, part)],
            dst_ref=incoming.at[k, field, me, side],
            send_sem=out_send.at[field, k, peer[2]], recv_sem=out_recv.at[field, k, own],
            device_id=device(peer), device_id_type=MESH)

    def arrival(field, k, peer):
        return pltpu.make_async_remote_copy(
            src_ref=outgoing.at[field, peer[2], pl.ds(k * part, part)],
            dst_ref=incoming.at[k, field, peer[0], peer[1]],
            send_sem=out_send.at[field, k, peer[2]], recv_sem=out_recv.at[field, k, peer[2]],
            device_id=device(peer), device_id_type=MESH)

    outgoing[0] = table_by_t(cos_v, rho[...]).reshape(2 * total, group, rows)
    for peer in peers:
        outward(0, 0, peer).start()
    row = lax.broadcasted_iota(jnp.int32, (rows, count), 0)
    col = lax.broadcasted_iota(jnp.int32, (rows, count), 1)
    last = side * rows + row == 2 * rows - 1
    wx = jnp.where(last, 0.0, mx[...])
    wy = jnp.where(col == count - 1, 0.0, my[...])
    row_halo.wait_recv()
    prior = jnp.where(jnp.full((1, count), side, jnp.int32) == 1, halo[7:8], 0.0)
    div = wx - jnp.where(row == 0, prior, pltpu.roll(wx, 1, 0)) + wy - pltpu.roll(wy, 1, 1)
    outgoing[1] = table_by_t(cos_v, flux_weight * div).reshape(2 * total, group, rows)
    for field, k in [(1, 0)] + [(f, k) for k in range(1, CHUNKS) for f in range(2)]:
        for peer in peers:
            outward(field, k, peer).start()
    for k in range(CHUNKS):
        for field in range(2):
            incoming[k, field, me, side] = outgoing[field, own, k * part:(k + 1) * part]
    loads[4].wait()
    c = coeff_v[...]
    pivot = 1.0 / c
    pivots[0] = pivot
    for t in range(1, total):
        pivot = 1.0 / (c - pivot)
        pivots[t] = pivot
    inverse = 1.0 / (1.0 - pivot * pivot)
    loads[5].wait()
    right = jnp.full((part, count), half, jnp.int32) == 1
    start, stride = half * (total - 1), 1 - 2 * half

    def swap(k):
        return pltpu.make_async_remote_copy(
            src_ref=cut.at[0, k], dst_ref=cut.at[1, k], send_sem=cut_sem.at[0, k],
            recv_sem=cut_sem.at[1, k], device_id=mirror, device_id_type=MESH)

    def homeward(k, peer):
        return pltpu.make_async_remote_copy(
            src_ref=back.at[k, peer[1], pl.ds(peer[0], 2)], dst_ref=home.at[k, own],
            send_sem=back_send.at[k, peer[2]], recv_sem=back_recv.at[k, own],
            device_id=device(peer), device_id_type=MESH)

    def landing(k, peer):
        return pltpu.make_async_remote_copy(
            src_ref=back.at[k, peer[1], pl.ds(peer[0], 2)], dst_ref=home.at[k, peer[2]],
            send_sem=back_send.at[k, peer[2]], recv_sem=back_recv.at[k, peer[2]],
            device_id=device(peer), device_id_type=MESH)

    ends = []
    for k in range(CHUNKS):
        span = slice(k * part, (k + 1) * part)
        for peer in reversed(peers):
            arrival(0, k, peer).wait_recv()
        for peer in reversed(peers):
            arrival(1, k, peer).wait_recv()
        slices = [
            [jnp.concatenate([incoming[k, f, t, 0], incoming[k, f, t, 1]], axis=1) for t in range(total)]
            for f in range(2)
        ]
        source = [slices[1][0] + slices[0][0]] + [
            slices[1][t] + (slices[0][t] - slices[0][t - 1]) for t in range(1, total)]
        modal = by_table(jnp.concatenate(source + [slices[0][total - 1]], axis=0), cos_t_v)
        steps[k] = modal[:total * part].reshape(total, part, count)
        value = jnp.zeros((part, count), jnp.float32)
        for i in range(total):
            value = (steps[k, start + stride * i] + value) * pivots[i, span]
            steps[k, start + stride * i] = value
        last_rho = jnp.where(right, 0.0, modal[total * part:])
        cut[0, k] = value - last_rho
        swap(k).start()
        ends.append((value, last_rho))
    for k in range(CHUNKS):
        span = slice(k * part, (k + 1) * part)
        value, last_rho = ends[k]
        swap(k).wait_recv()
        pivot = pivots[total - 1, span]
        beyond = cut[1, k] - pivot * last_rho
        value = (value + pivot * beyond) * inverse[span]
        phi[k, total] = jnp.where(right, 0.0, beyond + pivot * value)
        phi[k, start + stride * (total - 1)] = value
        for i in reversed(range(total - 1)):
            value = steps[k, start + stride * i] + pivots[i, span] * value
            phi[k, start + stride * i] = value
        halfback = by_table(phi[k].reshape((total + 1) * part, count), cos_v)
        back[k, 0] = halfback[:, :rows].reshape(total + 1, part, rows)
        back[k, 1] = halfback[:, rows:].reshape(total + 1, part, rows)
        for peer in peers:
            homeward(k, peer).start()
        home[k, own] = back[k, side, pl.ds(me, 2)]
    for k in range(CHUNKS):
        for peer in reversed(peers):
            landing(k, peer).wait_recv()

    def modes(field):
        return jnp.concatenate(
            [home[k, block, field] for block in range(2 * total) for k in range(CHUNKS)], axis=0)

    here = modes(0)
    both = jnp.concatenate([here, here - modes(1)], axis=1)
    values = table_by(cos_t_v, both)
    potential = values[:, :rows].T
    fields[0] = potential
    to_other = pltpu.make_async_remote_copy(
        src_ref=fields.at[0, pl.ds(0, 8)], dst_ref=edge, send_sem=edge_sem.at[0],
        recv_sem=edge_sem.at[1], device_id=other, device_id_type=MESH)
    to_other.start()
    fields[1] = values[:, rows:].T
    row_halo.wait_send()
    for k in range(CHUNKS):
        swap(k).wait_send()
        for peer in peers:
            outward(0, k, peer).wait_send()
            outward(1, k, peer).wait_send()
            homeward(k, peer).wait_send()
    to_other.wait()
    left = jnp.full((1, count), side, jnp.int32) == 0
    beyond_row[...] = jnp.broadcast_to(
        jnp.where(left, edge[0:1], potential[rows - 1:rows]), beyond_row.shape)


def finish_kernel(rho, mx, my, fields, beyond_row, out_d, out_x, out_y, res_d, res_x, res_y, store_sem):
    rows, count = rho.shape
    row = lax.broadcasted_iota(jnp.int32, (rows, count), 0)
    col = lax.broadcasted_iota(jnp.int32, (rows, count), 1)
    here = fields[0]
    after = jnp.where(row == rows - 1, beyond_row[0:1], pltpu.roll(here, rows - 1, 0))
    res_x[...] = mx[...] - flux_weight * (after - here)
    save_x = pltpu.make_async_copy(res_x, out_x.at[0], store_sem.at[0])
    save_x.start()
    grad = jnp.where(col == count - 1, 0.0, pltpu.roll(here, count - 1, 1) - here)
    res_y[...] = my[...] - flux_weight * grad
    save_y = pltpu.make_async_copy(res_y, out_y.at[0], store_sem.at[1])
    save_y.start()
    res_d[...] = rho[...] - fields[1]
    save_d = pltpu.make_async_copy(res_d, out_d.at[0], store_sem.at[2])
    save_d.start()
    for save in (save_x, save_y, save_d):
        save.wait()


def per_device_kernel(density, flux_x, flux_y):
    rows, count = density.shape[1:]
    total = lax.axis_size("tm") // 2
    solvers = 2 * total
    group = count // solvers
    part = group // CHUNKS
    tables = host_tables(count, solvers)
    f32, bf16 = jnp.float32, jnp.bfloat16
    vm = pltpu.VMEM
    dma = pltpu.SemaphoreType.DMA
    slab = vm((rows, count), f32)
    scratch = [slab] * 3 + [
        vm((2, count, count), bf16), vm((2, count, count), bf16), vm((group, count), f32),
        vm((8, count), f32),
        vm((2, solvers, group, rows), f32), vm((CHUNKS, 2, total, 2, part, rows), f32),
        vm((total, group, count), f32), vm((CHUNKS, total, part, count), f32),
        vm((2, CHUNKS, part, count), f32), vm((CHUNKS, total + 1, part, count), f32),
        vm((CHUNKS, 2, total + 1, part, rows), f32), vm((CHUNKS, solvers, 2, part, rows), f32),
        vm((8, count), f32),
        dma((6,)), dma((2,)), dma((2, CHUNKS, solvers)), dma((2, CHUNKS, solvers)),
        dma((2, CHUNKS)), dma((CHUNKS, solvers)), dma((CHUNKS, solvers)), dma((2,)),
    ]
    anywhere = pl.BlockSpec(memory_space=pl.ANY)

    def kernel(*refs):
        step_kernel(total, *refs)

    local = pl.BlockSpec(memory_space=pltpu.VMEM)
    held = pl.pallas_call(
        kernel,
        out_shape=[slab, slab, slab, vm((2, rows, count), f32), vm((8, count), f32)],
        in_specs=[anywhere] * 6,
        out_specs=[local] * 5,
        scratch_shapes=scratch,
        compiler_params=pltpu.CompilerParams(collective_id=0, has_side_effects=True),
    )(density, flux_x, flux_y, *tables)
    return pl.pallas_call(
        finish_kernel,
        out_shape=[jax.ShapeDtypeStruct(density.shape, f32)] * 3,
        in_specs=[local] * 5,
        out_specs=[anywhere] * 3,
        scratch_shapes=[slab, slab, slab, dma((3,))],
    )(*[pltpu.with_memory_space_constraint(x, pltpu.VMEM) for x in held])


def per_device(density, flux_x, flux_y):
    slabs, rows, count = density.shape
    size = lax.axis_size("tm")
    fits = (
        slabs == 1 and lax.axis_size("space") == 2 and size >= 2 and size & (size - 1) == 0
        and count % (8 * CHUNKS * size) == 0 and rows % 128 == 0 and 2 * rows == count
    )
    return (per_device_kernel if fits else per_device_xla)(density, flux_x, flux_y)


def solution(mesh):
    return jax.shard_map(
        per_device,
        mesh=mesh,
        in_specs=(P("tm", "space", None), P("tm", "space", None), P("tm", "space", None)),
        out_specs=(P("tm", "space", None), P("tm", "space", None), P("tm", "space", None)),
        check_vma=False,
    )
```

```python
import jax
import jax.numpy as jnp
import numpy as np
from jax import lax
from jax.experimental import pallas as pl
from jax.experimental.pallas import tpu as pltpu
from jax.sharding import PartitionSpec as P

NEWTON = 4


prox_weight = 1.0
regular_shift = 0.0001
space_weight = 0.25
flux_weight = 0.5
highest = lax.Precision.HIGHEST


def swapped(block, axis, distance):
    count = lax.axis_size(axis)
    route = []
    for low in range(count):
        high = low | 1 << distance
        if high != low and high < count:
            route += [(low, high), (high, low)]
    return lax.ppermute(block, axis, route)


def shifted(array, axis, by):
    size = lax.axis_size(axis)
    pairs = [(i, i + by) for i in range(size) if 0 <= i + by < size]
    return lax.ppermute(array, axis, pairs)


def kinetic_prox(density, flux_x, flux_y):
    square = flux_x * flux_x + flux_y * flux_y
    target = density + prox_weight + jnp.sqrt(square)
    for step in range(NEWTON):
        above = target + prox_weight
        value = (target - density) * above * above - 0.5 * prox_weight * square
        slope = above * (3.0 * target + prox_weight - 2.0 * density)
        target = target - value / slope
    shrink = target / (target + prox_weight)
    return (target, shrink * flux_x, shrink * flux_y)


def cosine_table(count):
    modes = jnp.arange(count).astype(jnp.float32)[:, None]
    points = jnp.arange(count).astype(jnp.float32)[None, :]
    table = jnp.cos(jnp.pi * modes * (2.0 * points + 1.0) / (2.0 * count))
    scales = jnp.where(modes == 0, jnp.sqrt(1.0 / count), jnp.sqrt(2.0 / count))
    return scales * table


def eigen_values(count):
    modes = jnp.arange(count).astype(jnp.float32)
    return 4.0 * jnp.sin(jnp.pi * modes / (2.0 * count)) ** 2


def move_outward(stacked, bit):
    return swapped(stacked, "tm", bit)


def move_homeward(stacked, bit):
    return swapped(stacked, "tm", bit)


def butterfly(blocks, mover):
    total = lax.axis_size("tm")
    position = lax.axis_index("tm")
    bit_count = total.bit_length() - 1
    for bit in range(bit_count):
        higher = total >> bit + 1
        lowest = 1 << bit
        shaped = blocks.reshape((higher, 2, lowest) + blocks.shape[1:])
        own_bit = position >> bit & 1
        keeping = jnp.where(own_bit == 0, shaped[:, 0], shaped[:, 1])
        leaving = jnp.where(own_bit == 0, shaped[:, 1], shaped[:, 0])
        arrived = mover(leaving, bit)
        first_half = jnp.where(own_bit == 0, keeping, arrived)
        second_half = jnp.where(own_bit == 0, arrived, keeping)
        blocks = jnp.stack([first_half, second_half], axis=1).reshape(blocks.shape)
    return blocks


def per_device_xla(density, flux_x, flux_y):
    slabs = density.shape[0]
    rows_local = density.shape[1]
    count = density.shape[2]
    parts = lax.axis_size("space")
    modes_local = count // parts
    own_start = lax.axis_index("space") * rows_local
    mode_start = lax.axis_index("space") * modes_local
    rho, mom_x, mom_y = kinetic_prox(density, flux_x, flux_y)
    prior = shifted(rho[slabs - 1], "tm", 1)
    before = jnp.concatenate([prior[None], rho[:-1]], axis=0)
    zeroed = mom_y.at[:, :, count - 1].set(0.0)
    div_second = zeroed - jnp.concatenate(
        [jnp.zeros_like(zeroed[:, :, :1]), zeroed[:, :, :-1]], axis=2
    )
    partial_source = rho - before + flux_weight * div_second
    table = cosine_table(count)
    diff_table = jnp.concatenate(
        [table[:, :-1] - table[:, 1:], jnp.zeros_like(table[:, :1])], axis=1
    )
    stacked = jnp.concatenate([partial_source, flux_weight * mom_x], axis=1)
    column_modes = jnp.einsum("tij,kj->itk", stacked, table, precision=highest)
    left = lax.dynamic_slice(
        table, (0, own_start), (modes_local * lax.axis_size("space"), rows_local)
    )
    left_diff = lax.dynamic_slice(
        diff_table, (0, own_start), (modes_local * lax.axis_size("space"), rows_local)
    )
    both = jnp.concatenate([left, left_diff], axis=1)
    modal = lax.psum_scatter(
        jnp.einsum("ki,itj->ktj", both, column_modes, precision=highest),
        "space",
        scatter_dimension=0,
        tiled=True,
    )
    lam = eigen_values(count)
    lam_local = lax.dynamic_slice_in_dim(lam, mode_start, modes_local)
    coeff = 2.0 + regular_shift + space_weight * (lam_local[:, None] + lam[None, :])
    devices_tm = lax.axis_size("tm")
    position = lax.axis_index("tm")
    lines_local = modes_local * count
    line_group = lines_local // devices_tm
    steps_all = devices_tm * slabs
    outgoing = jnp.transpose(modal, (0, 2, 1)).reshape(devices_tm, line_group, slabs)
    incoming = butterfly(outgoing, move_outward)
    series = jnp.transpose(incoming, (1, 0, 2)).reshape(line_group, steps_all)
    line_coeff = lax.dynamic_slice_in_dim(
        coeff.reshape(lines_local), position * line_group, line_group
    )
    column = lax.broadcasted_iota(jnp.int32, (line_group, steps_all), 1)
    below_band = jnp.where(column == 0, 0.0, -1.0).astype(jnp.float32)
    above_band = jnp.where(column == steps_all - 1, 0.0, -1.0).astype(jnp.float32)
    middle_band = jnp.broadcast_to(line_coeff[:, None], (line_group, steps_all))
    solution = lax.linalg.tridiagonal_solve(
        below_band, middle_band, above_band, series[:, :, None]
    )[:, :, 0]
    blocked = solution.reshape(line_group, devices_tm, slabs)
    leading_next = jnp.concatenate(
        [solution[:, slabs::slabs], jnp.zeros((line_group, 1), jnp.float32)], axis=1
    )
    padded = jnp.concatenate([blocked, leading_next[:, :, None]], axis=2)
    returned = butterfly(jnp.transpose(padded, (1, 0, 2)), move_homeward)
    local_lines = returned.reshape(modes_local, count, slabs + 1)
    extended = jnp.transpose(local_lines, (0, 2, 1))
    phihat = extended[:, :slabs, :]
    left = lax.dynamic_slice(
        table, (mode_start, 0), (modes_local, rows_local * lax.axis_size("space"))
    )
    left_diff = lax.dynamic_slice(
        diff_table, (mode_start, 0), (modes_local, rows_local * lax.axis_size("space"))
    )
    values = jnp.einsum("ki,ktj->itj", left, extended, precision=highest)
    slopes = -jnp.einsum("ki,ktj->itj", left_diff, phihat, precision=highest)
    gathered = lax.psum_scatter(
        jnp.concatenate([values, slopes], axis=1), "space", scatter_dimension=0, tiled=True
    )
    physical = jnp.einsum("itk,kj->tij", gathered, table, precision=highest)
    potential = physical[: slabs + 1]
    grad_first = physical[slabs + 1 :]
    present = potential[:slabs]
    grad_second = jnp.concatenate(
        [present[:, :, 1:] - present[:, :, :-1], jnp.zeros_like(present[:, :, :1])], axis=2
    )
    density_out = rho - (present - potential[1:])
    flux_x_out = mom_x - flux_weight * grad_first
    flux_y_out = mom_y - flux_weight * grad_second
    return (density_out, flux_x_out, flux_y_out)


MESH = pl.DeviceIdType.MESH


def split_table(table):
    high = table.astype(jnp.bfloat16)
    low = (table - high.astype(np.float32)).astype(jnp.bfloat16)
    return np.stack([high, low], axis=-3)


def host_tables(count, solvers):
    modes = np.arange(count, dtype=np.float64)[:, None]
    points = np.arange(count, dtype=np.float64)[None, :]
    table = np.cos(np.pi * modes * (2.0 * points + 1.0) / (2.0 * count))
    table = table * np.where(modes == 0, np.sqrt(1.0 / count), np.sqrt(2.0 / count))
    lam = 4.0 * np.sin(np.pi * np.arange(count) / (2.0 * count)) ** 2
    coeff = 2.0 + regular_shift + space_weight * (lam[:, None] + lam[None, :])
    f32 = np.float32
    return (
        split_table(table.astype(f32)),
        split_table(table.T.astype(f32)),
        coeff.reshape(solvers, count // solvers, count).astype(f32),
    )


def parted(x):
    high = x.astype(jnp.bfloat16)
    return high, (x - high.astype(jnp.float32)).astype(jnp.bfloat16)


def mul(a, b):
    return jnp.dot(a, b, preferred_element_type=jnp.float32)


def mul_nt(a, b):
    return lax.dot_general(a, b, (((1,), (1,)), ((), ())), preferred_element_type=jnp.float32)


def by_table(x, table):
    high, low = parted(x)
    return mul(high, table[0]) + (mul(high, table[1]) + mul(low, table[0]))


def table_by(table, x):
    high, low = parted(x)
    return mul(table[0], high) + (mul(table[1], high) + mul(table[0], low))


def table_by_t(table, x):
    high, low = parted(x)
    return mul_nt(table[0], high) + (mul_nt(table[1], high) + mul_nt(table[0], low))


def step_kernel(
    total, density, flux_x, flux_y, cos, cos_t, coeff,
    rho, mx, my, fields, beyond_row,
    dv, xv, yv, cos_v, cos_t_v, coeff_v,
    first_source, halo, outgoing, incoming, pivots, steps, cut, phi, back, home,
    load_sem, halo_sem, out_send, out_recv, cut_sem, back_send, back_recv,
):
    place = lax.axis_index("tm")
    half = place // total
    me = place - half * total
    base = half * total
    final = 2 * total - 1
    mirror = {"tm": lax.rem(place + total, 2 * total)}
    side = lax.axis_index("space")
    own = 2 * me + side
    rows, count = dv.shape
    group = coeff_v.shape[0]
    loads = [
        pltpu.make_async_copy(src, dst, load_sem.at[i])
        for i, (src, dst) in enumerate([
            (density.at[0], dv), (flux_x.at[0], xv), (flux_y.at[0], yv),
            (cos, cos_v), (coeff.at[own], coeff_v), (cos_t, cos_t_v),
        ])
    ]
    for load in loads:
        load.start()
    bits = [1 << i for i in range(total.bit_length() - 1)]
    flips = [bit * (1 - 2 * lax.rem(me // bit, 2)) for bit in bits]
    masks = sorted(range(total), key=lambda m: (-bin(m).count("1"), -m))
    peers = []
    for m in masks:
        chip = me + sum(f for f, bit in zip(flips, bits) if m & bit)
        for core in ([side] if m else []) + [1 - side]:
            peers.append((chip, core, 2 * chip + core))

    def device(peer):
        return {"tm": base + peer[0], "space": peer[1]}

    def choose(options):
        for test, action in options:
            pl.when(test)(action)

    barrier = pltpu.get_barrier_semaphore()
    for peer in peers:
        pl.semaphore_signal(barrier, inc=1, device_id=device(peer), device_id_type=MESH)
    pl.semaphore_signal(barrier, inc=1, device_id=mirror, device_id_type=MESH)
    for load in loads[:3]:
        load.wait()
    tile = min(rows, 64)

    def prox(i, carry):
        span = pl.ds(pl.multiple_of(i * tile, tile), tile)
        r, fx, fy = dv[span], xv[span], yv[span]
        q, a, b = kinetic_prox(r, fx, fy)
        rho[span] = q
        mx[span] = a
        my[span] = b
        return carry

    lax.fori_loop(0, rows // tile, prox, 0)
    row = lax.broadcasted_iota(jnp.int32, (rows, count), 0)
    col = lax.broadcasted_iota(jnp.int32, (rows, count), 1)
    lane = lax.broadcasted_iota(jnp.int32, (8, rows), 1)
    bottom = side * rows + row == 2 * rows - 1
    wx = jnp.where(bottom, 0.0, mx[...])
    wy = jnp.where(col == count - 1, 0.0, my[...])
    div = flux_weight * (
        wx - jnp.where(row == 0, 0.0, pltpu.roll(wx, 1, 0)) + wy - pltpu.roll(wy, 1, 1))
    crossing = jnp.broadcast_to(-flux_weight * wx[rows - 1:], (rows, count))
    whole = rho[...] + div
    closing = jnp.full((rows, count), place, jnp.int32) == final
    triple = jnp.concatenate(
        [jnp.where(closing, 0.0, rho[...]), jnp.where(closing, whole, div), crossing], axis=0)
    loads[3].wait()
    spread = table_by_t(cos_v, triple)
    for f in range(2):
        outgoing[:, f * group:(f + 1) * group] = spread[:, f * rows:(f + 1) * rows].reshape(
            2 * total, group, rows)
    tail = spread[:, 2 * rows:].reshape(2 * total, group, rows)
    packed = tail[:, :8]
    for m in range(1, group // 8):
        packed = jnp.where(lane[None] == m, tail[:, 8 * m:8 * m + 8], packed)
    outgoing[:, 2 * group:] = packed
    pl.semaphore_wait(barrier, 2 * total)

    def outward(peer, first, size):
        span = pl.ds(first, size)
        return pltpu.make_async_remote_copy(
            src_ref=outgoing.at[peer[2], span], dst_ref=incoming.at[me, side, span],
            send_sem=out_send.at[peer[2]], recv_sem=out_recv.at[own],
            device_id=device(peer), device_id_type=MESH)

    def arrival(peer, first, size):
        span = pl.ds(first, size)
        return pltpu.make_async_remote_copy(
            src_ref=outgoing.at[peer[2], span], dst_ref=incoming.at[peer[0], peer[1], span],
            send_sem=out_send.at[peer[2]], recv_sem=out_recv.at[peer[2]],
            device_id=device(peer), device_id_type=MESH)

    def out_kinds(chip, core, action):
        ending = chip == final
        inner = jnp.logical_not(ending)
        choose([
            (inner & (core == 0), lambda: action(0, 2 * group + 8)),
            (inner & (core == 1), lambda: action(0, 2 * group)),
            (ending & (core == 0), lambda: action(group, group + 8)),
            (ending & (core == 1), lambda: action(group, group)),
        ])

    def send_out(first, size):
        for peer in peers:
            outward(peer, first, size).start()

    out_kinds(place, side, send_out)

    row_halo = pltpu.make_async_remote_copy(
        src_ref=mx.at[pl.ds(rows - 8, 8)], dst_ref=halo, send_sem=halo_sem.at[0],
        recv_sem=halo_sem.at[1], device_id={"space": 1 - side}, device_id_type=MESH)

    @pl.when(place == 0)
    def _():
        row_halo.start()

    @pl.when(half == 1)
    def _():
        for core in range(2):
            incoming[total - 1, core, :group] = jnp.zeros((group, rows), jnp.float32)

    small = (place == 0) | (place == final)

    @pl.when(small)
    def _():
        for block in range(2 * total):
            home[block, 8 + group:] = jnp.zeros((group, rows), jnp.float32)

    incoming[me, side] = outgoing[own]
    loads[4].wait()
    c = coeff_v[...]
    pivot = 1.0 / c
    pivots[0] = pivot
    for t in range(1, total):
        pivot = 1.0 / (c - pivot)
        pivots[t] = pivot
    inverse = 1.0 / (1.0 - pivot * pivot)
    loads[5].wait()
    right = jnp.full((group, count), half, jnp.int32) == 1
    start, stride = half * (total - 1), 1 - 2 * half
    swap = pltpu.make_async_remote_copy(
        src_ref=cut.at[0], dst_ref=cut.at[1], send_sem=cut_sem.at[0],
        recv_sem=cut_sem.at[1], device_id=mirror, device_id_type=MESH)

    def homeward(peer, first, size):
        span = pl.ds(first, size)
        return pltpu.make_async_remote_copy(
            src_ref=back.at[peer[1], peer[0], span], dst_ref=home.at[own, span],
            send_sem=back_send.at[peer[2]], recv_sem=back_recv.at[own],
            device_id=device(peer), device_id_type=MESH)

    def landing(peer, first, size):
        span = pl.ds(first, size)
        return pltpu.make_async_remote_copy(
            src_ref=back.at[peer[1], peer[0], span], dst_ref=home.at[peer[2], span],
            send_sem=back_send.at[peer[2]], recv_sem=back_recv.at[peer[2]],
            device_id=device(peer), device_id_type=MESH)

    def back_kinds(chip, core, action):
        ending = (chip == 0) | (chip == final)
        inner = jnp.logical_not(ending)
        choose([
            (ending, lambda: action(0, 8 + group)),
            (inner & (core == 0), lambda: action(0, 8 + 2 * group)),
            (inner & (core == 1), lambda: action(8, 2 * group)),
        ])

    @pl.when(place == 0)
    def _():
        row_halo.wait()
        prior = jnp.where(jnp.full((1, count), side, jnp.int32) == 1, halo[7:], 0.0)
        first_source[...] = whole - jnp.where(row == 0, flux_weight * prior, 0.0)

    for peer in reversed(peers):
        out_kinds(base + peer[0], peer[1], lambda first, size: arrival(peer, first, size).wait_recv())

    def slices(t, f):
        return [incoming[t, core, f * group:(f + 1) * group] for core in range(2)]

    def beyond_halo(t):
        tail = incoming[t, 0, 2 * group:]
        turned = [tail] + [pltpu.roll(tail, rows - m, 1) for m in range(1, group // 8)]
        return jnp.concatenate([jnp.where(lane == 0, x, 0.0) for x in turned], axis=0)

    source = []
    for t in range(total):
        low, high = slices(t, 1)
        high = high + beyond_halo(t)
        now = slices(t, 0)
        if t > 0:
            now = [x - y for x, y in zip(now, slices(t - 1, 0))]
        source.append(jnp.concatenate([low + now[0], high + now[1]], axis=1))
    source.append(jnp.concatenate(slices(total - 1, 0), axis=1))
    modal = by_table(jnp.concatenate(source, axis=0), cos_t_v)
    steps[...] = modal[:total * group].reshape(total, group, count)
    value = jnp.zeros((group, count), jnp.float32)
    for i in range(total):
        value = (steps[start + stride * i] + value) * pivots[i]
        steps[start + stride * i] = value
    last_rho = jnp.where(right, 0.0, modal[total * group:])
    cut[0] = value - last_rho
    swap.start()

    def sent_out(first, size):
        for peer in peers:
            outward(peer, first, size).wait_send()

    out_kinds(place, side, sent_out)
    swap.wait()
    pivot = pivots[total - 1]
    beyond = cut[1] - pivot * last_rho
    value = (value + pivot * beyond) * inverse
    phi[total] = jnp.where(right, 0.0, beyond + pivot * value)
    phi[start + stride * (total - 1)] = value
    for i in reversed(range(total - 1)):
        value = steps[start + stride * i] + pivots[i] * value
        phi[start + stride * i] = value
    halfback = by_table(phi[...].reshape((total + 1) * group, count), cos_v)
    halves = [halfback[:, :rows], halfback[:, rows:]]
    for t in range(total + 1):
        for core in range(2):
            block = halves[core][t * group:(t + 1) * group]
            if t < total:
                back[core, t, 8:8 + group] = block
            if t > 0:
                back[core, t - 1, 8 + group:] = block
            if t < total and (core == 1 or t in (0, total - 1)):
                turn = 0 if core == 1 else 1
                near = None
                for m in range(group // 8):
                    x = block[8 * m:8 * m + 8]
                    x = pltpu.roll(x, m + turn, 1) if m + turn else x
                    near = x if near is None else jnp.where(lane == m, x, near)
                back[1 - core, t, :8] = near
    for core in range(2):
        @pl.when((half == 0) & (own != core))
        def _():
            homeward((0, core, core), 0, 8 + group).start()

    for peer in peers:
        @pl.when(base + peer[0] != 0)
        def _():
            back_kinds(base + peer[0], peer[1], lambda first, size: homeward(peer, first, size).start())

    home[own, :8 + group] = back[side, me, :8 + group]

    @pl.when(jnp.logical_not(small))
    def _():
        home[own, 8 + group:] = back[side, me, 8 + group:]

    def land(first, size):
        for peer in reversed(peers):
            landing(peer, first, size).wait_recv()

    for peer in peers:
        back_kinds(base + peer[0], peer[1], lambda first, size: homeward(peer, first, size).wait_send())
    back_kinds(place, side, land)

    def modes(first):
        return jnp.concatenate([home[block, first:first + group] for block in range(2 * total)], axis=0)

    def edges(block):
        tail = home[block, :8]
        return [tail] + [pltpu.roll(tail, rows - m, 1) for m in range(1, group // 8)]

    here = modes(8)
    near = jnp.concatenate([x for block in range(2 * total) for x in edges(block)], axis=0)
    upper = jnp.full((1, count), side, jnp.int32) == 0

    @pl.when(place != 0)
    def _():
        values = table_by(cos_t_v, jnp.concatenate([here, here - modes(8 + group), near], axis=1))
        pot = values[:, :rows].T
        edge = values[:, 2 * rows:].T[:1]
        fields[0] = pot
        fields[1] = values[:, rows:2 * rows].T
        beyond_row[...] = jnp.broadcast_to(jnp.where(upper, edge, pot[rows - 1:]), beyond_row.shape)

    @pl.when(place == 0)
    def _():
        values = table_by(cos_t_v, jnp.concatenate([here, near], axis=1))
        pot = values[:, :rows].T
        edge = values[:, rows:].T[:1]
        fields[0] = pot
        before_first = jnp.where(upper, pot[:1], edge)
        after_last = jnp.where(upper, edge, pot[rows - 1:])
        beyond_row[...] = jnp.broadcast_to(after_last, beyond_row.shape)
        left_of = jnp.where(col == 0, pot, pltpu.roll(pot, 1, 1))
        right_of = jnp.where(col == count - 1, pot, pltpu.roll(pot, count - 1, 1))
        over = jnp.where(row == 0, before_first, pltpu.roll(pot, 1, 0))
        under = jnp.where(row == rows - 1, after_last, pltpu.roll(pot, rows - 1, 0))
        bend = (pot - left_of) + (pot - right_of) + (pot - over) + (pot - under)
        following = (2.0 + regular_shift) * pot + space_weight * bend - first_source[...]
        fields[1] = pot - following


def finish_kernel(rho, mx, my, fields, beyond_row, out_d, out_x, out_y, res_d, res_x, res_y, store_sem):
    rows, count = rho.shape
    row = lax.broadcasted_iota(jnp.int32, (rows, count), 0)
    col = lax.broadcasted_iota(jnp.int32, (rows, count), 1)
    here = fields[0]
    after = jnp.where(row == rows - 1, beyond_row[0:1], pltpu.roll(here, rows - 1, 0))
    res_x[...] = mx[...] - flux_weight * (after - here)
    save_x = pltpu.make_async_copy(res_x, out_x.at[0], store_sem.at[0])
    save_x.start()
    grad = jnp.where(col == count - 1, 0.0, pltpu.roll(here, count - 1, 1) - here)
    res_y[...] = my[...] - flux_weight * grad
    save_y = pltpu.make_async_copy(res_y, out_y.at[0], store_sem.at[1])
    save_y.start()
    res_d[...] = rho[...] - fields[1]
    save_d = pltpu.make_async_copy(res_d, out_d.at[0], store_sem.at[2])
    save_d.start()
    for save in (save_x, save_y, save_d):
        save.wait()


def per_device_kernel(density, flux_x, flux_y):
    rows, count = density.shape[1:]
    total = lax.axis_size("tm") // 2
    solvers = 2 * total
    group = count // solvers
    tables = host_tables(count, solvers)
    f32, bf16 = jnp.float32, jnp.bfloat16
    vm = pltpu.VMEM
    dma = pltpu.SemaphoreType.DMA
    slab = vm((rows, count), f32)
    scratch = [slab] * 3 + [
        vm((2, count, count), bf16), vm((2, count, count), bf16), vm((group, count), f32),
        slab, vm((8, count), f32), vm((solvers, 2 * group + 8, rows), f32), vm((total, 2, 2 * group + 8, rows), f32),
        vm((total, group, count), f32), vm((total, group, count), f32),
        vm((2, group, count), f32), vm((total + 1, group, count), f32),
        vm((2, total, 8 + 2 * group, rows), f32), vm((solvers, 8 + 2 * group, rows), f32),
        dma((6,)), dma((2,)), dma((solvers,)), dma((solvers,)), dma((2,)), dma((solvers,)), dma((solvers,)),
    ]
    anywhere = pl.BlockSpec(memory_space=pl.ANY)

    def kernel(*refs):
        step_kernel(total, *refs)

    local = pl.BlockSpec(memory_space=pltpu.VMEM)
    held = pl.pallas_call(
        kernel,
        out_shape=[slab, slab, slab, vm((2, rows, count), f32), vm((8, count), f32)],
        in_specs=[anywhere] * 6,
        out_specs=[local] * 5,
        scratch_shapes=scratch,
        compiler_params=pltpu.CompilerParams(collective_id=0, has_side_effects=True),
    )(density, flux_x, flux_y, *tables)
    return pl.pallas_call(
        finish_kernel,
        out_shape=[jax.ShapeDtypeStruct(density.shape, f32)] * 3,
        in_specs=[local] * 5,
        out_specs=[anywhere] * 3,
        scratch_shapes=[slab, slab, slab, dma((3,))],
    )(*[pltpu.with_memory_space_constraint(x, pltpu.VMEM) for x in held])


def per_device(density, flux_x, flux_y):
    slabs, rows, count = density.shape
    size = lax.axis_size("tm")
    fits = (
        slabs == 1 and lax.axis_size("space") == 2 and size >= 2 and size & (size - 1) == 0
        and count % (8 * size) == 0 and rows % 128 == 0 and 2 * rows == count
    )
    return (per_device_kernel if fits else per_device_xla)(density, flux_x, flux_y)


def solution(mesh):
    return jax.shard_map(
        per_device,
        mesh=mesh,
        in_specs=(P("tm", "space", None), P("tm", "space", None), P("tm", "space", None)),
        out_specs=(P("tm", "space", None), P("tm", "space", None), P("tm", "space", None)),
        check_vma=False,
    )
```

```python
import jax
import jax.numpy as jnp
import numpy as np
from jax import lax
from jax.experimental import pallas as pl
from jax.experimental.pallas import tpu as pltpu
from jax.sharding import PartitionSpec as P

NEWTON = 4


prox_weight = 1.0
regular_shift = 0.0001
space_weight = 0.25
flux_weight = 0.5
highest = lax.Precision.HIGHEST


def swapped(block, axis, distance):
    count = lax.axis_size(axis)
    route = []
    for low in range(count):
        high = low | 1 << distance
        if high != low and high < count:
            route += [(low, high), (high, low)]
    return lax.ppermute(block, axis, route)


def shifted(array, axis, by):
    size = lax.axis_size(axis)
    pairs = [(i, i + by) for i in range(size) if 0 <= i + by < size]
    return lax.ppermute(array, axis, pairs)


def kinetic_prox(density, flux_x, flux_y):
    square = flux_x * flux_x + flux_y * flux_y
    target = density + prox_weight + jnp.sqrt(square)
    for step in range(NEWTON):
        above = target + prox_weight
        value = (target - density) * above * above - 0.5 * prox_weight * square
        slope = above * (3.0 * target + prox_weight - 2.0 * density)
        target = target - value / slope
    shrink = target / (target + prox_weight)
    return (target, shrink * flux_x, shrink * flux_y)


def cosine_table(count):
    modes = jnp.arange(count).astype(jnp.float32)[:, None]
    points = jnp.arange(count).astype(jnp.float32)[None, :]
    table = jnp.cos(jnp.pi * modes * (2.0 * points + 1.0) / (2.0 * count))
    scales = jnp.where(modes == 0, jnp.sqrt(1.0 / count), jnp.sqrt(2.0 / count))
    return scales * table


def eigen_values(count):
    modes = jnp.arange(count).astype(jnp.float32)
    return 4.0 * jnp.sin(jnp.pi * modes / (2.0 * count)) ** 2


def move_outward(stacked, bit):
    return swapped(stacked, "tm", bit)


def move_homeward(stacked, bit):
    return swapped(stacked, "tm", bit)


def butterfly(blocks, mover):
    total = lax.axis_size("tm")
    position = lax.axis_index("tm")
    bit_count = total.bit_length() - 1
    for bit in range(bit_count):
        higher = total >> bit + 1
        lowest = 1 << bit
        shaped = blocks.reshape((higher, 2, lowest) + blocks.shape[1:])
        own_bit = position >> bit & 1
        keeping = jnp.where(own_bit == 0, shaped[:, 0], shaped[:, 1])
        leaving = jnp.where(own_bit == 0, shaped[:, 1], shaped[:, 0])
        arrived = mover(leaving, bit)
        first_half = jnp.where(own_bit == 0, keeping, arrived)
        second_half = jnp.where(own_bit == 0, arrived, keeping)
        blocks = jnp.stack([first_half, second_half], axis=1).reshape(blocks.shape)
    return blocks


def per_device_xla(density, flux_x, flux_y):
    slabs = density.shape[0]
    rows_local = density.shape[1]
    count = density.shape[2]
    parts = lax.axis_size("space")
    modes_local = count // parts
    own_start = lax.axis_index("space") * rows_local
    mode_start = lax.axis_index("space") * modes_local
    rho, mom_x, mom_y = kinetic_prox(density, flux_x, flux_y)
    prior = shifted(rho[slabs - 1], "tm", 1)
    before = jnp.concatenate([prior[None], rho[:-1]], axis=0)
    zeroed = mom_y.at[:, :, count - 1].set(0.0)
    div_second = zeroed - jnp.concatenate(
        [jnp.zeros_like(zeroed[:, :, :1]), zeroed[:, :, :-1]], axis=2
    )
    partial_source = rho - before + flux_weight * div_second
    table = cosine_table(count)
    diff_table = jnp.concatenate(
        [table[:, :-1] - table[:, 1:], jnp.zeros_like(table[:, :1])], axis=1
    )
    stacked = jnp.concatenate([partial_source, flux_weight * mom_x], axis=1)
    column_modes = jnp.einsum("tij,kj->itk", stacked, table, precision=highest)
    left = lax.dynamic_slice(
        table, (0, own_start), (modes_local * lax.axis_size("space"), rows_local)
    )
    left_diff = lax.dynamic_slice(
        diff_table, (0, own_start), (modes_local * lax.axis_size("space"), rows_local)
    )
    both = jnp.concatenate([left, left_diff], axis=1)
    modal = lax.psum_scatter(
        jnp.einsum("ki,itj->ktj", both, column_modes, precision=highest),
        "space",
        scatter_dimension=0,
        tiled=True,
    )
    lam = eigen_values(count)
    lam_local = lax.dynamic_slice_in_dim(lam, mode_start, modes_local)
    coeff = 2.0 + regular_shift + space_weight * (lam_local[:, None] + lam[None, :])
    devices_tm = lax.axis_size("tm")
    position = lax.axis_index("tm")
    lines_local = modes_local * count
    line_group = lines_local // devices_tm
    steps_all = devices_tm * slabs
    outgoing = jnp.transpose(modal, (0, 2, 1)).reshape(devices_tm, line_group, slabs)
    incoming = butterfly(outgoing, move_outward)
    series = jnp.transpose(incoming, (1, 0, 2)).reshape(line_group, steps_all)
    line_coeff = lax.dynamic_slice_in_dim(
        coeff.reshape(lines_local), position * line_group, line_group
    )
    column = lax.broadcasted_iota(jnp.int32, (line_group, steps_all), 1)
    below_band = jnp.where(column == 0, 0.0, -1.0).astype(jnp.float32)
    above_band = jnp.where(column == steps_all - 1, 0.0, -1.0).astype(jnp.float32)
    middle_band = jnp.broadcast_to(line_coeff[:, None], (line_group, steps_all))
    solution = lax.linalg.tridiagonal_solve(
        below_band, middle_band, above_band, series[:, :, None]
    )[:, :, 0]
    blocked = solution.reshape(line_group, devices_tm, slabs)
    leading_next = jnp.concatenate(
        [solution[:, slabs::slabs], jnp.zeros((line_group, 1), jnp.float32)], axis=1
    )
    padded = jnp.concatenate([blocked, leading_next[:, :, None]], axis=2)
    returned = butterfly(jnp.transpose(padded, (1, 0, 2)), move_homeward)
    local_lines = returned.reshape(modes_local, count, slabs + 1)
    extended = jnp.transpose(local_lines, (0, 2, 1))
    phihat = extended[:, :slabs, :]
    left = lax.dynamic_slice(
        table, (mode_start, 0), (modes_local, rows_local * lax.axis_size("space"))
    )
    left_diff = lax.dynamic_slice(
        diff_table, (mode_start, 0), (modes_local, rows_local * lax.axis_size("space"))
    )
    values = jnp.einsum("ki,ktj->itj", left, extended, precision=highest)
    slopes = -jnp.einsum("ki,ktj->itj", left_diff, phihat, precision=highest)
    gathered = lax.psum_scatter(
        jnp.concatenate([values, slopes], axis=1), "space", scatter_dimension=0, tiled=True
    )
    physical = jnp.einsum("itk,kj->tij", gathered, table, precision=highest)
    potential = physical[: slabs + 1]
    grad_first = physical[slabs + 1 :]
    present = potential[:slabs]
    grad_second = jnp.concatenate(
        [present[:, :, 1:] - present[:, :, :-1], jnp.zeros_like(present[:, :, :1])], axis=2
    )
    density_out = rho - (present - potential[1:])
    flux_x_out = mom_x - flux_weight * grad_first
    flux_y_out = mom_y - flux_weight * grad_second
    return (density_out, flux_x_out, flux_y_out)


MESH = pl.DeviceIdType.MESH


def split_table(table):
    high = table.astype(jnp.bfloat16)
    low = (table - high.astype(np.float32)).astype(jnp.bfloat16)
    return np.stack([high, low], axis=-3)


def host_tables(count, solvers):
    modes = np.arange(count, dtype=np.float64)[:, None]
    points = np.arange(count, dtype=np.float64)[None, :]
    table = np.cos(np.pi * modes * (2.0 * points + 1.0) / (2.0 * count))
    table = table * np.where(modes == 0, np.sqrt(1.0 / count), np.sqrt(2.0 / count))
    lam = 4.0 * np.sin(np.pi * np.arange(count) / (2.0 * count)) ** 2
    coeff = 2.0 + regular_shift + space_weight * (lam[:, None] + lam[None, :])
    f32 = np.float32
    return (
        split_table(table.astype(f32)),
        split_table(table.T.astype(f32)),
        coeff.reshape(solvers, count // solvers, count).astype(f32),
    )


def parted(x):
    high = x.astype(jnp.bfloat16)
    return high, (x - high.astype(jnp.float32)).astype(jnp.bfloat16)


def mul(a, b):
    return jnp.dot(a, b, preferred_element_type=jnp.float32)


def mul_nt(a, b):
    return lax.dot_general(a, b, (((1,), (1,)), ((), ())), preferred_element_type=jnp.float32)


def by_table(x, table):
    high, low = parted(x)
    return mul(high, table[0]) + (mul(high, table[1]) + mul(low, table[0]))


def table_by(table, x):
    high, low = parted(x)
    return mul(table[0], high) + (mul(table[1], high) + mul(table[0], low))


def table_by_t(table, x):
    high, low = parted(x)
    return mul_nt(table[0], high) + (mul_nt(table[1], high) + mul_nt(table[0], low))


def step_kernel(
    total, density, flux_x, flux_y, cos, cos_t, coeff,
    rho, mx, my, fields, beyond_row,
    inputs, cos_v, cos_t_v, coeff_v,
    first_source, halo, outgoing, incoming, pivots, steps, cut, phi, back, home,
    load_sem, halo_sem, out_sem, cut_sem, back_sem,
):
    place = lax.axis_index("tm")
    half = place // total
    me = place - half * total
    base = half * total
    final = 2 * total - 1
    mirror = {"tm": lax.rem(place + total, 2 * total)}
    side = lax.axis_index("space")
    own = 2 * me + side
    rows, count = rho.shape
    group = coeff_v.shape[0]
    out_rows, back_rows = 2 * group + 8, 2 * group + 8
    feeds = [
        pltpu.make_async_copy(src.at[0], inputs.at[i], load_sem.at[0])
        for i, src in enumerate((density, flux_x, flux_y))
    ]
    loads = [
        pltpu.make_async_copy(src, dst, load_sem.at[i])
        for i, (src, dst) in enumerate([(cos, cos_v), (coeff.at[own], coeff_v), (cos_t, cos_t_v)], 1)
    ]
    for load in feeds + loads:
        load.start()

    def settle(ref, size, sem):
        span = ref.at[pl.ds(0, size)]
        pltpu.make_async_copy(span, span, sem).wait()

    bits = [1 << i for i in range(total.bit_length() - 1)]
    flips = [bit * (1 - 2 * lax.rem(me // bit, 2)) for bit in bits]
    masks = sorted(range(total), key=lambda m: (-bin(m).count("1"), -m))
    peers = []
    for m in masks:
        chip = me + sum(f for f, bit in zip(flips, bits) if m & bit)
        for core in ([side] if m else []) + [1 - side]:
            peers.append((chip, core, 2 * chip + core))

    def device(peer):
        return {"tm": base + peer[0], "space": peer[1]}

    def choose(options):
        for test, action in options:
            pl.when(test)(action)

    barrier = pltpu.get_barrier_semaphore()
    for peer in peers:
        pl.semaphore_signal(barrier, inc=1, device_id=device(peer), device_id_type=MESH)
    pl.semaphore_signal(barrier, inc=1, device_id=mirror, device_id_type=MESH)
    settle(inputs, 3, load_sem.at[0])
    tile = min(rows, 64)

    def prox(i, carry):
        span = pl.ds(pl.multiple_of(i * tile, tile), tile)
        r, fx, fy = inputs[0, span], inputs[1, span], inputs[2, span]
        q, a, b = kinetic_prox(r, fx, fy)
        rho[span] = q
        mx[span] = a
        my[span] = b
        return carry

    lax.fori_loop(0, rows // tile, prox, 0)
    row = lax.broadcasted_iota(jnp.int32, (rows, count), 0)
    col = lax.broadcasted_iota(jnp.int32, (rows, count), 1)
    lane = lax.broadcasted_iota(jnp.int32, (8, rows), 1)
    bottom = side * rows + row == 2 * rows - 1
    wx = jnp.where(bottom, 0.0, mx[...])
    wy = jnp.where(col == count - 1, 0.0, my[...])
    div = flux_weight * (
        wx - jnp.where(row == 0, 0.0, pltpu.roll(wx, 1, 0)) + wy - pltpu.roll(wy, 1, 1))
    crossing = jnp.broadcast_to(-flux_weight * wx[rows - 1:], (rows, count))
    whole = rho[...] + div
    closing = jnp.full((rows, count), place, jnp.int32) == final
    triple = jnp.concatenate(
        [jnp.where(closing, 0.0, rho[...]), jnp.where(closing, whole, div), crossing], axis=0)
    loads[0].wait()
    spread = table_by_t(cos_v, triple)
    for block in range(2 * total):
        span = slice(block * group, (block + 1) * group)
        first = block * out_rows
        for f in range(2):
            outgoing[first + f * group:first + (f + 1) * group] = spread[span, f * rows:(f + 1) * rows]
        tail = spread[span, 2 * rows:]
        packed = tail[:8]
        for m in range(1, group // 8):
            packed = jnp.where(lane == m, tail[8 * m:8 * m + 8], packed)
        outgoing[first + 2 * group:first + out_rows] = packed
    pl.semaphore_wait(barrier, 2 * total)

    def place_of(block, first, size):
        return pl.ds(pl.multiple_of(block * out_rows + first, 8), size)

    def outward(peer, first, size):
        return pltpu.make_async_remote_copy(
            src_ref=outgoing.at[place_of(peer[2], first, size)],
            dst_ref=incoming.at[place_of(own, first, size)],
            send_sem=out_sem.at[0], recv_sem=out_sem.at[1],
            device_id=device(peer), device_id_type=MESH)

    def out_kinds(chip, core, action):
        ending = chip == final
        inner = jnp.logical_not(ending)
        choose([
            (inner & (core == 0), lambda: action(0, 2 * group + 8)),
            (inner & (core == 1), lambda: action(0, 2 * group)),
            (ending & (core == 0), lambda: action(group, group + 8)),
            (ending & (core == 1), lambda: action(group, group)),
        ])

    def send_out(first, size):
        for peer in peers:
            outward(peer, first, size).start()

    out_kinds(place, side, send_out)

    row_halo = pltpu.make_async_remote_copy(
        src_ref=mx.at[pl.ds(rows - 8, 8)], dst_ref=halo, send_sem=halo_sem.at[0],
        recv_sem=halo_sem.at[1], device_id={"space": 1 - side}, device_id_type=MESH)

    @pl.when(place == 0)
    def _():
        row_halo.start()

    @pl.when(half == 1)
    def _():
        for block in (2 * total - 2, 2 * total - 1):
            incoming[pl.ds(block * out_rows, group)] = jnp.zeros((group, rows), jnp.float32)

    small = (place == 0) | (place == final)

    @pl.when(small)
    def _():
        for block in range(2 * total):
            home[pl.ds(block * back_rows + 8 + group, group)] = jnp.zeros((group, rows), jnp.float32)

    incoming[place_of(own, 0, out_rows)] = outgoing[place_of(own, 0, out_rows)]
    loads[1].wait()
    c = coeff_v[...]
    pivot = 1.0 / c
    pivots[0] = pivot
    for t in range(1, total):
        pivot = 1.0 / (c - pivot)
        pivots[t] = pivot
    inverse = 1.0 / (1.0 - pivot * pivot)
    loads[2].wait()
    right = jnp.full((group, count), half, jnp.int32) == 1
    start, stride = half * (total - 1), 1 - 2 * half
    swap = pltpu.make_async_remote_copy(
        src_ref=cut.at[0], dst_ref=cut.at[1], send_sem=cut_sem.at[0],
        recv_sem=cut_sem.at[1], device_id=mirror, device_id_type=MESH)

    def homeward(peer, first, size):
        return pltpu.make_async_remote_copy(
            src_ref=back.at[peer[1], place_of(peer[0], first, size)], dst_ref=home.at[place_of(own, first, size)],
            send_sem=back_sem.at[0], recv_sem=back_sem.at[1],
            device_id=device(peer), device_id_type=MESH)

    def back_kinds(chip, core, action):
        ending = (chip == 0) | (chip == final)
        inner = jnp.logical_not(ending)
        choose([
            (ending, lambda: action(0, 8 + group)),
            (inner & (core == 0), lambda: action(0, 8 + 2 * group)),
            (inner & (core == 1), lambda: action(8, 2 * group)),
        ])

    @pl.when(place == 0)
    def _():
        row_halo.wait()
        prior = jnp.where(jnp.full((1, count), side, jnp.int32) == 1, halo[7:], 0.0)
        first_source[...] = whole - jnp.where(row == 0, flux_weight * prior, 0.0)

    everything = total * (4 * group + 8)
    pl.when(half == 0)(lambda: out_kinds(
        place, side, lambda first, size: settle(incoming, everything - size, out_sem.at[1])))
    pl.when(half == 1)(lambda: out_kinds(
        place, side, lambda first, size: settle(incoming, everything - 2 * group - size, out_sem.at[1])))

    def slices(t, f):
        firsts = [(2 * t + core) * out_rows + f * group for core in range(2)]
        return [incoming[first:first + group] for first in firsts]

    def beyond_halo(t):
        tail = incoming[2 * t * out_rows + 2 * group:(2 * t + 1) * out_rows]
        turned = [tail] + [pltpu.roll(tail, rows - m, 1) for m in range(1, group // 8)]
        return jnp.concatenate([jnp.where(lane == 0, x, 0.0) for x in turned], axis=0)

    source = []
    for t in range(total):
        low, high = slices(t, 1)
        high = high + beyond_halo(t)
        now = slices(t, 0)
        if t > 0:
            now = [x - y for x, y in zip(now, slices(t - 1, 0))]
        source.append(jnp.concatenate([low + now[0], high + now[1]], axis=1))
    source.append(jnp.concatenate(slices(total - 1, 0), axis=1))
    modal = by_table(jnp.concatenate(source, axis=0), cos_t_v)
    steps[...] = modal[:total * group].reshape(total, group, count)
    value = jnp.zeros((group, count), jnp.float32)
    for i in range(total):
        value = (steps[start + stride * i] + value) * pivots[i]
        steps[start + stride * i] = value
    last_rho = jnp.where(right, 0.0, modal[total * group:])
    cut[0] = value - last_rho
    swap.start()

    out_kinds(place, side, lambda first, size: settle(outgoing, (2 * total - 1) * size, out_sem.at[0]))
    swap.wait()
    pivot = pivots[total - 1]
    beyond = cut[1] - pivot * last_rho
    value = (value + pivot * beyond) * inverse
    phi[total] = jnp.where(right, 0.0, beyond + pivot * value)
    phi[start + stride * (total - 1)] = value
    for i in reversed(range(total - 1)):
        value = steps[start + stride * i] + pivots[i] * value
        phi[start + stride * i] = value
    halfback = by_table(phi[...].reshape((total + 1) * group, count), cos_v)
    halves = [halfback[:, :rows], halfback[:, rows:]]
    for t in range(total + 1):
        for core in range(2):
            block = halves[core][t * group:(t + 1) * group]
            if t < total:
                back[core, t * back_rows + 8:t * back_rows + 8 + group] = block
            if t > 0:
                back[core, t * back_rows - group:t * back_rows] = block
            if t < total and (core == 1 or t in (0, total - 1)):
                turn = 0 if core == 1 else 1
                near = None
                for m in range(group // 8):
                    x = block[8 * m:8 * m + 8]
                    x = pltpu.roll(x, m + turn, 1) if m + turn else x
                    near = x if near is None else jnp.where(lane == m, x, near)
                back[1 - core, t * back_rows:t * back_rows + 8] = near
    for core in range(2):
        @pl.when((half == 0) & (own != core))
        def _():
            homeward((0, core, core), 0, 8 + group).start()

    for peer in peers:
        @pl.when(base + peer[0] != 0)
        def _():
            back_kinds(base + peer[0], peer[1], lambda first, size: homeward(peer, first, size).start())

    home[place_of(own, 0, 8 + group)] = back[side, place_of(me, 0, 8 + group)]

    @pl.when(jnp.logical_not(small))
    def _():
        home[place_of(own, 8 + group, group)] = back[side, place_of(me, 8 + group, group)]

    returned = 2 * (8 + group) + (total - 1) * (8 + 4 * group)
    back_kinds(place, side, lambda first, size: settle(home, returned - size, back_sem.at[0]))
    back_kinds(place, side, lambda first, size: settle(home, (2 * total - 1) * size, back_sem.at[1]))

    def modes(first):
        spans = [block * back_rows + first for block in range(2 * total)]
        return jnp.concatenate([home[at:at + group] for at in spans], axis=0)

    def edges(block):
        tail = home[block * back_rows:block * back_rows + 8]
        return [tail] + [pltpu.roll(tail, rows - m, 1) for m in range(1, group // 8)]

    here = modes(8)
    near = jnp.concatenate([x for block in range(2 * total) for x in edges(block)], axis=0)
    upper = jnp.full((1, count), side, jnp.int32) == 0

    @pl.when(place != 0)
    def _():
        values = table_by(cos_t_v, jnp.concatenate([here, here - modes(8 + group), near], axis=1))
        pot = values[:, :rows].T
        edge = values[:, 2 * rows:].T[:1]
        fields[0] = pot
        fields[1] = values[:, rows:2 * rows].T
        beyond_row[...] = jnp.broadcast_to(jnp.where(upper, edge, pot[rows - 1:]), beyond_row.shape)

    @pl.when(place == 0)
    def _():
        values = table_by(cos_t_v, jnp.concatenate([here, near], axis=1))
        pot = values[:, :rows].T
        edge = values[:, rows:].T[:1]
        fields[0] = pot
        before_first = jnp.where(upper, pot[:1], edge)
        after_last = jnp.where(upper, edge, pot[rows - 1:])
        beyond_row[...] = jnp.broadcast_to(after_last, beyond_row.shape)
        left_of = jnp.where(col == 0, pot, pltpu.roll(pot, 1, 1))
        right_of = jnp.where(col == count - 1, pot, pltpu.roll(pot, count - 1, 1))
        over = jnp.where(row == 0, before_first, pltpu.roll(pot, 1, 0))
        under = jnp.where(row == rows - 1, after_last, pltpu.roll(pot, rows - 1, 0))
        bend = (pot - left_of) + (pot - right_of) + (pot - over) + (pot - under)
        following = (2.0 + regular_shift) * pot + space_weight * bend - first_source[...]
        fields[1] = pot - following


def finish_kernel(rho, mx, my, fields, beyond_row, out_d, out_x, out_y, res_d, res_x, res_y, store_sem):
    rows, count = rho.shape
    row = lax.broadcasted_iota(jnp.int32, (rows, count), 0)
    col = lax.broadcasted_iota(jnp.int32, (rows, count), 1)
    here = fields[0]
    after = jnp.where(row == rows - 1, beyond_row[0:1], pltpu.roll(here, rows - 1, 0))
    res_x[...] = mx[...] - flux_weight * (after - here)
    save_x = pltpu.make_async_copy(res_x, out_x.at[0], store_sem.at[0])
    save_x.start()
    grad = jnp.where(col == count - 1, 0.0, pltpu.roll(here, count - 1, 1) - here)
    res_y[...] = my[...] - flux_weight * grad
    save_y = pltpu.make_async_copy(res_y, out_y.at[0], store_sem.at[1])
    save_y.start()
    res_d[...] = rho[...] - fields[1]
    save_d = pltpu.make_async_copy(res_d, out_d.at[0], store_sem.at[2])
    save_d.start()
    for save in (save_x, save_y, save_d):
        save.wait()


def per_device_kernel(density, flux_x, flux_y):
    rows, count = density.shape[1:]
    total = lax.axis_size("tm") // 2
    solvers = 2 * total
    group = count // solvers
    tables = host_tables(count, solvers)
    f32, bf16 = jnp.float32, jnp.bfloat16
    vm = pltpu.VMEM
    dma = pltpu.SemaphoreType.DMA
    slab = vm((rows, count), f32)
    tall = solvers * (2 * group + 8)
    scratch = [
        vm((3, rows, count), f32), vm((2, count, count), bf16), vm((2, count, count), bf16), vm((group, count), f32),
        slab, vm((8, count), f32), vm((tall, rows), f32), vm((tall, rows), f32),
        vm((total, group, count), f32), vm((total, group, count), f32),
        vm((2, group, count), f32), vm((total + 1, group, count), f32),
        vm((2, total * (2 * group + 8), rows), f32), vm((tall, rows), f32),
        dma((4,)), dma((2,)), dma((2,)), dma((2,)), dma((2,)),
    ]
    anywhere = pl.BlockSpec(memory_space=pl.ANY)

    def kernel(*refs):
        step_kernel(total, *refs)

    local = pl.BlockSpec(memory_space=pltpu.VMEM)
    held = pl.pallas_call(
        kernel,
        out_shape=[slab, slab, slab, vm((2, rows, count), f32), vm((8, count), f32)],
        in_specs=[anywhere] * 6,
        out_specs=[local] * 5,
        scratch_shapes=scratch,
        compiler_params=pltpu.CompilerParams(collective_id=0, has_side_effects=True),
    )(density, flux_x, flux_y, *tables)
    return pl.pallas_call(
        finish_kernel,
        out_shape=[jax.ShapeDtypeStruct(density.shape, f32)] * 3,
        in_specs=[local] * 5,
        out_specs=[anywhere] * 3,
        scratch_shapes=[slab, slab, slab, dma((3,))],
    )(*[pltpu.with_memory_space_constraint(x, pltpu.VMEM) for x in held])


def per_device(density, flux_x, flux_y):
    slabs, rows, count = density.shape
    size = lax.axis_size("tm")
    fits = (
        slabs == 1 and lax.axis_size("space") == 2 and size >= 2 and size & (size - 1) == 0
        and count % (8 * size) == 0 and rows % 128 == 0 and 2 * rows == count
    )
    return (per_device_kernel if fits else per_device_xla)(density, flux_x, flux_y)


def solution(mesh):
    return jax.shard_map(
        per_device,
        mesh=mesh,
        in_specs=(P("tm", "space", None), P("tm", "space", None), P("tm", "space", None)),
        out_specs=(P("tm", "space", None), P("tm", "space", None), P("tm", "space", None)),
        check_vma=False,
    )
```

```python
import jax
import jax.numpy as jnp
import numpy as np
from jax import lax
from jax.experimental import pallas as pl
from jax.experimental.pallas import tpu as pltpu
from jax.sharding import PartitionSpec as P

NEWTON = 4


prox_weight = 1.0
regular_shift = 0.0001
space_weight = 0.25
flux_weight = 0.5
highest = lax.Precision.HIGHEST


def swapped(block, axis, distance):
    count = lax.axis_size(axis)
    route = []
    for low in range(count):
        high = low | 1 << distance
        if high != low and high < count:
            route += [(low, high), (high, low)]
    return lax.ppermute(block, axis, route)


def shifted(array, axis, by):
    size = lax.axis_size(axis)
    pairs = [(i, i + by) for i in range(size) if 0 <= i + by < size]
    return lax.ppermute(array, axis, pairs)


def kinetic_prox(density, flux_x, flux_y):
    square = flux_x * flux_x + flux_y * flux_y
    target = density + prox_weight + jnp.sqrt(square)
    for step in range(NEWTON):
        above = target + prox_weight
        value = (target - density) * above * above - 0.5 * prox_weight * square
        slope = above * (3.0 * target + prox_weight - 2.0 * density)
        target = target - value / slope
    shrink = target / (target + prox_weight)
    return (target, shrink * flux_x, shrink * flux_y)


def cosine_table(count):
    modes = jnp.arange(count).astype(jnp.float32)[:, None]
    points = jnp.arange(count).astype(jnp.float32)[None, :]
    table = jnp.cos(jnp.pi * modes * (2.0 * points + 1.0) / (2.0 * count))
    scales = jnp.where(modes == 0, jnp.sqrt(1.0 / count), jnp.sqrt(2.0 / count))
    return scales * table


def eigen_values(count):
    modes = jnp.arange(count).astype(jnp.float32)
    return 4.0 * jnp.sin(jnp.pi * modes / (2.0 * count)) ** 2


def move_outward(stacked, bit):
    return swapped(stacked, "tm", bit)


def move_homeward(stacked, bit):
    return swapped(stacked, "tm", bit)


def butterfly(blocks, mover):
    total = lax.axis_size("tm")
    position = lax.axis_index("tm")
    bit_count = total.bit_length() - 1
    for bit in range(bit_count):
        higher = total >> bit + 1
        lowest = 1 << bit
        shaped = blocks.reshape((higher, 2, lowest) + blocks.shape[1:])
        own_bit = position >> bit & 1
        keeping = jnp.where(own_bit == 0, shaped[:, 0], shaped[:, 1])
        leaving = jnp.where(own_bit == 0, shaped[:, 1], shaped[:, 0])
        arrived = mover(leaving, bit)
        first_half = jnp.where(own_bit == 0, keeping, arrived)
        second_half = jnp.where(own_bit == 0, arrived, keeping)
        blocks = jnp.stack([first_half, second_half], axis=1).reshape(blocks.shape)
    return blocks


def per_device_xla(density, flux_x, flux_y):
    slabs = density.shape[0]
    rows_local = density.shape[1]
    count = density.shape[2]
    parts = lax.axis_size("space")
    modes_local = count // parts
    own_start = lax.axis_index("space") * rows_local
    mode_start = lax.axis_index("space") * modes_local
    rho, mom_x, mom_y = kinetic_prox(density, flux_x, flux_y)
    prior = shifted(rho[slabs - 1], "tm", 1)
    before = jnp.concatenate([prior[None], rho[:-1]], axis=0)
    zeroed = mom_y.at[:, :, count - 1].set(0.0)
    div_second = zeroed - jnp.concatenate(
        [jnp.zeros_like(zeroed[:, :, :1]), zeroed[:, :, :-1]], axis=2
    )
    partial_source = rho - before + flux_weight * div_second
    table = cosine_table(count)
    diff_table = jnp.concatenate(
        [table[:, :-1] - table[:, 1:], jnp.zeros_like(table[:, :1])], axis=1
    )
    stacked = jnp.concatenate([partial_source, flux_weight * mom_x], axis=1)
    column_modes = jnp.einsum("tij,kj->itk", stacked, table, precision=highest)
    left = lax.dynamic_slice(
        table, (0, own_start), (modes_local * lax.axis_size("space"), rows_local)
    )
    left_diff = lax.dynamic_slice(
        diff_table, (0, own_start), (modes_local * lax.axis_size("space"), rows_local)
    )
    both = jnp.concatenate([left, left_diff], axis=1)
    modal = lax.psum_scatter(
        jnp.einsum("ki,itj->ktj", both, column_modes, precision=highest),
        "space",
        scatter_dimension=0,
        tiled=True,
    )
    lam = eigen_values(count)
    lam_local = lax.dynamic_slice_in_dim(lam, mode_start, modes_local)
    coeff = 2.0 + regular_shift + space_weight * (lam_local[:, None] + lam[None, :])
    devices_tm = lax.axis_size("tm")
    position = lax.axis_index("tm")
    lines_local = modes_local * count
    line_group = lines_local // devices_tm
    steps_all = devices_tm * slabs
    outgoing = jnp.transpose(modal, (0, 2, 1)).reshape(devices_tm, line_group, slabs)
    incoming = butterfly(outgoing, move_outward)
    series = jnp.transpose(incoming, (1, 0, 2)).reshape(line_group, steps_all)
    line_coeff = lax.dynamic_slice_in_dim(
        coeff.reshape(lines_local), position * line_group, line_group
    )
    column = lax.broadcasted_iota(jnp.int32, (line_group, steps_all), 1)
    below_band = jnp.where(column == 0, 0.0, -1.0).astype(jnp.float32)
    above_band = jnp.where(column == steps_all - 1, 0.0, -1.0).astype(jnp.float32)
    middle_band = jnp.broadcast_to(line_coeff[:, None], (line_group, steps_all))
    solution = lax.linalg.tridiagonal_solve(
        below_band, middle_band, above_band, series[:, :, None]
    )[:, :, 0]
    blocked = solution.reshape(line_group, devices_tm, slabs)
    leading_next = jnp.concatenate(
        [solution[:, slabs::slabs], jnp.zeros((line_group, 1), jnp.float32)], axis=1
    )
    padded = jnp.concatenate([blocked, leading_next[:, :, None]], axis=2)
    returned = butterfly(jnp.transpose(padded, (1, 0, 2)), move_homeward)
    local_lines = returned.reshape(modes_local, count, slabs + 1)
    extended = jnp.transpose(local_lines, (0, 2, 1))
    phihat = extended[:, :slabs, :]
    left = lax.dynamic_slice(
        table, (mode_start, 0), (modes_local, rows_local * lax.axis_size("space"))
    )
    left_diff = lax.dynamic_slice(
        diff_table, (mode_start, 0), (modes_local, rows_local * lax.axis_size("space"))
    )
    values = jnp.einsum("ki,ktj->itj", left, extended, precision=highest)
    slopes = -jnp.einsum("ki,ktj->itj", left_diff, phihat, precision=highest)
    gathered = lax.psum_scatter(
        jnp.concatenate([values, slopes], axis=1), "space", scatter_dimension=0, tiled=True
    )
    physical = jnp.einsum("itk,kj->tij", gathered, table, precision=highest)
    potential = physical[: slabs + 1]
    grad_first = physical[slabs + 1 :]
    present = potential[:slabs]
    grad_second = jnp.concatenate(
        [present[:, :, 1:] - present[:, :, :-1], jnp.zeros_like(present[:, :, :1])], axis=2
    )
    density_out = rho - (present - potential[1:])
    flux_x_out = mom_x - flux_weight * grad_first
    flux_y_out = mom_y - flux_weight * grad_second
    return (density_out, flux_x_out, flux_y_out)


MESH = pl.DeviceIdType.MESH


def split_table(table):
    high = table.astype(jnp.bfloat16)
    low = (table - high.astype(np.float32)).astype(jnp.bfloat16)
    return np.stack([high, low], axis=-3)


def host_tables(count, solvers):
    modes = np.arange(count, dtype=np.float64)[:, None]
    points = np.arange(count, dtype=np.float64)[None, :]
    table = np.cos(np.pi * modes * (2.0 * points + 1.0) / (2.0 * count))
    table = table * np.where(modes == 0, np.sqrt(1.0 / count), np.sqrt(2.0 / count))
    lam = 4.0 * np.sin(np.pi * np.arange(count) / (2.0 * count)) ** 2
    coeff = 2.0 + regular_shift + space_weight * (lam[:, None] + lam[None, :])
    f32 = np.float32
    return (
        split_table(table.astype(f32)),
        split_table(table.T.astype(f32)),
        coeff.reshape(solvers, count // solvers, count).astype(f32),
    )


def parted(x):
    high = x.astype(jnp.bfloat16)
    return high, (x - high.astype(jnp.float32)).astype(jnp.bfloat16)


def mul(a, b):
    return jnp.dot(a, b, preferred_element_type=jnp.float32)


def mul_nt(a, b):
    return lax.dot_general(a, b, (((1,), (1,)), ((), ())), preferred_element_type=jnp.float32)


def by_table(x, table):
    high, low = parted(x)
    return mul(high, table[0]) + (mul(high, table[1]) + mul(low, table[0]))


def table_by(table, x):
    high, low = parted(x)
    return mul(table[0], high) + (mul(table[1], high) + mul(table[0], low))


def table_by_t(table, x):
    high, low = parted(x)
    return mul_nt(table[0], high) + (mul_nt(table[1], high) + mul_nt(table[0], low))


def by_table_t(x, table):
    high, low = parted(x)
    return mul_nt(high, table[0]) + (mul_nt(high, table[1]) + mul_nt(low, table[0]))


def step_kernel(
    total, density, flux_x, flux_y, cos, cos_t, coeff,
    rho, mx, my, fields, beyond_row,
    inputs, cos_v, cos_t_v, coeff_v,
    first_source, halo, outgoing, incoming, pivots, steps, cut, phi, back, home,
    load_sem, halo_sem, out_sem, cut_sem, back_sem,
):
    place = lax.axis_index("tm")
    half = place // total
    me = place - half * total
    base = half * total
    final = 2 * total - 1
    mirror = {"tm": lax.rem(place + total, 2 * total)}
    side = lax.axis_index("space")
    own = 2 * me + side
    rows, count = rho.shape
    group = coeff_v.shape[0]
    stride_rows, filled = 2 * group + 8, 2 * group + 1
    pieces = inputs.shape[0]
    tile = rows // pieces
    feeds = [
        pltpu.make_async_copy(src.at[0, pl.ds(j * tile, tile)], inputs.at[j, i], load_sem.at[j])
        for j in range(pieces) for i, src in enumerate((density, flux_x, flux_y))
    ]
    loads = [
        pltpu.make_async_copy(src, dst, load_sem.at[i])
        for i, (src, dst) in enumerate([(cos, cos_v), (coeff.at[own], coeff_v), (cos_t, cos_t_v)], pieces)
    ]
    for load in feeds + loads:
        load.start()

    def settle(ref, size, sem):
        span = ref.at[pl.ds(0, size)]
        pltpu.make_async_copy(span, span, sem).wait()

    bits = [1 << i for i in range(total.bit_length() - 1)]
    flips = [bit * (1 - 2 * lax.rem(me // bit, 2)) for bit in bits]
    masks = sorted(range(total), key=lambda m: (-bin(m).count("1"), -m))
    peers = []
    for m in masks:
        chip = me + sum(f for f, bit in zip(flips, bits) if m & bit)
        for core in ([side] if m else []) + [1 - side]:
            peers.append((chip, core, 2 * chip + core))

    def device(peer):
        return {"tm": base + peer[0], "space": peer[1]}

    def choose(options):
        for test, action in options:
            pl.when(test)(action)

    barrier = pltpu.get_barrier_semaphore()
    for peer in peers:
        pl.semaphore_signal(barrier, inc=1, device_id=device(peer), device_id_type=MESH)
    pl.semaphore_signal(barrier, inc=1, device_id=mirror, device_id_type=MESH)
    for j in range(pieces):
        settle(inputs.at[j], 3, load_sem.at[j])
        span = slice(j * tile, (j + 1) * tile)
        rho[span], mx[span], my[span] = kinetic_prox(inputs[j, 0], inputs[j, 1], inputs[j, 2])

    row = lax.broadcasted_iota(jnp.int32, (rows, count), 0)
    col = lax.broadcasted_iota(jnp.int32, (rows, count), 1)
    bottom = side * rows + row == 2 * rows - 1
    wx = jnp.where(bottom, 0.0, mx[...])
    wy = jnp.where(col == count - 1, 0.0, my[...])
    div = flux_weight * (
        wx - jnp.where(row == 0, 0.0, pltpu.roll(wx, 1, 0)) + wy - pltpu.roll(wy, 1, 1))
    whole = rho[...] + div
    closing = jnp.full((rows, count), place, jnp.int32) == final
    pair = jnp.concatenate(
        [jnp.where(closing, 0.0, rho[...]), jnp.where(closing, whole, div)], axis=0)
    loads[0].wait()
    spread = table_by_t(cos_v, pair)
    crossing = by_table_t(jnp.broadcast_to(-flux_weight * wx[rows - 1:], (8, count)), cos_v)
    for block in range(2 * total):
        span = slice(block * group, (block + 1) * group)
        first = block * stride_rows
        for f in range(2):
            outgoing[first + f * group:first + (f + 1) * group] = spread[span, f * rows:(f + 1) * rows]
        part = block // total * rows
        outgoing[first + 2 * group:first + filled] = crossing[:1, part:part + rows]
    pl.semaphore_wait(barrier, 2 * total)

    def place_of(block, first, size):
        return pl.ds(pl.multiple_of(block * stride_rows + first, 8), size)

    def outward(peer, first, size):
        return pltpu.make_async_remote_copy(
            src_ref=outgoing.at[place_of(peer[2], first, size)],
            dst_ref=incoming.at[place_of(own, first, size)],
            send_sem=out_sem.at[0], recv_sem=out_sem.at[1],
            device_id=device(peer), device_id_type=MESH)

    def out_kinds(chip, core, action):
        ending = chip == final
        inner = jnp.logical_not(ending)
        choose([
            (inner & (core == 0), lambda: action(0, filled)),
            (inner & (core == 1), lambda: action(0, 2 * group)),
            (ending & (core == 0), lambda: action(group, group + 1)),
            (ending & (core == 1), lambda: action(group, group)),
        ])

    def send_out(first, size):
        for peer in peers:
            outward(peer, first, size).start()

    out_kinds(place, side, send_out)

    row_halo = pltpu.make_async_remote_copy(
        src_ref=mx.at[pl.ds(rows - 8, 8)], dst_ref=halo, send_sem=halo_sem.at[0],
        recv_sem=halo_sem.at[1], device_id={"space": 1 - side}, device_id_type=MESH)

    @pl.when(place == 0)
    def _():
        row_halo.start()

    @pl.when(half == 1)
    def _():
        for block in (2 * total - 2, 2 * total - 1):
            incoming[pl.ds(block * stride_rows, group)] = jnp.zeros((group, rows), jnp.float32)

    small = (place == 0) | (place == final)

    @pl.when(small)
    def _():
        for block in range(2 * total):
            home[pl.ds(block * stride_rows, group)] = jnp.zeros((group, rows), jnp.float32)

    incoming[place_of(own, 0, stride_rows)] = outgoing[place_of(own, 0, stride_rows)]
    loads[1].wait()
    c = coeff_v[...]
    pivot = 1.0 / c
    pivots[0] = pivot
    for t in range(1, total):
        pivot = 1.0 / (c - pivot)
        pivots[t] = pivot
    inverse = 1.0 / (1.0 - pivot * pivot)
    loads[2].wait()
    right = jnp.full((group, count), half, jnp.int32) == 1
    start, stride = half * (total - 1), 1 - 2 * half
    swap = pltpu.make_async_remote_copy(
        src_ref=cut.at[0], dst_ref=cut.at[1], send_sem=cut_sem.at[0],
        recv_sem=cut_sem.at[1], device_id=mirror, device_id_type=MESH)

    def homeward(peer, first, size):
        return pltpu.make_async_remote_copy(
            src_ref=back.at[peer[1], place_of(peer[0], first, size)], dst_ref=home.at[place_of(own, first, size)],
            send_sem=back_sem.at[0], recv_sem=back_sem.at[1],
            device_id=device(peer), device_id_type=MESH)

    def back_kinds(chip, core, action):
        ending = (chip == 0) | (chip == final)
        inner = jnp.logical_not(ending)
        choose([
            (ending, lambda: action(group, group + 1)),
            (inner & (core == 0), lambda: action(0, filled)),
            (inner & (core == 1), lambda: action(0, 2 * group)),
        ])

    @pl.when(place == 0)
    def _():
        row_halo.wait()
        prior = jnp.where(jnp.full((1, count), side, jnp.int32) == 1, halo[7:], 0.0)
        first_source[...] = whole - jnp.where(row == 0, flux_weight * prior, 0.0)

    everything = total * (filled + 2 * group)
    pl.when(half == 0)(lambda: out_kinds(
        place, side, lambda first, size: settle(incoming, everything - size, out_sem.at[1])))
    pl.when(half == 1)(lambda: out_kinds(
        place, side, lambda first, size: settle(incoming, everything - 2 * group - size, out_sem.at[1])))

    def slices(t, f):
        firsts = [(2 * t + core) * stride_rows + f * group for core in range(2)]
        return [incoming[first:first + group] for first in firsts]

    shares = incoming[pl.ds(2 * group, total, stride=2 * stride_rows)]
    lanes = lax.broadcasted_iota(jnp.int32, (group, rows), 1)
    picked = lanes == lax.rem(own, total) * group + lax.broadcasted_iota(jnp.int32, (group, rows), 0)

    def beyond_halo(t):
        mine = jnp.where(picked, jnp.broadcast_to(shares[t:t + 1], (group, rows)), 0.0)
        return jnp.where(lanes == 0, jnp.sum(mine, axis=1, keepdims=True), 0.0)

    source = []
    for t in range(total):
        low, high = slices(t, 1)
        high = high + beyond_halo(t)
        now = slices(t, 0)
        if t > 0:
            now = [x - y for x, y in zip(now, slices(t - 1, 0))]
        source.append(jnp.concatenate([low + now[0], high + now[1]], axis=1))
    source.append(jnp.concatenate(slices(total - 1, 0), axis=1))
    modal = by_table(jnp.concatenate(source, axis=0), cos_t_v)
    steps[...] = modal[:total * group].reshape(total, group, count)
    value = jnp.zeros((group, count), jnp.float32)
    for i in range(total):
        value = (steps[start + stride * i] + value) * pivots[i]
        steps[start + stride * i] = value
    last_rho = jnp.where(right, 0.0, modal[total * group:])
    cut[0] = value - last_rho
    swap.start()

    out_kinds(place, side, lambda first, size: settle(outgoing, (2 * total - 1) * size, out_sem.at[0]))
    swap.wait()
    pivot = pivots[total - 1]
    beyond = cut[1] - pivot * last_rho
    value = (value + pivot * beyond) * inverse
    phi[total] = jnp.where(right, 0.0, beyond + pivot * value)
    phi[start + stride * (total - 1)] = value
    for i in reversed(range(total - 1)):
        value = steps[start + stride * i] + pivots[i] * value
        phi[start + stride * i] = value
    lines = phi[...].reshape((total + 1) * group, count)
    halfback = by_table(lines, cos_v)
    halves = [halfback[:, :rows], halfback[:, rows:]]
    brink = table_by_t(cos_t_v[:, rows - 8:rows + 8], lines[:total * group])
    for t in range(total + 1):
        for core in range(2):
            block = halves[core][t * group:(t + 1) * group]
            if t < total:
                first = t * stride_rows
                back[core, first + group:first + 2 * group] = block
                back[core, first + 2 * group:first + filled] = brink[8 - core:9 - core]
            if t > 0:
                first = (t - 1) * stride_rows
                back[core, first:first + group] = block
    for core in range(2):
        @pl.when((half == 0) & (own != core))
        def _():
            homeward((0, core, core), group, group + 1).start()

    for peer in peers:
        @pl.when(base + peer[0] != 0)
        def _():
            back_kinds(base + peer[0], peer[1], lambda first, size: homeward(peer, first, size).start())

    home[place_of(own, group, group + 8)] = back[side, place_of(me, group, group + 8)]

    @pl.when(jnp.logical_not(small))
    def _():
        home[place_of(own, 0, group)] = back[side, place_of(me, 0, group)]

    returned = 2 * (group + 1) + (total - 1) * (filled + 2 * group)
    back_kinds(place, side, lambda first, size: settle(home, returned - size, back_sem.at[0]))
    back_kinds(place, side, lambda first, size: settle(home, (2 * total - 1) * size, back_sem.at[1]))

    def modes(first):
        spans = [block * stride_rows + first for block in range(2 * total)]
        return jnp.concatenate([home[at:at + group] for at in spans], axis=0)

    here = modes(group)
    offset = lax.rem(total - me, total) * group
    row8 = lax.broadcasted_iota(jnp.int32, (total, rows), 0)
    lane8 = lax.broadcasted_iota(jnp.int32, (total, rows), 1)
    strip = []
    for part in range(2):
        tail = home[pl.ds(part * total * stride_rows + 2 * group, total, stride=stride_rows)]
        tail = jnp.where(lane8 < group, pltpu.roll(tail, offset, 1), 0.0)
        tail = sum(jnp.where(row8 == d, pltpu.roll(tail, d * group, 1) if d else tail, 0.0) for d in range(total))
        strip.append(jnp.broadcast_to(jnp.sum(tail, axis=0, keepdims=True), (8, rows)))
    edge = by_table(jnp.concatenate(strip, axis=1), cos_v)[:1]
    upper = jnp.full((1, count), side, jnp.int32) == 0

    @pl.when(place != 0)
    def _():
        values = table_by(cos_t_v, jnp.concatenate([here, here - modes(0)], axis=1))
        pot = values[:, :rows].T
        fields[0] = pot
        fields[1] = values[:, rows:2 * rows].T
        beyond_row[...] = jnp.broadcast_to(jnp.where(upper, edge, pot[rows - 1:]), beyond_row.shape)

    @pl.when(place == 0)
    def _():
        pot = table_by(cos_t_v, here).T
        fields[0] = pot
        before_first = jnp.where(upper, pot[:1], edge)
        after_last = jnp.where(upper, edge, pot[rows - 1:])
        beyond_row[...] = jnp.broadcast_to(after_last, beyond_row.shape)
        left_of = jnp.where(col == 0, pot, pltpu.roll(pot, 1, 1))
        right_of = jnp.where(col == count - 1, pot, pltpu.roll(pot, count - 1, 1))
        over = jnp.where(row == 0, before_first, pltpu.roll(pot, 1, 0))
        under = jnp.where(row == rows - 1, after_last, pltpu.roll(pot, rows - 1, 0))
        bend = (pot - left_of) + (pot - right_of) + (pot - over) + (pot - under)
        following = (2.0 + regular_shift) * pot + space_weight * bend - first_source[...]
        fields[1] = pot - following


def finish_kernel(rho, mx, my, fields, beyond_row, out_d, out_x, out_y, res_d, res_x, res_y, store_sem):
    rows, count = rho.shape
    row = lax.broadcasted_iota(jnp.int32, (rows, count), 0)
    col = lax.broadcasted_iota(jnp.int32, (rows, count), 1)
    here = fields[0]
    after = jnp.where(row == rows - 1, beyond_row[0:1], pltpu.roll(here, rows - 1, 0))
    res_x[...] = mx[...] - flux_weight * (after - here)
    save_x = pltpu.make_async_copy(res_x, out_x.at[0], store_sem.at[0])
    save_x.start()
    grad = jnp.where(col == count - 1, 0.0, pltpu.roll(here, count - 1, 1) - here)
    res_y[...] = my[...] - flux_weight * grad
    save_y = pltpu.make_async_copy(res_y, out_y.at[0], store_sem.at[1])
    save_y.start()
    res_d[...] = rho[...] - fields[1]
    save_d = pltpu.make_async_copy(res_d, out_d.at[0], store_sem.at[2])
    save_d.start()
    for save in (save_x, save_y, save_d):
        save.wait()


def per_device_kernel(density, flux_x, flux_y):
    rows, count = density.shape[1:]
    total = lax.axis_size("tm") // 2
    solvers = 2 * total
    group = count // solvers
    tables = host_tables(count, solvers)
    f32, bf16 = jnp.float32, jnp.bfloat16
    vm = pltpu.VMEM
    dma = pltpu.SemaphoreType.DMA
    slab = vm((rows, count), f32)
    tall = solvers * (2 * group + 8)
    scratch = [
        vm((2, 3, rows // 2, count), f32), vm((2, count, count), bf16), vm((2, count, count), bf16), vm((group, count), f32),
        slab, vm((8, count), f32), vm((tall, rows), f32), vm((tall, rows), f32),
        vm((total, group, count), f32), vm((total, group, count), f32),
        vm((2, group, count), f32), vm((total + 1, group, count), f32),
        vm((2, total * (2 * group + 8), rows), f32), vm((tall, rows), f32),
        dma((5,)), dma((2,)), dma((2,)), dma((2,)), dma((2,)),
    ]
    anywhere = pl.BlockSpec(memory_space=pl.ANY)

    def kernel(*refs):
        step_kernel(total, *refs)

    local = pl.BlockSpec(memory_space=pltpu.VMEM)
    held = pl.pallas_call(
        kernel,
        out_shape=[slab, slab, slab, vm((2, rows, count), f32), vm((8, count), f32)],
        in_specs=[anywhere] * 6,
        out_specs=[local] * 5,
        scratch_shapes=scratch,
        compiler_params=pltpu.CompilerParams(collective_id=0, has_side_effects=True),
    )(density, flux_x, flux_y, *tables)
    return pl.pallas_call(
        finish_kernel,
        out_shape=[jax.ShapeDtypeStruct(density.shape, f32)] * 3,
        in_specs=[local] * 5,
        out_specs=[anywhere] * 3,
        scratch_shapes=[slab, slab, slab, dma((3,))],
    )(*[pltpu.with_memory_space_constraint(x, pltpu.VMEM) for x in held])


def per_device(density, flux_x, flux_y):
    slabs, rows, count = density.shape
    size = lax.axis_size("tm")
    fits = (
        slabs == 1 and lax.axis_size("space") == 2 and size >= 2 and size & (size - 1) == 0
        and count % (8 * size) == 0 and rows % 128 == 0 and 2 * rows == count
    )
    return (per_device_kernel if fits else per_device_xla)(density, flux_x, flux_y)


def solution(mesh):
    return jax.shard_map(
        per_device,
        mesh=mesh,
        in_specs=(P("tm", "space", None), P("tm", "space", None), P("tm", "space", None)),
        out_specs=(P("tm", "space", None), P("tm", "space", None), P("tm", "space", None)),
        check_vma=False,
    )
```

```python
import jax
import jax.numpy as jnp
import numpy as np
from jax import lax
from jax.experimental import pallas as pl
from jax.experimental.pallas import tpu as pltpu
from jax.sharding import PartitionSpec as P

NEWTON = 4


prox_weight = 1.0
regular_shift = 0.0001
space_weight = 0.25
flux_weight = 0.5
highest = lax.Precision.HIGHEST


def swapped(block, axis, distance):
    count = lax.axis_size(axis)
    route = []
    for low in range(count):
        high = low | 1 << distance
        if high != low and high < count:
            route += [(low, high), (high, low)]
    return lax.ppermute(block, axis, route)


def shifted(array, axis, by):
    size = lax.axis_size(axis)
    pairs = [(i, i + by) for i in range(size) if 0 <= i + by < size]
    return lax.ppermute(array, axis, pairs)


def kinetic_prox(density, flux_x, flux_y):
    square = flux_x * flux_x + flux_y * flux_y
    target = density + prox_weight + jnp.sqrt(square)
    for step in range(NEWTON):
        above = target + prox_weight
        value = (target - density) * above * above - 0.5 * prox_weight * square
        slope = above * (3.0 * target + prox_weight - 2.0 * density)
        target = target - value / slope
    shrink = target / (target + prox_weight)
    return (target, shrink * flux_x, shrink * flux_y)


def cosine_table(count):
    modes = jnp.arange(count).astype(jnp.float32)[:, None]
    points = jnp.arange(count).astype(jnp.float32)[None, :]
    table = jnp.cos(jnp.pi * modes * (2.0 * points + 1.0) / (2.0 * count))
    scales = jnp.where(modes == 0, jnp.sqrt(1.0 / count), jnp.sqrt(2.0 / count))
    return scales * table


def eigen_values(count):
    modes = jnp.arange(count).astype(jnp.float32)
    return 4.0 * jnp.sin(jnp.pi * modes / (2.0 * count)) ** 2


def move_outward(stacked, bit):
    return swapped(stacked, "tm", bit)


def move_homeward(stacked, bit):
    return swapped(stacked, "tm", bit)


def butterfly(blocks, mover):
    total = lax.axis_size("tm")
    position = lax.axis_index("tm")
    bit_count = total.bit_length() - 1
    for bit in range(bit_count):
        higher = total >> bit + 1
        lowest = 1 << bit
        shaped = blocks.reshape((higher, 2, lowest) + blocks.shape[1:])
        own_bit = position >> bit & 1
        keeping = jnp.where(own_bit == 0, shaped[:, 0], shaped[:, 1])
        leaving = jnp.where(own_bit == 0, shaped[:, 1], shaped[:, 0])
        arrived = mover(leaving, bit)
        first_half = jnp.where(own_bit == 0, keeping, arrived)
        second_half = jnp.where(own_bit == 0, arrived, keeping)
        blocks = jnp.stack([first_half, second_half], axis=1).reshape(blocks.shape)
    return blocks


def per_device_xla(density, flux_x, flux_y):
    slabs = density.shape[0]
    rows_local = density.shape[1]
    count = density.shape[2]
    parts = lax.axis_size("space")
    modes_local = count // parts
    own_start = lax.axis_index("space") * rows_local
    mode_start = lax.axis_index("space") * modes_local
    rho, mom_x, mom_y = kinetic_prox(density, flux_x, flux_y)
    prior = shifted(rho[slabs - 1], "tm", 1)
    before = jnp.concatenate([prior[None], rho[:-1]], axis=0)
    zeroed = mom_y.at[:, :, count - 1].set(0.0)
    div_second = zeroed - jnp.concatenate(
        [jnp.zeros_like(zeroed[:, :, :1]), zeroed[:, :, :-1]], axis=2
    )
    partial_source = rho - before + flux_weight * div_second
    table = cosine_table(count)
    diff_table = jnp.concatenate(
        [table[:, :-1] - table[:, 1:], jnp.zeros_like(table[:, :1])], axis=1
    )
    stacked = jnp.concatenate([partial_source, flux_weight * mom_x], axis=1)
    column_modes = jnp.einsum("tij,kj->itk", stacked, table, precision=highest)
    left = lax.dynamic_slice(
        table, (0, own_start), (modes_local * lax.axis_size("space"), rows_local)
    )
    left_diff = lax.dynamic_slice(
        diff_table, (0, own_start), (modes_local * lax.axis_size("space"), rows_local)
    )
    both = jnp.concatenate([left, left_diff], axis=1)
    modal = lax.psum_scatter(
        jnp.einsum("ki,itj->ktj", both, column_modes, precision=highest),
        "space",
        scatter_dimension=0,
        tiled=True,
    )
    lam = eigen_values(count)
    lam_local = lax.dynamic_slice_in_dim(lam, mode_start, modes_local)
    coeff = 2.0 + regular_shift + space_weight * (lam_local[:, None] + lam[None, :])
    devices_tm = lax.axis_size("tm")
    position = lax.axis_index("tm")
    lines_local = modes_local * count
    line_group = lines_local // devices_tm
    steps_all = devices_tm * slabs
    outgoing = jnp.transpose(modal, (0, 2, 1)).reshape(devices_tm, line_group, slabs)
    incoming = butterfly(outgoing, move_outward)
    series = jnp.transpose(incoming, (1, 0, 2)).reshape(line_group, steps_all)
    line_coeff = lax.dynamic_slice_in_dim(
        coeff.reshape(lines_local), position * line_group, line_group
    )
    column = lax.broadcasted_iota(jnp.int32, (line_group, steps_all), 1)
    below_band = jnp.where(column == 0, 0.0, -1.0).astype(jnp.float32)
    above_band = jnp.where(column == steps_all - 1, 0.0, -1.0).astype(jnp.float32)
    middle_band = jnp.broadcast_to(line_coeff[:, None], (line_group, steps_all))
    solution = lax.linalg.tridiagonal_solve(
        below_band, middle_band, above_band, series[:, :, None]
    )[:, :, 0]
    blocked = solution.reshape(line_group, devices_tm, slabs)
    leading_next = jnp.concatenate(
        [solution[:, slabs::slabs], jnp.zeros((line_group, 1), jnp.float32)], axis=1
    )
    padded = jnp.concatenate([blocked, leading_next[:, :, None]], axis=2)
    returned = butterfly(jnp.transpose(padded, (1, 0, 2)), move_homeward)
    local_lines = returned.reshape(modes_local, count, slabs + 1)
    extended = jnp.transpose(local_lines, (0, 2, 1))
    phihat = extended[:, :slabs, :]
    left = lax.dynamic_slice(
        table, (mode_start, 0), (modes_local, rows_local * lax.axis_size("space"))
    )
    left_diff = lax.dynamic_slice(
        diff_table, (mode_start, 0), (modes_local, rows_local * lax.axis_size("space"))
    )
    values = jnp.einsum("ki,ktj->itj", left, extended, precision=highest)
    slopes = -jnp.einsum("ki,ktj->itj", left_diff, phihat, precision=highest)
    gathered = lax.psum_scatter(
        jnp.concatenate([values, slopes], axis=1), "space", scatter_dimension=0, tiled=True
    )
    physical = jnp.einsum("itk,kj->tij", gathered, table, precision=highest)
    potential = physical[: slabs + 1]
    grad_first = physical[slabs + 1 :]
    present = potential[:slabs]
    grad_second = jnp.concatenate(
        [present[:, :, 1:] - present[:, :, :-1], jnp.zeros_like(present[:, :, :1])], axis=2
    )
    density_out = rho - (present - potential[1:])
    flux_x_out = mom_x - flux_weight * grad_first
    flux_y_out = mom_y - flux_weight * grad_second
    return (density_out, flux_x_out, flux_y_out)


MESH = pl.DeviceIdType.MESH


def split_table(table):
    high = table.astype(jnp.bfloat16)
    low = (table - high.astype(np.float32)).astype(jnp.bfloat16)
    return np.stack([high, low], axis=-3)


def host_tables(count, solvers):
    modes = np.arange(count, dtype=np.float64)[:, None]
    points = np.arange(count, dtype=np.float64)[None, :]
    table = np.cos(np.pi * modes * (2.0 * points + 1.0) / (2.0 * count))
    table = table * np.where(modes == 0, np.sqrt(1.0 / count), np.sqrt(2.0 / count))
    lam = 4.0 * np.sin(np.pi * np.arange(count) / (2.0 * count)) ** 2
    coeff = 2.0 + regular_shift + space_weight * (lam[:, None] + lam[None, :])
    f32 = np.float32
    return (
        split_table(table.astype(f32)),
        split_table(table.T.astype(f32)),
        coeff.reshape(solvers, count // solvers, count).astype(f32),
    )


def parted(x):
    high = x.astype(jnp.bfloat16)
    return high, (x - high.astype(jnp.float32)).astype(jnp.bfloat16)


def mul(a, b):
    return jnp.dot(a, b, preferred_element_type=jnp.float32)


def mul_nt(a, b):
    return lax.dot_general(a, b, (((1,), (1,)), ((), ())), preferred_element_type=jnp.float32)


def by_table(x, table):
    high, low = parted(x)
    return mul(high, table[0]) + (mul(high, table[1]) + mul(low, table[0]))


def table_by(table, x):
    high, low = parted(x)
    return mul(table[0], high) + (mul(table[1], high) + mul(table[0], low))


def table_by_t(table, x):
    high, low = parted(x)
    return mul_nt(table[0], high) + (mul_nt(table[1], high) + mul_nt(table[0], low))


def by_table_t(x, table):
    high, low = parted(x)
    return mul_nt(high, table[0]) + (mul_nt(high, table[1]) + mul_nt(low, table[0]))


def mul_tn(a, b):
    return lax.dot_general(a, b, (((0,), (0,)), ((), ())), preferred_element_type=jnp.float32)


def by_table_tn(x, table):
    high, low = parted(x)
    return mul_tn(high, table[0]) + (mul_tn(high, table[1]) + mul_tn(low, table[0]))


def step_kernel(
    total, density, flux_x, flux_y, cos, cos_t, coeff,
    rho, mx, my, fields, beyond_row,
    inputs, cos_v, cos_t_v, coeff_v,
    first_source, halo, outgoing, incoming, pivots, steps, cut, phi, back, home,
    load_sem, halo_sem, out_sem, cut_sem, back_sem,
):
    place = lax.axis_index("tm")
    half = place // total
    me = place - half * total
    base = half * total
    final = 2 * total - 1
    mirror = {"tm": lax.rem(place + total, 2 * total)}
    side = lax.axis_index("space")
    own = 2 * me + side
    rows, count = rho.shape
    group = coeff_v.shape[0]
    stride_rows, filled = 2 * group + 8, 2 * group + 1
    pieces = inputs.shape[0]
    tile = rows // pieces
    feeds = [
        pltpu.make_async_copy(src.at[0, pl.ds(j * tile, tile)], inputs.at[j, i], load_sem.at[j])
        for j in range(pieces) for i, src in enumerate((density, flux_x, flux_y))
    ]
    loads = [
        pltpu.make_async_copy(src, dst, load_sem.at[i])
        for i, (src, dst) in enumerate([(cos, cos_v), (coeff.at[own], coeff_v), (cos_t, cos_t_v)], pieces)
    ]
    for load in feeds + loads:
        load.start()

    def settle(ref, size, sem):
        span = ref.at[pl.ds(0, size)]
        pltpu.make_async_copy(span, span, sem).wait()

    bits = [1 << i for i in range(total.bit_length() - 1)]
    flips = [bit * (1 - 2 * lax.rem(me // bit, 2)) for bit in bits]
    masks = sorted(range(total), key=lambda m: (-bin(m).count("1"), -m))
    peers = []
    for m in masks:
        chip = me + sum(f for f, bit in zip(flips, bits) if m & bit)
        for core in ([side] if m else []) + [1 - side]:
            peers.append((chip, core, 2 * chip + core))

    def device(peer):
        return {"tm": base + peer[0], "space": peer[1]}

    def choose(options):
        for test, action in options:
            pl.when(test)(action)

    barrier = pltpu.get_barrier_semaphore()
    for peer in peers:
        pl.semaphore_signal(barrier, inc=1, device_id=device(peer), device_id_type=MESH)
    pl.semaphore_signal(barrier, inc=1, device_id=mirror, device_id_type=MESH)
    for j in range(pieces):
        settle(inputs.at[j], 3, load_sem.at[j])
        span = slice(j * tile, (j + 1) * tile)
        rho[span], mx[span], my[span] = kinetic_prox(inputs[j, 0], inputs[j, 1], inputs[j, 2])

    row = lax.broadcasted_iota(jnp.int32, (rows, count), 0)
    col = lax.broadcasted_iota(jnp.int32, (rows, count), 1)
    bottom = side * rows + row == 2 * rows - 1
    wx = jnp.where(bottom, 0.0, mx[...])
    wy = jnp.where(col == count - 1, 0.0, my[...])
    div = flux_weight * (
        wx - jnp.where(row == 0, 0.0, pltpu.roll(wx, 1, 0)) + wy - pltpu.roll(wy, 1, 1))
    whole = rho[...] + div
    closing = jnp.full((rows, count), place, jnp.int32) == final
    pair = jnp.concatenate(
        [jnp.where(closing, 0.0, rho[...]), jnp.where(closing, whole, div)], axis=0)
    loads[0].wait()
    spread = table_by_t(cos_v, pair)
    crossing = by_table_t(jnp.broadcast_to(-flux_weight * wx[rows - 1:], (8, count)), cos_v)
    for block in range(2 * total):
        span = slice(block * group, (block + 1) * group)
        first = block * stride_rows
        for f in range(2):
            outgoing[first + f * group:first + (f + 1) * group] = spread[span, f * rows:(f + 1) * rows]
        part = block // total * rows
        outgoing[first + 2 * group:first + filled] = crossing[:1, part:part + rows]
    pl.semaphore_wait(barrier, 2 * total)

    def place_of(block, first, size):
        return pl.ds(pl.multiple_of(block * stride_rows + first, 8), size)

    def outward(peer, first, size):
        return pltpu.make_async_remote_copy(
            src_ref=outgoing.at[place_of(peer[2], first, size)],
            dst_ref=incoming.at[place_of(own, first, size)],
            send_sem=out_sem.at[0], recv_sem=out_sem.at[1],
            device_id=device(peer), device_id_type=MESH)

    def out_kinds(chip, core, action):
        ending = chip == final
        inner = jnp.logical_not(ending)
        choose([
            (inner & (core == 0), lambda: action(0, filled)),
            (inner & (core == 1), lambda: action(0, 2 * group)),
            (ending & (core == 0), lambda: action(group, group + 1)),
            (ending & (core == 1), lambda: action(group, group)),
        ])

    def send_out(first, size):
        for peer in peers:
            outward(peer, first, size).start()

    out_kinds(place, side, send_out)

    row_halo = pltpu.make_async_remote_copy(
        src_ref=mx.at[pl.ds(rows - 8, 8)], dst_ref=halo, send_sem=halo_sem.at[0],
        recv_sem=halo_sem.at[1], device_id={"space": 1 - side}, device_id_type=MESH)

    @pl.when(place == 0)
    def _():
        row_halo.start()

    @pl.when(half == 1)
    def _():
        for block in (2 * total - 2, 2 * total - 1):
            incoming[pl.ds(block * stride_rows, group)] = jnp.zeros((group, rows), jnp.float32)

    small = (place == 0) | (place == final)

    @pl.when(small)
    def _():
        for block in range(2 * total):
            home[pl.ds(block * stride_rows, group)] = jnp.zeros((group, rows), jnp.float32)

    incoming[place_of(own, 0, stride_rows)] = outgoing[place_of(own, 0, stride_rows)]
    loads[1].wait()
    c = coeff_v[...]
    pivot = 1.0 / c
    pivots[0] = pivot
    for t in range(1, total):
        pivot = 1.0 / (c - pivot)
        pivots[t] = pivot
    inverse = 1.0 / (1.0 - pivot * pivot)
    loads[2].wait()
    right = jnp.full((group, count), half, jnp.int32) == 1
    start, stride = half * (total - 1), 1 - 2 * half
    swap = pltpu.make_async_remote_copy(
        src_ref=cut.at[0], dst_ref=cut.at[1], send_sem=cut_sem.at[0],
        recv_sem=cut_sem.at[1], device_id=mirror, device_id_type=MESH)

    def homeward(peer, first, size):
        return pltpu.make_async_remote_copy(
            src_ref=back.at[peer[1], place_of(peer[0], first, size)], dst_ref=home.at[place_of(own, first, size)],
            send_sem=back_sem.at[0], recv_sem=back_sem.at[1],
            device_id=device(peer), device_id_type=MESH)

    def back_kinds(chip, core, action):
        ending = (chip == 0) | (chip == final)
        inner = jnp.logical_not(ending)
        choose([
            (ending, lambda: action(group, group + 1)),
            (inner & (core == 0), lambda: action(0, filled)),
            (inner & (core == 1), lambda: action(0, 2 * group)),
        ])

    @pl.when(place == 0)
    def _():
        row_halo.wait()
        prior = jnp.where(jnp.full((1, count), side, jnp.int32) == 1, halo[7:], 0.0)
        first_source[...] = whole - jnp.where(row == 0, flux_weight * prior, 0.0)

    everything = total * (filled + 2 * group)
    pl.when(half == 0)(lambda: out_kinds(
        place, side, lambda first, size: settle(incoming, everything - size, out_sem.at[1])))
    pl.when(half == 1)(lambda: out_kinds(
        place, side, lambda first, size: settle(incoming, everything - 2 * group - size, out_sem.at[1])))

    def slices(t, f):
        firsts = [(2 * t + core) * stride_rows + f * group for core in range(2)]
        return [incoming[first:first + group] for first in firsts]

    shares = incoming[pl.ds(2 * group, total, stride=2 * stride_rows)]
    lanes = lax.broadcasted_iota(jnp.int32, (group, rows), 1)
    picked = lanes == lax.rem(own, total) * group + lax.broadcasted_iota(jnp.int32, (group, rows), 0)

    def beyond_halo(t):
        mine = jnp.where(picked, jnp.broadcast_to(shares[t:t + 1], (group, rows)), 0.0)
        return jnp.where(lanes == 0, jnp.sum(mine, axis=1, keepdims=True), 0.0)

    source = []
    for t in range(total):
        low, high = slices(t, 1)
        high = high + beyond_halo(t)
        now = slices(t, 0)
        if t > 0:
            now = [x - y for x, y in zip(now, slices(t - 1, 0))]
        source.append(jnp.concatenate([low + now[0], high + now[1]], axis=1))
    source.append(jnp.concatenate(slices(total - 1, 0), axis=1))
    modal = by_table(jnp.concatenate(source, axis=0), cos_t_v)
    steps[...] = modal[:total * group].reshape(total, group, count)
    value = jnp.zeros((group, count), jnp.float32)
    for i in range(total):
        value = (steps[start + stride * i] + value) * pivots[i]
        steps[start + stride * i] = value
    last_rho = jnp.where(right, 0.0, modal[total * group:])
    cut[0] = value - last_rho
    swap.start()

    out_kinds(place, side, lambda first, size: settle(outgoing, (2 * total - 1) * size, out_sem.at[0]))
    swap.wait()
    pivot = pivots[total - 1]
    beyond = cut[1] - pivot * last_rho
    value = (value + pivot * beyond) * inverse
    phi[total] = jnp.where(right, 0.0, beyond + pivot * value)
    phi[start + stride * (total - 1)] = value
    for i in reversed(range(total - 1)):
        value = steps[start + stride * i] + pivots[i] * value
        phi[start + stride * i] = value
    lines = phi[...].reshape((total + 1) * group, count)
    halfback = by_table(lines, cos_v)
    halves = [halfback[:, :rows], halfback[:, rows:]]
    brink = table_by_t(cos_t_v[:, rows - 8:rows + 8], lines[:total * group])
    for t in range(total + 1):
        for core in range(2):
            block = halves[core][t * group:(t + 1) * group]
            if t < total:
                first = t * stride_rows
                back[core, first + group:first + 2 * group] = block
                back[core, first + 2 * group:first + filled] = brink[8 - core:9 - core]
            if t > 0:
                first = (t - 1) * stride_rows
                back[core, first:first + group] = block
    for core in range(2):
        @pl.when((half == 0) & (own != core))
        def _():
            homeward((0, core, core), group, group + 1).start()

    for peer in peers:
        @pl.when(base + peer[0] != 0)
        def _():
            back_kinds(base + peer[0], peer[1], lambda first, size: homeward(peer, first, size).start())

    home[place_of(own, group, group + 8)] = back[side, place_of(me, group, group + 8)]

    @pl.when(jnp.logical_not(small))
    def _():
        home[place_of(own, 0, group)] = back[side, place_of(me, 0, group)]

    returned = 2 * (group + 1) + (total - 1) * (filled + 2 * group)
    back_kinds(place, side, lambda first, size: settle(home, returned - size, back_sem.at[0]))
    back_kinds(place, side, lambda first, size: settle(home, (2 * total - 1) * size, back_sem.at[1]))

    def modes(first):
        spans = [block * stride_rows + first for block in range(2 * total)]
        return jnp.concatenate([home[at:at + group] for at in spans], axis=0)

    here = modes(group)
    offset = lax.rem(total - me, total) * group
    row8 = lax.broadcasted_iota(jnp.int32, (total, rows), 0)
    lane8 = lax.broadcasted_iota(jnp.int32, (total, rows), 1)
    def find_edge():
        strip = []
        for part in range(2):
            tail = home[pl.ds(part * total * stride_rows + 2 * group, total, stride=stride_rows)]
            tail = jnp.where(lane8 < group, pltpu.roll(tail, offset, 1), 0.0)
            tail = sum(jnp.where(row8 == d, pltpu.roll(tail, d * group, 1) if d else tail, 0.0) for d in range(total))
            strip.append(jnp.broadcast_to(jnp.sum(tail, axis=0, keepdims=True), (8, rows)))
        return by_table(jnp.concatenate(strip, axis=1), cos_v)[:1]

    upper = jnp.full((1, count), side, jnp.int32) == 0

    @pl.when(place != 0)
    def _():
        values = by_table_tn(jnp.concatenate([here, here - modes(0)], axis=1), cos_v)
        edge = find_edge()
        pot = values[:rows]
        fields[0] = pot
        fields[1] = values[rows:]
        beyond_row[...] = jnp.broadcast_to(jnp.where(upper, edge, pot[rows - 1:]), beyond_row.shape)

    @pl.when(place == 0)
    def _():
        edge = find_edge()
        pot = by_table_tn(here, cos_v)
        fields[0] = pot
        before_first = jnp.where(upper, pot[:1], edge)
        after_last = jnp.where(upper, edge, pot[rows - 1:])
        beyond_row[...] = jnp.broadcast_to(after_last, beyond_row.shape)
        left_of = jnp.where(col == 0, pot, pltpu.roll(pot, 1, 1))
        right_of = jnp.where(col == count - 1, pot, pltpu.roll(pot, count - 1, 1))
        over = jnp.where(row == 0, before_first, pltpu.roll(pot, 1, 0))
        under = jnp.where(row == rows - 1, after_last, pltpu.roll(pot, rows - 1, 0))
        bend = (pot - left_of) + (pot - right_of) + (pot - over) + (pot - under)
        following = (2.0 + regular_shift) * pot + space_weight * bend - first_source[...]
        fields[1] = pot - following


def finish_kernel(rho, mx, my, fields, beyond_row, out_d, out_x, out_y, res_d, res_x, res_y, store_sem):
    rows, count = rho.shape
    row = lax.broadcasted_iota(jnp.int32, (rows, count), 0)
    col = lax.broadcasted_iota(jnp.int32, (rows, count), 1)
    here = fields[0]
    after = jnp.where(row == rows - 1, beyond_row[0:1], pltpu.roll(here, rows - 1, 0))
    res_x[...] = mx[...] - flux_weight * (after - here)
    save_x = pltpu.make_async_copy(res_x, out_x.at[0], store_sem.at[0])
    save_x.start()
    grad = jnp.where(col == count - 1, 0.0, pltpu.roll(here, count - 1, 1) - here)
    res_y[...] = my[...] - flux_weight * grad
    save_y = pltpu.make_async_copy(res_y, out_y.at[0], store_sem.at[1])
    save_y.start()
    res_d[...] = rho[...] - fields[1]
    save_d = pltpu.make_async_copy(res_d, out_d.at[0], store_sem.at[2])
    save_d.start()
    for save in (save_x, save_y, save_d):
        save.wait()


def per_device_kernel(density, flux_x, flux_y):
    rows, count = density.shape[1:]
    total = lax.axis_size("tm") // 2
    solvers = 2 * total
    group = count // solvers
    tables = host_tables(count, solvers)
    f32, bf16 = jnp.float32, jnp.bfloat16
    vm = pltpu.VMEM
    dma = pltpu.SemaphoreType.DMA
    slab = vm((rows, count), f32)
    tall = solvers * (2 * group + 8)
    scratch = [
        vm((2, 3, rows // 2, count), f32), vm((2, count, count), bf16), vm((2, count, count), bf16), vm((group, count), f32),
        slab, vm((8, count), f32), vm((tall, rows), f32), vm((tall, rows), f32),
        vm((total, group, count), f32), vm((total, group, count), f32),
        vm((2, group, count), f32), vm((total + 1, group, count), f32),
        vm((2, total * (2 * group + 8), rows), f32), vm((tall, rows), f32),
        dma((5,)), dma((2,)), dma((2,)), dma((2,)), dma((2,)),
    ]
    anywhere = pl.BlockSpec(memory_space=pl.ANY)

    def kernel(*refs):
        step_kernel(total, *refs)

    local = pl.BlockSpec(memory_space=pltpu.VMEM)
    held = pl.pallas_call(
        kernel,
        out_shape=[slab, slab, slab, vm((2, rows, count), f32), vm((8, count), f32)],
        in_specs=[anywhere] * 6,
        out_specs=[local] * 5,
        scratch_shapes=scratch,
        compiler_params=pltpu.CompilerParams(collective_id=0, has_side_effects=True),
    )(density, flux_x, flux_y, *tables)
    return pl.pallas_call(
        finish_kernel,
        out_shape=[jax.ShapeDtypeStruct(density.shape, f32)] * 3,
        in_specs=[local] * 5,
        out_specs=[anywhere] * 3,
        scratch_shapes=[slab, slab, slab, dma((3,))],
    )(*[pltpu.with_memory_space_constraint(x, pltpu.VMEM) for x in held])


def per_device(density, flux_x, flux_y):
    slabs, rows, count = density.shape
    size = lax.axis_size("tm")
    fits = (
        slabs == 1 and lax.axis_size("space") == 2 and size >= 2 and size & (size - 1) == 0
        and count % (8 * size) == 0 and rows % 128 == 0 and 2 * rows == count
    )
    return (per_device_kernel if fits else per_device_xla)(density, flux_x, flux_y)


def solution(mesh):
    return jax.shard_map(
        per_device,
        mesh=mesh,
        in_specs=(P("tm", "space", None), P("tm", "space", None), P("tm", "space", None)),
        out_specs=(P("tm", "space", None), P("tm", "space", None), P("tm", "space", None)),
        check_vma=False,
    )
```

```python
import jax
import jax.numpy as jnp
import numpy as np
from jax import lax
from jax.experimental import pallas as pl
from jax.experimental.pallas import tpu as pltpu
from jax.sharding import PartitionSpec as P

NEWTON = 4


prox_weight = 1.0
regular_shift = 0.0001
space_weight = 0.25
flux_weight = 0.5
highest = lax.Precision.HIGHEST


def swapped(block, axis, distance):
    count = lax.axis_size(axis)
    route = []
    for low in range(count):
        high = low | 1 << distance
        if high != low and high < count:
            route += [(low, high), (high, low)]
    return lax.ppermute(block, axis, route)


def shifted(array, axis, by):
    size = lax.axis_size(axis)
    pairs = [(i, i + by) for i in range(size) if 0 <= i + by < size]
    return lax.ppermute(array, axis, pairs)


def kinetic_prox(density, flux_x, flux_y):
    square = flux_x * flux_x + flux_y * flux_y
    target = density + prox_weight + jnp.sqrt(square)
    for step in range(NEWTON):
        above = target + prox_weight
        value = (target - density) * above * above - 0.5 * prox_weight * square
        slope = above * (3.0 * target + prox_weight - 2.0 * density)
        target = target - value / slope
    shrink = target / (target + prox_weight)
    return (target, shrink * flux_x, shrink * flux_y)


def cosine_table(count):
    modes = jnp.arange(count).astype(jnp.float32)[:, None]
    points = jnp.arange(count).astype(jnp.float32)[None, :]
    table = jnp.cos(jnp.pi * modes * (2.0 * points + 1.0) / (2.0 * count))
    scales = jnp.where(modes == 0, jnp.sqrt(1.0 / count), jnp.sqrt(2.0 / count))
    return scales * table


def eigen_values(count):
    modes = jnp.arange(count).astype(jnp.float32)
    return 4.0 * jnp.sin(jnp.pi * modes / (2.0 * count)) ** 2


def move_outward(stacked, bit):
    return swapped(stacked, "tm", bit)


def move_homeward(stacked, bit):
    return swapped(stacked, "tm", bit)


def butterfly(blocks, mover):
    total = lax.axis_size("tm")
    position = lax.axis_index("tm")
    bit_count = total.bit_length() - 1
    for bit in range(bit_count):
        higher = total >> bit + 1
        lowest = 1 << bit
        shaped = blocks.reshape((higher, 2, lowest) + blocks.shape[1:])
        own_bit = position >> bit & 1
        keeping = jnp.where(own_bit == 0, shaped[:, 0], shaped[:, 1])
        leaving = jnp.where(own_bit == 0, shaped[:, 1], shaped[:, 0])
        arrived = mover(leaving, bit)
        first_half = jnp.where(own_bit == 0, keeping, arrived)
        second_half = jnp.where(own_bit == 0, arrived, keeping)
        blocks = jnp.stack([first_half, second_half], axis=1).reshape(blocks.shape)
    return blocks


def per_device_xla(density, flux_x, flux_y):
    slabs = density.shape[0]
    rows_local = density.shape[1]
    count = density.shape[2]
    parts = lax.axis_size("space")
    modes_local = count // parts
    own_start = lax.axis_index("space") * rows_local
    mode_start = lax.axis_index("space") * modes_local
    rho, mom_x, mom_y = kinetic_prox(density, flux_x, flux_y)
    prior = shifted(rho[slabs - 1], "tm", 1)
    before = jnp.concatenate([prior[None], rho[:-1]], axis=0)
    zeroed = mom_y.at[:, :, count - 1].set(0.0)
    div_second = zeroed - jnp.concatenate(
        [jnp.zeros_like(zeroed[:, :, :1]), zeroed[:, :, :-1]], axis=2
    )
    partial_source = rho - before + flux_weight * div_second
    table = cosine_table(count)
    diff_table = jnp.concatenate(
        [table[:, :-1] - table[:, 1:], jnp.zeros_like(table[:, :1])], axis=1
    )
    stacked = jnp.concatenate([partial_source, flux_weight * mom_x], axis=1)
    column_modes = jnp.einsum("tij,kj->itk", stacked, table, precision=highest)
    left = lax.dynamic_slice(
        table, (0, own_start), (modes_local * lax.axis_size("space"), rows_local)
    )
    left_diff = lax.dynamic_slice(
        diff_table, (0, own_start), (modes_local * lax.axis_size("space"), rows_local)
    )
    both = jnp.concatenate([left, left_diff], axis=1)
    modal = lax.psum_scatter(
        jnp.einsum("ki,itj->ktj", both, column_modes, precision=highest),
        "space",
        scatter_dimension=0,
        tiled=True,
    )
    lam = eigen_values(count)
    lam_local = lax.dynamic_slice_in_dim(lam, mode_start, modes_local)
    coeff = 2.0 + regular_shift + space_weight * (lam_local[:, None] + lam[None, :])
    devices_tm = lax.axis_size("tm")
    position = lax.axis_index("tm")
    lines_local = modes_local * count
    line_group = lines_local // devices_tm
    steps_all = devices_tm * slabs
    outgoing = jnp.transpose(modal, (0, 2, 1)).reshape(devices_tm, line_group, slabs)
    incoming = butterfly(outgoing, move_outward)
    series = jnp.transpose(incoming, (1, 0, 2)).reshape(line_group, steps_all)
    line_coeff = lax.dynamic_slice_in_dim(
        coeff.reshape(lines_local), position * line_group, line_group
    )
    column = lax.broadcasted_iota(jnp.int32, (line_group, steps_all), 1)
    below_band = jnp.where(column == 0, 0.0, -1.0).astype(jnp.float32)
    above_band = jnp.where(column == steps_all - 1, 0.0, -1.0).astype(jnp.float32)
    middle_band = jnp.broadcast_to(line_coeff[:, None], (line_group, steps_all))
    solution = lax.linalg.tridiagonal_solve(
        below_band, middle_band, above_band, series[:, :, None]
    )[:, :, 0]
    blocked = solution.reshape(line_group, devices_tm, slabs)
    leading_next = jnp.concatenate(
        [solution[:, slabs::slabs], jnp.zeros((line_group, 1), jnp.float32)], axis=1
    )
    padded = jnp.concatenate([blocked, leading_next[:, :, None]], axis=2)
    returned = butterfly(jnp.transpose(padded, (1, 0, 2)), move_homeward)
    local_lines = returned.reshape(modes_local, count, slabs + 1)
    extended = jnp.transpose(local_lines, (0, 2, 1))
    phihat = extended[:, :slabs, :]
    left = lax.dynamic_slice(
        table, (mode_start, 0), (modes_local, rows_local * lax.axis_size("space"))
    )
    left_diff = lax.dynamic_slice(
        diff_table, (mode_start, 0), (modes_local, rows_local * lax.axis_size("space"))
    )
    values = jnp.einsum("ki,ktj->itj", left, extended, precision=highest)
    slopes = -jnp.einsum("ki,ktj->itj", left_diff, phihat, precision=highest)
    gathered = lax.psum_scatter(
        jnp.concatenate([values, slopes], axis=1), "space", scatter_dimension=0, tiled=True
    )
    physical = jnp.einsum("itk,kj->tij", gathered, table, precision=highest)
    potential = physical[: slabs + 1]
    grad_first = physical[slabs + 1 :]
    present = potential[:slabs]
    grad_second = jnp.concatenate(
        [present[:, :, 1:] - present[:, :, :-1], jnp.zeros_like(present[:, :, :1])], axis=2
    )
    density_out = rho - (present - potential[1:])
    flux_x_out = mom_x - flux_weight * grad_first
    flux_y_out = mom_y - flux_weight * grad_second
    return (density_out, flux_x_out, flux_y_out)


MESH = pl.DeviceIdType.MESH


def split_table(table):
    high = table.astype(jnp.bfloat16)
    low = (table - high.astype(np.float32)).astype(jnp.bfloat16)
    return np.stack([high, low], axis=-3)


def host_tables(count, solvers):
    modes = np.arange(count, dtype=np.float64)[:, None]
    points = np.arange(count, dtype=np.float64)[None, :]
    table = np.cos(np.pi * modes * (2.0 * points + 1.0) / (2.0 * count))
    table = table * np.where(modes == 0, np.sqrt(1.0 / count), np.sqrt(2.0 / count))
    lam = 4.0 * np.sin(np.pi * np.arange(count) / (2.0 * count)) ** 2
    coeff = 2.0 + regular_shift + space_weight * (lam[:, None] + lam[None, :])
    f32 = np.float32
    return (
        split_table(table.astype(f32)),
        split_table(table.T.astype(f32)),
        coeff.reshape(solvers, count // solvers, count).astype(f32),
    )


def parted(x):
    high = x.astype(jnp.bfloat16)
    return high, (x - high.astype(jnp.float32)).astype(jnp.bfloat16)


def mul(a, b):
    return jnp.dot(a, b, preferred_element_type=jnp.float32)


def mul_nt(a, b):
    return lax.dot_general(a, b, (((1,), (1,)), ((), ())), preferred_element_type=jnp.float32)


def by_table(x, table):
    high, low = parted(x)
    return mul(high, table[0]) + (mul(high, table[1]) + mul(low, table[0]))


def table_by(table, x):
    high, low = parted(x)
    return mul(table[0], high) + (mul(table[1], high) + mul(table[0], low))


def table_by_t(table, x):
    high, low = parted(x)
    return mul_nt(table[0], high) + (mul_nt(table[1], high) + mul_nt(table[0], low))


def by_table_t(x, table):
    high, low = parted(x)
    return mul_nt(high, table[0]) + (mul_nt(high, table[1]) + mul_nt(low, table[0]))


def mul_tn(a, b):
    return lax.dot_general(a, b, (((0,), (0,)), ((), ())), preferred_element_type=jnp.float32)


def by_table_tn(x, table):
    high, low = parted(x)
    return mul_tn(high, table[0]) + (mul_tn(high, table[1]) + mul_tn(low, table[0]))


def step_kernel(
    total, density, flux_x, flux_y, cos, cos_t, coeff,
    rho, mx, my, fields, beyond_row,
    inputs, cos_v, cos_t_v, coeff_v,
    first_source, halo, outgoing, incoming, pivots, slope, steps, cut, back, home,
    load_sem, halo_sem, out_sem, cut_sem, back_sem,
):
    place = lax.axis_index("tm")
    half = place // total
    me = place - half * total
    base = half * total
    final = 2 * total - 1
    mirror = {"tm": lax.rem(place + total, 2 * total)}
    side = lax.axis_index("space")
    own = 2 * me + side
    rows, count = rho.shape
    group = coeff_v.shape[0]
    stride_rows, filled = 2 * group + 8, 2 * group + 1
    per = rows // group
    solving = side == 1
    pieces = inputs.shape[0]
    tile = rows // pieces
    feeds = [
        pltpu.make_async_copy(src.at[0, pl.ds(j * tile, tile)], inputs.at[j, i], load_sem.at[j])
        for j in range(pieces) for i, src in enumerate((density, flux_x, flux_y))
    ]
    loads = [
        pltpu.make_async_copy(src, dst, load_sem.at[i])
        for i, (src, dst) in enumerate([(cos, cos_v), (coeff.at[me], coeff_v), (cos_t, cos_t_v)], pieces)
    ]
    for load in feeds + loads:
        load.start()

    def settle(ref, size, sem):
        span = ref.at[pl.ds(0, size)]
        pltpu.make_async_copy(span, span, sem).wait()

    bits = [1 << i for i in range(total.bit_length() - 1)]
    flips = [bit * (1 - 2 * lax.rem(me // bit, 2)) for bit in bits]
    masks = sorted(range(total), key=lambda m: (-bin(m).count("1"), -m))
    chips = [me + sum(f for f, bit in zip(flips, bits) if m & bit) for m in masks]
    others = [chip for chip, m in zip(chips, masks) if m]

    def device(chip, core):
        return {"tm": base + chip, "space": core}

    def choose(options):
        for test, action in options:
            pl.when(test)(action)

    barrier = pltpu.get_barrier_semaphore()
    for chip in others:
        pl.semaphore_signal(barrier, inc=1, device_id=device(chip, 1), device_id_type=MESH)
    pl.semaphore_signal(barrier, inc=1, device_id={"space": 1 - side}, device_id_type=MESH)

    @pl.when(solving)
    def _():
        for chip in others:
            pl.semaphore_signal(barrier, inc=1, device_id=device(chip, 0), device_id_type=MESH)
        pl.semaphore_signal(barrier, inc=1, device_id=mirror, device_id_type=MESH)

    for j in range(pieces):
        settle(inputs.at[j], 3, load_sem.at[j])
        span = slice(j * tile, (j + 1) * tile)
        rho[span], mx[span], my[span] = kinetic_prox(inputs[j, 0], inputs[j, 1], inputs[j, 2])

    row = lax.broadcasted_iota(jnp.int32, (rows, count), 0)
    col = lax.broadcasted_iota(jnp.int32, (rows, count), 1)
    bottom = side * rows + row == 2 * rows - 1
    wx = jnp.where(bottom, 0.0, mx[...])
    wy = jnp.where(col == count - 1, 0.0, my[...])
    div = flux_weight * (
        wx - jnp.where(row == 0, 0.0, pltpu.roll(wx, 1, 0)) + wy - pltpu.roll(wy, 1, 1))
    whole = rho[...] + div
    closing = jnp.full((rows, count), place, jnp.int32) == final
    pair = jnp.concatenate(
        [jnp.where(closing, 0.0, rho[...]), jnp.where(closing, whole, div)], axis=0)
    loads[0].wait()
    spread = table_by_t(cos_v, pair)
    crossing = by_table_t(jnp.broadcast_to(-flux_weight * wx[rows - 1:], (8, count)), cos_v)
    for block in range(total):
        span = slice(block * group, (block + 1) * group)
        first = block * stride_rows
        for f in range(2):
            outgoing[first + f * group:first + (f + 1) * group] = spread[span, f * rows:(f + 1) * rows]
        part = block // per * rows
        outgoing[first + 2 * group:first + filled] = crossing[:1, part:part + rows]
    pl.semaphore_wait(barrier, total * (1 + side))

    def place_of(block, first, size):
        return pl.ds(pl.multiple_of(block * stride_rows + first, 8), size)

    def outward(chip, first, size):
        return pltpu.make_async_remote_copy(
            src_ref=outgoing.at[place_of(chip, first, size)],
            dst_ref=incoming.at[place_of(own, first, size)],
            send_sem=out_sem.at[0], recv_sem=out_sem.at[1],
            device_id=device(chip, 1), device_id_type=MESH)

    def out_kinds(chip, core, action):
        ending = chip == final
        inner = jnp.logical_not(ending)
        choose([
            (inner & (core == 0), lambda: action(0, filled)),
            (inner & (core == 1), lambda: action(0, 2 * group)),
            (ending & (core == 0), lambda: action(group, group + 1)),
            (ending & (core == 1), lambda: action(group, group)),
        ])

    def send_out(first, size):
        for chip in others:
            outward(chip, first, size).start()

        @pl.when(side == 0)
        def _():
            outward(me, first, size).start()

    out_kinds(place, side, send_out)

    row_halo = pltpu.make_async_remote_copy(
        src_ref=mx.at[pl.ds(rows - 8, 8)], dst_ref=halo, send_sem=halo_sem.at[0],
        recv_sem=halo_sem.at[1], device_id={"space": 1 - side}, device_id_type=MESH)

    @pl.when(place == 0)
    def _():
        row_halo.start()

    @pl.when(half == 1)
    def _():
        for block in (2 * total - 2, 2 * total - 1):
            incoming[pl.ds(block * stride_rows, group)] = jnp.zeros((group, rows), jnp.float32)

    small = (place == 0) | (place == final)

    @pl.when(small)
    def _():
        for block in range(total):
            home[pl.ds(block * stride_rows, group)] = jnp.zeros((group, rows), jnp.float32)

    loads[1].wait()
    loads[2].wait()
    swap = pltpu.make_async_remote_copy(
        src_ref=cut.at[0], dst_ref=cut.at[1], send_sem=cut_sem.at[0],
        recv_sem=cut_sem.at[1], device_id=mirror, device_id_type=MESH)

    def homeward(chip, core, first, size):
        return pltpu.make_async_remote_copy(
            src_ref=back.at[place_of(core * total + chip, first, size)], dst_ref=home.at[place_of(me, first, size)],
            send_sem=back_sem.at[0], recv_sem=back_sem.at[1],
            device_id=device(chip, core), device_id_type=MESH)

    def back_kinds(chip, core, action):
        ending = (chip == 0) | (chip == final)
        inner = jnp.logical_not(ending)
        choose([
            (ending, lambda: action(group, group + 1)),
            (inner & (core == 0), lambda: action(0, filled)),
            (inner & (core == 1), lambda: action(0, 2 * group)),
        ])

    @pl.when(place == 0)
    def _():
        row_halo.wait()
        prior = jnp.where(jnp.full((1, count), side, jnp.int32) == 1, halo[7:], 0.0)
        first_source[...] = whole - jnp.where(row == 0, flux_weight * prior, 0.0)

    def solve():
        incoming[place_of(own, 0, stride_rows)] = outgoing[place_of(me, 0, stride_rows)]
        c = coeff_v[...]
        pivot = 1.0 / c
        pivots[0] = pivot
        for t in range(1, total):
            pivot = 1.0 / (c - pivot)
            pivots[t] = pivot
        inverse = 1.0 / (1.0 - pivot * pivot)
        start, stride = half * (total - 1), 1 - 2 * half
        gain = jnp.ones((group, count), jnp.float32)
        slope[start + stride * (total - 1)] = gain
        for i in reversed(range(total - 1)):
            gain = gain * pivots[i]
            slope[start + stride * i] = gain
        right = jnp.full((group, count), half, jnp.int32) == 1
        everything = total * (filled + 2 * group)
        pl.when(half == 0)(lambda: out_kinds(
            place, side, lambda first, size: settle(incoming, everything - size, out_sem.at[1])))
        pl.when(half == 1)(lambda: out_kinds(
            place, side, lambda first, size: settle(incoming, everything - 2 * group - size, out_sem.at[1])))

        def slices(t, f):
            firsts = [(2 * t + core) * stride_rows + f * group for core in range(2)]
            return [incoming[first:first + group] for first in firsts]

        shares = incoming[pl.ds(2 * group, total, stride=2 * stride_rows)]
        lanes = lax.broadcasted_iota(jnp.int32, (group, rows), 1)
        picked = lanes == lax.rem(me, per) * group + lax.broadcasted_iota(jnp.int32, (group, rows), 0)

        def beyond_halo(t):
            mine = jnp.where(picked, jnp.broadcast_to(shares[t:t + 1], (group, rows)), 0.0)
            return jnp.where(lanes == 0, jnp.sum(mine, axis=1, keepdims=True), 0.0)

        source = []
        for t in range(total):
            low, high = slices(t, 1)
            high = high + beyond_halo(t)
            now = slices(t, 0)
            if t > 0:
                now = [x - y for x, y in zip(now, slices(t - 1, 0))]
            source.append(jnp.concatenate([low + now[0], high + now[1]], axis=1))
        source.append(jnp.concatenate(slices(total - 1, 0), axis=1))
        modal = by_table(jnp.concatenate(source, axis=0), cos_t_v)
        steps[...] = modal[:total * group].reshape(total, group, count)
        reach = sum(modal[t * group:(t + 1) * group] * slope[t] for t in range(total))
        last_rho = jnp.where(right, 0.0, modal[total * group:])
        cut[0] = pivots[total - 1] * reach - last_rho
        swap.start()

        out_kinds(place, side, lambda first, size: settle(outgoing, (total - 1) * size, out_sem.at[0]))
        value = jnp.zeros((group, count), jnp.float32)
        for i in range(total):
            value = (steps[start + stride * i] + value) * pivots[i]
            steps[start + stride * i] = value
        rest = jnp.zeros((group, count), jnp.float32)
        steps[start + stride * (total - 1)] = rest
        for i in reversed(range(total - 1)):
            rest = steps[start + stride * i] + pivots[i] * rest
            steps[start + stride * i] = rest
        near_edge = cos_t_v[:, rows - 8:rows + 8]
        swap.wait()
        pivot = pivots[total - 1]
        beyond = cut[1] - pivot * last_rho
        value = (value + pivot * beyond) * inverse

        def put(t, block, brink):
            for core in range(2):
                piece = block[:, core * rows:(core + 1) * rows]
                if t < total:
                    first = (core * total + t) * stride_rows
                    part = t // per * rows
                    back[first + group:first + 2 * group] = piece
                    back[first + 2 * group:first + filled] = brink[8 - core:9 - core, part:part + rows]
                if t > 0:
                    first = (core * total + t - 1) * stride_rows
                    back[first:first + group] = piece

        leading = steps[0] + slope[0] * value
        put(0, by_table(leading, cos_v), table_by_t(near_edge, jnp.concatenate([leading] * per, axis=0)))
        @pl.when(half == 0)
        def _():
            homeward(0, 0, group, group + 1).start()

            @pl.when(me != 0)
            def _():
                homeward(0, 1, group, group + 1).start()

        lines = [leading] + [steps[t] + slope[t] * value for t in range(1, total)]
        lines.append(jnp.where(right, 0.0, beyond + pivot * value))
        brink = table_by_t(near_edge, jnp.concatenate(lines[:total], axis=0))
        halfback = by_table(jnp.concatenate(lines[1:], axis=0), cos_v)
        for t in range(1, total + 1):
            put(t, halfback[(t - 1) * group:t * group], brink)

        def send_back(chip, core):
            back_kinds(base + chip, core, lambda first, size: homeward(chip, core, first, size).start())

        for chip in others:
            @pl.when(base + chip != 0)
            def _():
                send_back(chip, 0)
                send_back(chip, 1)

        @pl.when(place != 0)
        def _():
            send_back(me, 0)

        home[place_of(me, group, group + 8)] = back[place_of(total + me, group, group + 8)]

        @pl.when(jnp.logical_not(small))
        def _():
            home[place_of(me, 0, group)] = back[place_of(total + me, 0, group)]

    pl.when(solving)(solve)
    returned = 2 * (group + 1) + (total - 1) * (filled + 2 * group)
    pl.when(side == 0)(lambda: back_kinds(
        place, side, lambda first, size: settle(home, total * size, back_sem.at[1])))
    pl.when(solving)(lambda: back_kinds(
        place, side, lambda first, size: settle(home, (total - 1) * size, back_sem.at[1])))

    def modes(first):
        spans = [block * stride_rows + first for block in range(total)]
        return jnp.concatenate([home[at:at + group] for at in spans], axis=0)

    here = modes(group)
    offset = lax.rem(total - me, per) * group
    parts = count // rows
    row_at = lax.broadcasted_iota(jnp.int32, (per, rows), 0)
    lane_at = lax.broadcasted_iota(jnp.int32, (per, rows), 1)

    def find_edge():
        strip = []
        for part in range(parts):
            tail = home[pl.ds(part * per * stride_rows + 2 * group, per, stride=stride_rows)]
            tail = jnp.where(lane_at < group, pltpu.roll(tail, offset, 1), 0.0)
            tail = sum(jnp.where(row_at == d, pltpu.roll(tail, d * group, 1) if d else tail, 0.0) for d in range(per))
            strip.append(jnp.broadcast_to(jnp.sum(tail, axis=0, keepdims=True), (8, rows)))
        return by_table(jnp.concatenate(strip, axis=1), cos_v)[:1]

    upper = jnp.full((1, count), side, jnp.int32) == 0

    @pl.when(place != 0)
    def _():
        values = by_table_tn(jnp.concatenate([here, here - modes(0)], axis=1), cos_v)
        edge = find_edge()
        pot = values[:rows]
        fields[0] = pot
        fields[1] = values[rows:]
        beyond_row[...] = jnp.broadcast_to(jnp.where(upper, edge, pot[rows - 1:]), beyond_row.shape)

    @pl.when(place == 0)
    def _():
        edge = find_edge()
        pot = by_table_tn(here, cos_v)
        fields[0] = pot
        before_first = jnp.where(upper, pot[:1], edge)
        after_last = jnp.where(upper, edge, pot[rows - 1:])
        beyond_row[...] = jnp.broadcast_to(after_last, beyond_row.shape)
        left_of = jnp.where(col == 0, pot, pltpu.roll(pot, 1, 1))
        right_of = jnp.where(col == count - 1, pot, pltpu.roll(pot, count - 1, 1))
        over = jnp.where(row == 0, before_first, pltpu.roll(pot, 1, 0))
        under = jnp.where(row == rows - 1, after_last, pltpu.roll(pot, rows - 1, 0))
        bend = (pot - left_of) + (pot - right_of) + (pot - over) + (pot - under)
        following = (2.0 + regular_shift) * pot + space_weight * bend - first_source[...]
        fields[1] = pot - following

    pl.when(solving)(lambda: back_kinds(
        place, side, lambda first, size: settle(back, returned - size, back_sem.at[0])))
    pl.when(side == 0)(lambda: out_kinds(
        place, side, lambda first, size: settle(outgoing, total * size, out_sem.at[0])))


def finish_kernel(rho, mx, my, fields, beyond_row, out_d, out_x, out_y, res_d, res_x, res_y, store_sem):
    rows, count = rho.shape
    row = lax.broadcasted_iota(jnp.int32, (rows, count), 0)
    col = lax.broadcasted_iota(jnp.int32, (rows, count), 1)
    here = fields[0]
    after = jnp.where(row == rows - 1, beyond_row[0:1], pltpu.roll(here, rows - 1, 0))
    res_x[...] = mx[...] - flux_weight * (after - here)
    save_x = pltpu.make_async_copy(res_x, out_x.at[0], store_sem.at[0])
    save_x.start()
    grad = jnp.where(col == count - 1, 0.0, pltpu.roll(here, count - 1, 1) - here)
    res_y[...] = my[...] - flux_weight * grad
    save_y = pltpu.make_async_copy(res_y, out_y.at[0], store_sem.at[1])
    save_y.start()
    res_d[...] = rho[...] - fields[1]
    save_d = pltpu.make_async_copy(res_d, out_d.at[0], store_sem.at[2])
    save_d.start()
    for save in (save_x, save_y, save_d):
        save.wait()


def per_device_kernel(density, flux_x, flux_y):
    rows, count = density.shape[1:]
    total = lax.axis_size("tm") // 2
    group = count // total
    tables = host_tables(count, total)
    f32, bf16 = jnp.float32, jnp.bfloat16
    vm = pltpu.VMEM
    dma = pltpu.SemaphoreType.DMA
    slab = vm((rows, count), f32)
    tall = total * (2 * group + 8)
    scratch = [
        vm((2, 3, rows // 2, count), f32), vm((2, count, count), bf16), vm((2, count, count), bf16), vm((group, count), f32),
        slab, vm((8, count), f32), vm((tall, rows), f32), vm((2 * tall, rows), f32),
        vm((total, group, count), f32), vm((total, group, count), f32), vm((total, group, count), f32),
        vm((2, group, count), f32),
        vm((2 * tall, rows), f32), vm((tall, rows), f32),
        dma((5,)), dma((2,)), dma((2,)), dma((2,)), dma((2,)),
    ]
    anywhere = pl.BlockSpec(memory_space=pl.ANY)

    def kernel(*refs):
        step_kernel(total, *refs)

    local = pl.BlockSpec(memory_space=pltpu.VMEM)
    held = pl.pallas_call(
        kernel,
        out_shape=[slab, slab, slab, vm((2, rows, count), f32), vm((8, count), f32)],
        in_specs=[anywhere] * 6,
        out_specs=[local] * 5,
        scratch_shapes=scratch,
        compiler_params=pltpu.CompilerParams(collective_id=0, has_side_effects=True),
    )(density, flux_x, flux_y, *tables)
    return pl.pallas_call(
        finish_kernel,
        out_shape=[jax.ShapeDtypeStruct(density.shape, f32)] * 3,
        in_specs=[local] * 5,
        out_specs=[anywhere] * 3,
        scratch_shapes=[slab, slab, slab, dma((3,))],
    )(*[pltpu.with_memory_space_constraint(x, pltpu.VMEM) for x in held])


def per_device(density, flux_x, flux_y):
    slabs, rows, count = density.shape
    size = lax.axis_size("tm")
    fits = (
        slabs == 1 and lax.axis_size("space") == 2 and size >= 2 and size & (size - 1) == 0
        and count % (8 * size) == 0 and rows == 128 and 2 * rows == count
    )
    return (per_device_kernel if fits else per_device_xla)(density, flux_x, flux_y)


def solution(mesh):
    return jax.shard_map(
        per_device,
        mesh=mesh,
        in_specs=(P("tm", "space", None), P("tm", "space", None), P("tm", "space", None)),
        out_specs=(P("tm", "space", None), P("tm", "space", None), P("tm", "space", None)),
        check_vma=False,
    )
```

```python
import jax
import jax.numpy as jnp
import numpy as np
from jax import lax
from jax.experimental import pallas as pl
from jax.experimental.pallas import tpu as pltpu
from jax.sharding import PartitionSpec as P

NEWTON = 4


prox_weight = 1.0
regular_shift = 0.0001
space_weight = 0.25
flux_weight = 0.5
highest = lax.Precision.HIGHEST


def swapped(block, axis, distance):
    count = lax.axis_size(axis)
    route = []
    for low in range(count):
        high = low | 1 << distance
        if high != low and high < count:
            route += [(low, high), (high, low)]
    return lax.ppermute(block, axis, route)


def shifted(array, axis, by):
    size = lax.axis_size(axis)
    pairs = [(i, i + by) for i in range(size) if 0 <= i + by < size]
    return lax.ppermute(array, axis, pairs)


def kinetic_prox(density, flux_x, flux_y):
    square = flux_x * flux_x + flux_y * flux_y
    target = density + prox_weight + jnp.sqrt(square)
    for step in range(NEWTON):
        above = target + prox_weight
        value = (target - density) * above * above - 0.5 * prox_weight * square
        slope = above * (3.0 * target + prox_weight - 2.0 * density)
        target = target - value / slope
    shrink = target / (target + prox_weight)
    return (target, shrink * flux_x, shrink * flux_y)


def cosine_table(count):
    modes = jnp.arange(count).astype(jnp.float32)[:, None]
    points = jnp.arange(count).astype(jnp.float32)[None, :]
    table = jnp.cos(jnp.pi * modes * (2.0 * points + 1.0) / (2.0 * count))
    scales = jnp.where(modes == 0, jnp.sqrt(1.0 / count), jnp.sqrt(2.0 / count))
    return scales * table


def eigen_values(count):
    modes = jnp.arange(count).astype(jnp.float32)
    return 4.0 * jnp.sin(jnp.pi * modes / (2.0 * count)) ** 2


def move_outward(stacked, bit):
    return swapped(stacked, "tm", bit)


def move_homeward(stacked, bit):
    return swapped(stacked, "tm", bit)


def butterfly(blocks, mover):
    total = lax.axis_size("tm")
    position = lax.axis_index("tm")
    bit_count = total.bit_length() - 1
    for bit in range(bit_count):
        higher = total >> bit + 1
        lowest = 1 << bit
        shaped = blocks.reshape((higher, 2, lowest) + blocks.shape[1:])
        own_bit = position >> bit & 1
        keeping = jnp.where(own_bit == 0, shaped[:, 0], shaped[:, 1])
        leaving = jnp.where(own_bit == 0, shaped[:, 1], shaped[:, 0])
        arrived = mover(leaving, bit)
        first_half = jnp.where(own_bit == 0, keeping, arrived)
        second_half = jnp.where(own_bit == 0, arrived, keeping)
        blocks = jnp.stack([first_half, second_half], axis=1).reshape(blocks.shape)
    return blocks


def per_device_xla(density, flux_x, flux_y):
    slabs = density.shape[0]
    rows_local = density.shape[1]
    count = density.shape[2]
    parts = lax.axis_size("space")
    modes_local = count // parts
    own_start = lax.axis_index("space") * rows_local
    mode_start = lax.axis_index("space") * modes_local
    rho, mom_x, mom_y = kinetic_prox(density, flux_x, flux_y)
    prior = shifted(rho[slabs - 1], "tm", 1)
    before = jnp.concatenate([prior[None], rho[:-1]], axis=0)
    zeroed = mom_y.at[:, :, count - 1].set(0.0)
    div_second = zeroed - jnp.concatenate(
        [jnp.zeros_like(zeroed[:, :, :1]), zeroed[:, :, :-1]], axis=2
    )
    partial_source = rho - before + flux_weight * div_second
    table = cosine_table(count)
    diff_table = jnp.concatenate(
        [table[:, :-1] - table[:, 1:], jnp.zeros_like(table[:, :1])], axis=1
    )
    stacked = jnp.concatenate([partial_source, flux_weight * mom_x], axis=1)
    column_modes = jnp.einsum("tij,kj->itk", stacked, table, precision=highest)
    left = lax.dynamic_slice(
        table, (0, own_start), (modes_local * lax.axis_size("space"), rows_local)
    )
    left_diff = lax.dynamic_slice(
        diff_table, (0, own_start), (modes_local * lax.axis_size("space"), rows_local)
    )
    both = jnp.concatenate([left, left_diff], axis=1)
    modal = lax.psum_scatter(
        jnp.einsum("ki,itj->ktj", both, column_modes, precision=highest),
        "space",
        scatter_dimension=0,
        tiled=True,
    )
    lam = eigen_values(count)
    lam_local = lax.dynamic_slice_in_dim(lam, mode_start, modes_local)
    coeff = 2.0 + regular_shift + space_weight * (lam_local[:, None] + lam[None, :])
    devices_tm = lax.axis_size("tm")
    position = lax.axis_index("tm")
    lines_local = modes_local * count
    line_group = lines_local // devices_tm
    steps_all = devices_tm * slabs
    outgoing = jnp.transpose(modal, (0, 2, 1)).reshape(devices_tm, line_group, slabs)
    incoming = butterfly(outgoing, move_outward)
    series = jnp.transpose(incoming, (1, 0, 2)).reshape(line_group, steps_all)
    line_coeff = lax.dynamic_slice_in_dim(
        coeff.reshape(lines_local), position * line_group, line_group
    )
    column = lax.broadcasted_iota(jnp.int32, (line_group, steps_all), 1)
    below_band = jnp.where(column == 0, 0.0, -1.0).astype(jnp.float32)
    above_band = jnp.where(column == steps_all - 1, 0.0, -1.0).astype(jnp.float32)
    middle_band = jnp.broadcast_to(line_coeff[:, None], (line_group, steps_all))
    solution = lax.linalg.tridiagonal_solve(
        below_band, middle_band, above_band, series[:, :, None]
    )[:, :, 0]
    blocked = solution.reshape(line_group, devices_tm, slabs)
    leading_next = jnp.concatenate(
        [solution[:, slabs::slabs], jnp.zeros((line_group, 1), jnp.float32)], axis=1
    )
    padded = jnp.concatenate([blocked, leading_next[:, :, None]], axis=2)
    returned = butterfly(jnp.transpose(padded, (1, 0, 2)), move_homeward)
    local_lines = returned.reshape(modes_local, count, slabs + 1)
    extended = jnp.transpose(local_lines, (0, 2, 1))
    phihat = extended[:, :slabs, :]
    left = lax.dynamic_slice(
        table, (mode_start, 0), (modes_local, rows_local * lax.axis_size("space"))
    )
    left_diff = lax.dynamic_slice(
        diff_table, (mode_start, 0), (modes_local, rows_local * lax.axis_size("space"))
    )
    values = jnp.einsum("ki,ktj->itj", left, extended, precision=highest)
    slopes = -jnp.einsum("ki,ktj->itj", left_diff, phihat, precision=highest)
    gathered = lax.psum_scatter(
        jnp.concatenate([values, slopes], axis=1), "space", scatter_dimension=0, tiled=True
    )
    physical = jnp.einsum("itk,kj->tij", gathered, table, precision=highest)
    potential = physical[: slabs + 1]
    grad_first = physical[slabs + 1 :]
    present = potential[:slabs]
    grad_second = jnp.concatenate(
        [present[:, :, 1:] - present[:, :, :-1], jnp.zeros_like(present[:, :, :1])], axis=2
    )
    density_out = rho - (present - potential[1:])
    flux_x_out = mom_x - flux_weight * grad_first
    flux_y_out = mom_y - flux_weight * grad_second
    return (density_out, flux_x_out, flux_y_out)


MESH = pl.DeviceIdType.MESH
CHUNKS = 2


def split_table(table):
    high = table.astype(jnp.bfloat16)
    low = (table - high.astype(np.float32)).astype(jnp.bfloat16)
    return np.stack([high, low], axis=-3)


def host_tables(count, solvers):
    modes = np.arange(count, dtype=np.float64)[:, None]
    points = np.arange(count, dtype=np.float64)[None, :]
    table = np.cos(np.pi * modes * (2.0 * points + 1.0) / (2.0 * count))
    table = table * np.where(modes == 0, np.sqrt(1.0 / count), np.sqrt(2.0 / count))
    lam = 4.0 * np.sin(np.pi * np.arange(count) / (2.0 * count)) ** 2
    coeff = 2.0 + regular_shift + space_weight * (lam[:, None] + lam[None, :])
    f32 = np.float32
    return (
        split_table(table.astype(f32)),
        split_table(table.T.astype(f32)),
        coeff.reshape(solvers, count // solvers, count).astype(f32),
    )


def parted(x):
    high = x.astype(jnp.bfloat16)
    return high, (x - high.astype(jnp.float32)).astype(jnp.bfloat16)


def mul(a, b):
    return jnp.dot(a, b, preferred_element_type=jnp.float32)


def mul_nt(a, b):
    return lax.dot_general(a, b, (((1,), (1,)), ((), ())), preferred_element_type=jnp.float32)


def by_table(x, table):
    high, low = parted(x)
    return mul(high, table[0]) + (mul(high, table[1]) + mul(low, table[0]))


def table_by(table, x):
    high, low = parted(x)
    return mul(table[0], high) + (mul(table[1], high) + mul(table[0], low))


def table_by_t(table, x):
    high, low = parted(x)
    return mul_nt(table[0], high) + (mul_nt(table[1], high) + mul_nt(table[0], low))


def by_table_t(x, table):
    high, low = parted(x)
    return mul_nt(high, table[0]) + (mul_nt(high, table[1]) + mul_nt(low, table[0]))


def mul_tn(a, b):
    return lax.dot_general(a, b, (((0,), (0,)), ((), ())), preferred_element_type=jnp.float32)


def by_table_tn(x, table):
    high, low = parted(x)
    return mul_tn(high, table[0]) + (mul_tn(high, table[1]) + mul_tn(low, table[0]))


def step_kernel(
    total, density, flux_x, flux_y, cos, cos_t, coeff,
    rho, mx, my, fields, beyond_row,
    inputs, cos_v, cos_t_v, coeff_v,
    first_source, halo, outgoing, incoming, pivots, slope, steps, cut, back, home,
    load_sem, halo_sem, out_sem, cut_sem, back_sem,
):
    place = lax.axis_index("tm")
    half = place // total
    me = place - half * total
    base = half * total
    final = 2 * total - 1
    mirror = {"tm": lax.rem(place + total, 2 * total)}
    side = lax.axis_index("space")
    own = 2 * me + side
    rows, count = rho.shape
    full = coeff_v.shape[0]
    group = full // CHUNKS
    stride_rows, filled = 2 * group + 8, 2 * group + 1
    per = rows // full
    chunks = range(CHUNKS)
    solving = side == 1
    pieces = inputs.shape[0]
    tile = rows // pieces
    feeds = [
        pltpu.make_async_copy(src.at[0, pl.ds(j * tile, tile)], inputs.at[j, i], load_sem.at[j])
        for j in range(pieces) for i, src in enumerate((density, flux_x, flux_y))
    ]
    loads = [
        pltpu.make_async_copy(src, dst, load_sem.at[i])
        for i, (src, dst) in enumerate([(cos, cos_v), (coeff.at[me], coeff_v), (cos_t, cos_t_v)], pieces)
    ]
    for load in feeds + loads:
        load.start()

    def settle(ref, size, sem):
        span = ref.at[pl.ds(0, size)]
        pltpu.make_async_copy(span, span, sem).wait()

    bits = [1 << i for i in range(total.bit_length() - 1)]
    flips = [bit * (1 - 2 * lax.rem(me // bit, 2)) for bit in bits]
    masks = sorted(range(total), key=lambda m: (-bin(m).count("1"), -m))
    chips = [me + sum(f for f, bit in zip(flips, bits) if m & bit) for m in masks]
    others = [chip for chip, m in zip(chips, masks) if m]

    def device(chip, core):
        return {"tm": base + chip, "space": core}

    def choose(options):
        for test, action in options:
            pl.when(test)(action)

    barrier = pltpu.get_barrier_semaphore()
    for chip in others:
        pl.semaphore_signal(barrier, inc=1, device_id=device(chip, 1), device_id_type=MESH)
    pl.semaphore_signal(barrier, inc=1, device_id={"space": 1 - side}, device_id_type=MESH)

    @pl.when(solving)
    def _():
        for chip in others:
            pl.semaphore_signal(barrier, inc=1, device_id=device(chip, 0), device_id_type=MESH)
        pl.semaphore_signal(barrier, inc=1, device_id=mirror, device_id_type=MESH)

    for j in range(pieces):
        settle(inputs.at[j], 3, load_sem.at[j])
        span = slice(j * tile, (j + 1) * tile)
        rho[span], mx[span], my[span] = kinetic_prox(inputs[j, 0], inputs[j, 1], inputs[j, 2])

    row = lax.broadcasted_iota(jnp.int32, (rows, count), 0)
    col = lax.broadcasted_iota(jnp.int32, (rows, count), 1)
    bottom = side * rows + row == 2 * rows - 1
    wx = jnp.where(bottom, 0.0, mx[...])
    wy = jnp.where(col == count - 1, 0.0, my[...])
    div = flux_weight * (
        wx - jnp.where(row == 0, 0.0, pltpu.roll(wx, 1, 0)) + wy - pltpu.roll(wy, 1, 1))
    whole = rho[...] + div
    closing = jnp.full((rows, count), place, jnp.int32) == final
    pair = jnp.concatenate(
        [jnp.where(closing, 0.0, rho[...]), jnp.where(closing, whole, div)], axis=0)
    loads[0].wait()
    spread = table_by_t(cos_v, pair)
    crossing = by_table_t(jnp.broadcast_to(-flux_weight * wx[rows - 1:], (8, count)), cos_v)
    for k in chunks:
        for block in range(total):
            span = slice(block * full + k * group, block * full + (k + 1) * group)
            first = (k * total + block) * stride_rows
            for f in range(2):
                outgoing[first + f * group:first + (f + 1) * group] = spread[span, f * rows:(f + 1) * rows]
            part = block // per * rows
            outgoing[first + 2 * group:first + filled] = crossing[:1, part:part + rows]
    pl.semaphore_wait(barrier, total * (1 + side))

    def place_of(block, first, size):
        return pl.ds(pl.multiple_of(block * stride_rows + first, 8), size)

    def outward(k, chip, first, size):
        return pltpu.make_async_remote_copy(
            src_ref=outgoing.at[place_of(k * total + chip, first, size)],
            dst_ref=incoming.at[place_of(2 * k * total + own, first, size)],
            send_sem=out_sem.at[0], recv_sem=out_sem.at[1 + k],
            device_id=device(chip, 1), device_id_type=MESH)

    def out_kinds(chip, core, action):
        ending = chip == final
        inner = jnp.logical_not(ending)
        choose([
            (inner & (core == 0), lambda: action(0, filled)),
            (inner & (core == 1), lambda: action(0, 2 * group)),
            (ending & (core == 0), lambda: action(group, group + 1)),
            (ending & (core == 1), lambda: action(group, group)),
        ])

    def send_out(first, size):
        for k in chunks:
            for chip in others:
                outward(k, chip, first, size).start()

            @pl.when(side == 0)
            def _():
                outward(k, me, first, size).start()

    out_kinds(place, side, send_out)

    row_halo = pltpu.make_async_remote_copy(
        src_ref=mx.at[pl.ds(rows - 8, 8)], dst_ref=halo, send_sem=halo_sem.at[0],
        recv_sem=halo_sem.at[1], device_id={"space": 1 - side}, device_id_type=MESH)

    @pl.when(place == 0)
    def _():
        row_halo.start()

    @pl.when(half == 1)
    def _():
        for block in [2 * (k + 1) * total - 1 - core for k in chunks for core in range(2)]:
            incoming[pl.ds(block * stride_rows, group)] = jnp.zeros((group, rows), jnp.float32)

    small = (place == 0) | (place == final)

    @pl.when(small)
    def _():
        for block in range(CHUNKS * total):
            home[pl.ds(block * stride_rows, group)] = jnp.zeros((group, rows), jnp.float32)

    loads[1].wait()
    loads[2].wait()
    def swap(k):
        return pltpu.make_async_remote_copy(
            src_ref=cut.at[0, k], dst_ref=cut.at[1, k], send_sem=cut_sem.at[k],
            recv_sem=cut_sem.at[CHUNKS + k], device_id=mirror, device_id_type=MESH)

    def homeward(k, chip, core, first, size):
        return pltpu.make_async_remote_copy(
            src_ref=back.at[place_of((2 * k + core) * total + chip, first, size)],
            dst_ref=home.at[place_of(k * total + me, first, size)],
            send_sem=back_sem.at[0], recv_sem=back_sem.at[1],
            device_id=device(chip, core), device_id_type=MESH)

    def back_kinds(chip, core, action):
        ending = (chip == 0) | (chip == final)
        inner = jnp.logical_not(ending)
        choose([
            (ending, lambda: action(group, group + 1)),
            (inner & (core == 0), lambda: action(0, filled)),
            (inner & (core == 1), lambda: action(0, 2 * group)),
        ])

    @pl.when(place == 0)
    def _():
        row_halo.wait()
        prior = jnp.where(jnp.full((1, count), side, jnp.int32) == 1, halo[7:], 0.0)
        first_source[...] = whole - jnp.where(row == 0, flux_weight * prior, 0.0)

    def solve():
        for k in chunks:
            incoming[place_of(2 * k * total + own, 0, stride_rows)] = outgoing[place_of(k * total + me, 0, stride_rows)]
        c = coeff_v[...]
        pivot = 1.0 / c
        pivots[0] = pivot
        for t in range(1, total):
            pivot = 1.0 / (c - pivot)
            pivots[t] = pivot
        inverse = 1.0 / (1.0 - pivot * pivot)
        start, stride = half * (total - 1), 1 - 2 * half
        gain = jnp.ones((full, count), jnp.float32)
        slope[start + stride * (total - 1)] = gain
        for i in reversed(range(total - 1)):
            gain = gain * pivots[i]
            slope[start + stride * i] = gain
        right = jnp.full((group, count), half, jnp.int32) == 1
        lanes = lax.broadcasted_iota(jnp.int32, (group, rows), 1)
        modes_at = lax.broadcasted_iota(jnp.int32, (group, rows), 0)
        everything = total * (filled + 2 * group)
        ends = []
        for k in chunks:
            span = slice(k * group, (k + 1) * group)
            pl.when(half == 0)(lambda: out_kinds(
                place, side, lambda first, size: settle(incoming, everything - size, out_sem.at[1 + k])))
            pl.when(half == 1)(lambda: out_kinds(
                place, side, lambda first, size: settle(incoming, everything - 2 * group - size, out_sem.at[1 + k])))
            zero = 2 * k * total

            def slices(t, f):
                firsts = [(zero + 2 * t + core) * stride_rows + f * group for core in range(2)]
                return [incoming[first:first + group] for first in firsts]

            shares = incoming[pl.ds(zero * stride_rows + 2 * group, total, stride=2 * stride_rows)]
            picked = lanes == lax.rem(me, per) * full + k * group + modes_at

            def beyond_halo(t):
                mine = jnp.where(picked, jnp.broadcast_to(shares[t:t + 1], (group, rows)), 0.0)
                return jnp.where(lanes == 0, jnp.sum(mine, axis=1, keepdims=True), 0.0)

            source = []
            for t in range(total):
                low, high = slices(t, 1)
                high = high + beyond_halo(t)
                now = slices(t, 0)
                if t > 0:
                    now = [x - y for x, y in zip(now, slices(t - 1, 0))]
                source.append(jnp.concatenate([low + now[0], high + now[1]], axis=1))
            source.append(jnp.concatenate(slices(total - 1, 0), axis=1))
            modal = by_table(jnp.concatenate(source, axis=0), cos_t_v)
            reach = sum(modal[t * group:(t + 1) * group] * slope[t, span] for t in range(total))
            last_rho = jnp.where(right, 0.0, modal[total * group:])
            cut[0, k] = pivots[total - 1, span] * reach - last_rho
            swap(k).start()
            steps[:, span] = modal[:total * group].reshape(total, group, count)
            value = jnp.zeros((group, count), jnp.float32)
            for i in range(total):
                value = (steps[start + stride * i, span] + value) * pivots[i, span]
                steps[start + stride * i, span] = value
            rest = jnp.zeros((group, count), jnp.float32)
            steps[start + stride * (total - 1), span] = rest
            for i in reversed(range(total - 1)):
                rest = steps[start + stride * i, span] + pivots[i, span] * rest
                steps[start + stride * i, span] = rest
            ends.append((value, last_rho))

        out_kinds(place, side, lambda first, size: settle(outgoing, CHUNKS * (total - 1) * size, out_sem.at[0]))
        near_edge = cos_t_v[:, rows - 8:rows + 8]

        def put(k, t, block, brink):
            for core in range(2):
                piece = block[:, core * rows:(core + 1) * rows]
                zero = (2 * k + core) * total
                if t < total:
                    first = (zero + t) * stride_rows
                    back[first + group:first + 2 * group] = piece
                    back[first + 2 * group:first + filled] = brink[8 - core:9 - core]
                if t > 0:
                    first = (zero + t - 1) * stride_rows
                    back[first:first + group] = piece

        def send_back(k, chip, core):
            back_kinds(base + chip, core, lambda first, size: homeward(k, chip, core, first, size).start())

        for k in chunks:
            span = slice(k * group, (k + 1) * group)
            swap(k).wait()
            value, last_rho = ends[k]
            pivot = pivots[total - 1, span]
            beyond = cut[1, k] - pivot * last_rho
            value = (value + pivot * beyond) * inverse[span]
            leading = steps[0, span] + slope[0, span] * value
            put(k, 0, by_table(leading, cos_v),
                table_by_t(near_edge, jnp.concatenate([leading] * total, axis=0)))

            @pl.when(half == 0)
            def _():
                homeward(k, 0, 0, group, group + 1).start()

                @pl.when(me != 0)
                def _():
                    homeward(k, 0, 1, group, group + 1).start()

            lines = [leading] + [steps[t, span] + slope[t, span] * value for t in range(1, total)]
            lines.append(jnp.where(right, 0.0, beyond + pivot * value))
            brink = table_by_t(near_edge, jnp.concatenate(lines[:total], axis=0))
            halfback = by_table(jnp.concatenate(lines[1:], axis=0), cos_v)
            for t in range(1, total + 1):
                put(k, t, halfback[(t - 1) * group:t * group], brink)
            for chip in others:
                @pl.when(base + chip != 0)
                def _():
                    send_back(k, chip, 0)
                    send_back(k, chip, 1)

            @pl.when(place != 0)
            def _():
                send_back(k, me, 0)

            mine = (2 * k + 1) * total + me
            home[place_of(k * total + me, group, group + 8)] = back[place_of(mine, group, group + 8)]

            @pl.when(jnp.logical_not(small))
            def _():
                home[place_of(k * total + me, 0, group)] = back[place_of(mine, 0, group)]

    pl.when(solving)(solve)
    returned = 2 * (group + 1) + (total - 1) * (filled + 2 * group)
    pl.when(side == 0)(lambda: back_kinds(
        place, side, lambda first, size: settle(home, CHUNKS * total * size, back_sem.at[1])))
    pl.when(solving)(lambda: back_kinds(
        place, side, lambda first, size: settle(home, CHUNKS * (total - 1) * size, back_sem.at[1])))

    def modes(first):
        spans = [(k * total + block) * stride_rows + first for block in range(total) for k in chunks]
        return jnp.concatenate([home[at:at + group] for at in spans], axis=0)

    here = modes(group)
    offset = lax.rem(total - me, total) * group
    row_at = lax.broadcasted_iota(jnp.int32, (per, rows), 0)
    lane_at = lax.broadcasted_iota(jnp.int32, (per, rows), 1)

    def find_edge():
        strip = []
        for part in range(count // rows):
            placed = jnp.zeros((per, rows), jnp.float32)
            for k in chunks:
                tail = home[pl.ds((k * total + part * per) * stride_rows + 2 * group, per, stride=stride_rows)]
                tail = jnp.where(lane_at < group, pltpu.roll(tail, offset, 1), 0.0)
                for d in range(per):
                    shift = d * full + k * group
                    placed = placed + jnp.where(row_at == d, pltpu.roll(tail, shift, 1) if shift else tail, 0.0)
            strip.append(jnp.broadcast_to(jnp.sum(placed, axis=0, keepdims=True), (8, rows)))
        return by_table(jnp.concatenate(strip, axis=1), cos_v)[:1]

    upper = jnp.full((1, count), side, jnp.int32) == 0

    @pl.when(place != 0)
    def _():
        values = by_table_tn(jnp.concatenate([here, here - modes(0)], axis=1), cos_v)
        edge = find_edge()
        pot = values[:rows]
        fields[0] = pot
        fields[1] = values[rows:]
        beyond_row[...] = jnp.broadcast_to(jnp.where(upper, edge, pot[rows - 1:]), beyond_row.shape)

    @pl.when(place == 0)
    def _():
        edge = find_edge()
        pot = by_table_tn(here, cos_v)
        fields[0] = pot
        before_first = jnp.where(upper, pot[:1], edge)
        after_last = jnp.where(upper, edge, pot[rows - 1:])
        beyond_row[...] = jnp.broadcast_to(after_last, beyond_row.shape)
        left_of = jnp.where(col == 0, pot, pltpu.roll(pot, 1, 1))
        right_of = jnp.where(col == count - 1, pot, pltpu.roll(pot, count - 1, 1))
        over = jnp.where(row == 0, before_first, pltpu.roll(pot, 1, 0))
        under = jnp.where(row == rows - 1, after_last, pltpu.roll(pot, rows - 1, 0))
        bend = (pot - left_of) + (pot - right_of) + (pot - over) + (pot - under)
        following = (2.0 + regular_shift) * pot + space_weight * bend - first_source[...]
        fields[1] = pot - following

    pl.when(solving)(lambda: back_kinds(
        place, side, lambda first, size: settle(back, CHUNKS * (returned - size), back_sem.at[0])))
    pl.when(side == 0)(lambda: out_kinds(
        place, side, lambda first, size: settle(outgoing, CHUNKS * total * size, out_sem.at[0])))


def finish_kernel(rho, mx, my, fields, beyond_row, out_d, out_x, out_y, res_d, res_x, res_y, store_sem):
    rows, count = rho.shape
    row = lax.broadcasted_iota(jnp.int32, (rows, count), 0)
    col = lax.broadcasted_iota(jnp.int32, (rows, count), 1)
    here = fields[0]
    after = jnp.where(row == rows - 1, beyond_row[0:1], pltpu.roll(here, rows - 1, 0))
    res_x[...] = mx[...] - flux_weight * (after - here)
    save_x = pltpu.make_async_copy(res_x, out_x.at[0], store_sem.at[0])
    save_x.start()
    grad = jnp.where(col == count - 1, 0.0, pltpu.roll(here, count - 1, 1) - here)
    res_y[...] = my[...] - flux_weight * grad
    save_y = pltpu.make_async_copy(res_y, out_y.at[0], store_sem.at[1])
    save_y.start()
    res_d[...] = rho[...] - fields[1]
    save_d = pltpu.make_async_copy(res_d, out_d.at[0], store_sem.at[2])
    save_d.start()
    for save in (save_x, save_y, save_d):
        save.wait()


def per_device_kernel(density, flux_x, flux_y):
    rows, count = density.shape[1:]
    total = lax.axis_size("tm") // 2
    group = count // total
    tables = host_tables(count, total)
    f32, bf16 = jnp.float32, jnp.bfloat16
    vm = pltpu.VMEM
    dma = pltpu.SemaphoreType.DMA
    slab = vm((rows, count), f32)
    tall = total * (2 * group + 8 * CHUNKS)
    scratch = [
        vm((2, 3, rows // 2, count), f32), vm((2, count, count), bf16), vm((2, count, count), bf16), vm((group, count), f32),
        slab, vm((8, count), f32), vm((tall, rows), f32), vm((2 * tall, rows), f32),
        vm((total, group, count), f32), vm((total, group, count), f32), vm((total, group, count), f32),
        vm((2, CHUNKS, group // CHUNKS, count), f32),
        vm((2 * tall, rows), f32), vm((tall, rows), f32),
        dma((5,)), dma((2,)), dma((1 + CHUNKS,)), dma((2 * CHUNKS,)), dma((2,)),
    ]
    anywhere = pl.BlockSpec(memory_space=pl.ANY)

    def kernel(*refs):
        step_kernel(total, *refs)

    local = pl.BlockSpec(memory_space=pltpu.VMEM)
    held = pl.pallas_call(
        kernel,
        out_shape=[slab, slab, slab, vm((2, rows, count), f32), vm((8, count), f32)],
        in_specs=[anywhere] * 6,
        out_specs=[local] * 5,
        scratch_shapes=scratch,
        compiler_params=pltpu.CompilerParams(collective_id=0, has_side_effects=True),
    )(density, flux_x, flux_y, *tables)
    return pl.pallas_call(
        finish_kernel,
        out_shape=[jax.ShapeDtypeStruct(density.shape, f32)] * 3,
        in_specs=[local] * 5,
        out_specs=[anywhere] * 3,
        scratch_shapes=[slab, slab, slab, dma((3,))],
    )(*[pltpu.with_memory_space_constraint(x, pltpu.VMEM) for x in held])


def per_device(density, flux_x, flux_y):
    slabs, rows, count = density.shape
    size = lax.axis_size("tm")
    fits = (
        slabs == 1 and lax.axis_size("space") == 2 and size >= 2 and size & (size - 1) == 0
        and count % (8 * size) == 0 and rows == 128 and 2 * rows == count
    )
    return (per_device_kernel if fits else per_device_xla)(density, flux_x, flux_y)


def solution(mesh):
    return jax.shard_map(
        per_device,
        mesh=mesh,
        in_specs=(P("tm", "space", None), P("tm", "space", None), P("tm", "space", None)),
        out_specs=(P("tm", "space", None), P("tm", "space", None), P("tm", "space", None)),
        check_vma=False,
    )
```

```python
import jax
import jax.numpy as jnp
import numpy as np
from jax import lax
from jax.experimental import pallas as pl
from jax.experimental.pallas import tpu as pltpu
from jax.sharding import PartitionSpec as P

NEWTON = 4


prox_weight = 1.0
regular_shift = 0.0001
space_weight = 0.25
flux_weight = 0.5
highest = lax.Precision.HIGHEST


def swapped(block, axis, distance):
    count = lax.axis_size(axis)
    route = []
    for low in range(count):
        high = low | 1 << distance
        if high != low and high < count:
            route += [(low, high), (high, low)]
    return lax.ppermute(block, axis, route)


def shifted(array, axis, by):
    size = lax.axis_size(axis)
    pairs = [(i, i + by) for i in range(size) if 0 <= i + by < size]
    return lax.ppermute(array, axis, pairs)


def kinetic_prox(density, flux_x, flux_y):
    square = flux_x * flux_x + flux_y * flux_y
    target = density + prox_weight + jnp.sqrt(square)
    for step in range(NEWTON):
        above = target + prox_weight
        value = (target - density) * above * above - 0.5 * prox_weight * square
        slope = above * (3.0 * target + prox_weight - 2.0 * density)
        target = target - value / slope
    shrink = target / (target + prox_weight)
    return (target, shrink * flux_x, shrink * flux_y)


def cosine_table(count):
    modes = jnp.arange(count).astype(jnp.float32)[:, None]
    points = jnp.arange(count).astype(jnp.float32)[None, :]
    table = jnp.cos(jnp.pi * modes * (2.0 * points + 1.0) / (2.0 * count))
    scales = jnp.where(modes == 0, jnp.sqrt(1.0 / count), jnp.sqrt(2.0 / count))
    return scales * table


def eigen_values(count):
    modes = jnp.arange(count).astype(jnp.float32)
    return 4.0 * jnp.sin(jnp.pi * modes / (2.0 * count)) ** 2


def move_outward(stacked, bit):
    return swapped(stacked, "tm", bit)


def move_homeward(stacked, bit):
    return swapped(stacked, "tm", bit)


def butterfly(blocks, mover):
    total = lax.axis_size("tm")
    position = lax.axis_index("tm")
    bit_count = total.bit_length() - 1
    for bit in range(bit_count):
        higher = total >> bit + 1
        lowest = 1 << bit
        shaped = blocks.reshape((higher, 2, lowest) + blocks.shape[1:])
        own_bit = position >> bit & 1
        keeping = jnp.where(own_bit == 0, shaped[:, 0], shaped[:, 1])
        leaving = jnp.where(own_bit == 0, shaped[:, 1], shaped[:, 0])
        arrived = mover(leaving, bit)
        first_half = jnp.where(own_bit == 0, keeping, arrived)
        second_half = jnp.where(own_bit == 0, arrived, keeping)
        blocks = jnp.stack([first_half, second_half], axis=1).reshape(blocks.shape)
    return blocks


def per_device_xla(density, flux_x, flux_y):
    slabs = density.shape[0]
    rows_local = density.shape[1]
    count = density.shape[2]
    parts = lax.axis_size("space")
    modes_local = count // parts
    own_start = lax.axis_index("space") * rows_local
    mode_start = lax.axis_index("space") * modes_local
    rho, mom_x, mom_y = kinetic_prox(density, flux_x, flux_y)
    prior = shifted(rho[slabs - 1], "tm", 1)
    before = jnp.concatenate([prior[None], rho[:-1]], axis=0)
    zeroed = mom_y.at[:, :, count - 1].set(0.0)
    div_second = zeroed - jnp.concatenate(
        [jnp.zeros_like(zeroed[:, :, :1]), zeroed[:, :, :-1]], axis=2
    )
    partial_source = rho - before + flux_weight * div_second
    table = cosine_table(count)
    diff_table = jnp.concatenate(
        [table[:, :-1] - table[:, 1:], jnp.zeros_like(table[:, :1])], axis=1
    )
    stacked = jnp.concatenate([partial_source, flux_weight * mom_x], axis=1)
    column_modes = jnp.einsum("tij,kj->itk", stacked, table, precision=highest)
    left = lax.dynamic_slice(
        table, (0, own_start), (modes_local * lax.axis_size("space"), rows_local)
    )
    left_diff = lax.dynamic_slice(
        diff_table, (0, own_start), (modes_local * lax.axis_size("space"), rows_local)
    )
    both = jnp.concatenate([left, left_diff], axis=1)
    modal = lax.psum_scatter(
        jnp.einsum("ki,itj->ktj", both, column_modes, precision=highest),
        "space",
        scatter_dimension=0,
        tiled=True,
    )
    lam = eigen_values(count)
    lam_local = lax.dynamic_slice_in_dim(lam, mode_start, modes_local)
    coeff = 2.0 + regular_shift + space_weight * (lam_local[:, None] + lam[None, :])
    devices_tm = lax.axis_size("tm")
    position = lax.axis_index("tm")
    lines_local = modes_local * count
    line_group = lines_local // devices_tm
    steps_all = devices_tm * slabs
    outgoing = jnp.transpose(modal, (0, 2, 1)).reshape(devices_tm, line_group, slabs)
    incoming = butterfly(outgoing, move_outward)
    series = jnp.transpose(incoming, (1, 0, 2)).reshape(line_group, steps_all)
    line_coeff = lax.dynamic_slice_in_dim(
        coeff.reshape(lines_local), position * line_group, line_group
    )
    column = lax.broadcasted_iota(jnp.int32, (line_group, steps_all), 1)
    below_band = jnp.where(column == 0, 0.0, -1.0).astype(jnp.float32)
    above_band = jnp.where(column == steps_all - 1, 0.0, -1.0).astype(jnp.float32)
    middle_band = jnp.broadcast_to(line_coeff[:, None], (line_group, steps_all))
    solution = lax.linalg.tridiagonal_solve(
        below_band, middle_band, above_band, series[:, :, None]
    )[:, :, 0]
    blocked = solution.reshape(line_group, devices_tm, slabs)
    leading_next = jnp.concatenate(
        [solution[:, slabs::slabs], jnp.zeros((line_group, 1), jnp.float32)], axis=1
    )
    padded = jnp.concatenate([blocked, leading_next[:, :, None]], axis=2)
    returned = butterfly(jnp.transpose(padded, (1, 0, 2)), move_homeward)
    local_lines = returned.reshape(modes_local, count, slabs + 1)
    extended = jnp.transpose(local_lines, (0, 2, 1))
    phihat = extended[:, :slabs, :]
    left = lax.dynamic_slice(
        table, (mode_start, 0), (modes_local, rows_local * lax.axis_size("space"))
    )
    left_diff = lax.dynamic_slice(
        diff_table, (mode_start, 0), (modes_local, rows_local * lax.axis_size("space"))
    )
    values = jnp.einsum("ki,ktj->itj", left, extended, precision=highest)
    slopes = -jnp.einsum("ki,ktj->itj", left_diff, phihat, precision=highest)
    gathered = lax.psum_scatter(
        jnp.concatenate([values, slopes], axis=1), "space", scatter_dimension=0, tiled=True
    )
    physical = jnp.einsum("itk,kj->tij", gathered, table, precision=highest)
    potential = physical[: slabs + 1]
    grad_first = physical[slabs + 1 :]
    present = potential[:slabs]
    grad_second = jnp.concatenate(
        [present[:, :, 1:] - present[:, :, :-1], jnp.zeros_like(present[:, :, :1])], axis=2
    )
    density_out = rho - (present - potential[1:])
    flux_x_out = mom_x - flux_weight * grad_first
    flux_y_out = mom_y - flux_weight * grad_second
    return (density_out, flux_x_out, flux_y_out)


MESH = pl.DeviceIdType.MESH
CHUNKS = 2


def split_table(table):
    high = table.astype(jnp.bfloat16)
    low = (table - high.astype(np.float32)).astype(jnp.bfloat16)
    return np.stack([high, low], axis=-3)


def host_tables(count, solvers):
    modes = np.arange(count, dtype=np.float64)[:, None]
    points = np.arange(count, dtype=np.float64)[None, :]
    table = np.cos(np.pi * modes * (2.0 * points + 1.0) / (2.0 * count))
    table = table * np.where(modes == 0, np.sqrt(1.0 / count), np.sqrt(2.0 / count))
    lam = 4.0 * np.sin(np.pi * np.arange(count) / (2.0 * count)) ** 2
    coeff = 2.0 + regular_shift + space_weight * (lam[:, None] + lam[None, :])
    f32 = np.float32
    return (
        split_table(table.astype(f32)),
        split_table(table.T.astype(f32)),
        coeff.reshape(solvers, count // solvers, count).astype(f32),
    )


def parted(x):
    high = x.astype(jnp.bfloat16)
    return high, (x - high.astype(jnp.float32)).astype(jnp.bfloat16)


def mul(a, b):
    return jnp.dot(a, b, preferred_element_type=jnp.float32)


def mul_nt(a, b):
    return lax.dot_general(a, b, (((1,), (1,)), ((), ())), preferred_element_type=jnp.float32)


def by_table(x, table):
    high, low = parted(x)
    return mul(high, table[0]) + (mul(high, table[1]) + mul(low, table[0]))


def table_by(table, x):
    high, low = parted(x)
    return mul(table[0], high) + (mul(table[1], high) + mul(table[0], low))


def table_by_t(table, x):
    high, low = parted(x)
    return mul_nt(table[0], high) + (mul_nt(table[1], high) + mul_nt(table[0], low))


def by_table_t(x, table):
    high, low = parted(x)
    return mul_nt(high, table[0]) + (mul_nt(high, table[1]) + mul_nt(low, table[0]))


def mul_tn(a, b):
    return lax.dot_general(a, b, (((0,), (0,)), ((), ())), preferred_element_type=jnp.float32)


def by_table_tn(x, table):
    high, low = parted(x)
    return mul_tn(high, table[0]) + (mul_tn(high, table[1]) + mul_tn(low, table[0]))


def step_kernel(
    total, density, flux_x, flux_y, cos, cos_t, coeff,
    rho, mx, my, fields, beyond_row,
    inputs, cos_v, cos_t_v, coeff_v,
    first_source, halo, outgoing, incoming, pivots, slope, steps, cut, back, home,
    ready, load_sem, halo_sem, out_sem, cut_sem, back_sem,
):
    place = lax.axis_index("tm")
    half = place // total
    me = place - half * total
    base = half * total
    final = 2 * total - 1
    mirror = {"tm": lax.rem(place + total, 2 * total)}
    side = lax.axis_index("space")
    own = 2 * me + side
    rows, count = rho.shape
    full = coeff_v.shape[0]
    group = full // CHUNKS
    stride_rows, filled = 2 * group + 8, 2 * group + 1
    per = rows // full
    chunks = range(CHUNKS)
    solving = side == 1
    pieces = inputs.shape[0]
    tile = rows // pieces
    feeds = [
        pltpu.make_async_copy(src.at[0, pl.ds(j * tile, tile)], inputs.at[j, i], load_sem.at[j])
        for j in range(pieces) for i, src in enumerate((density, flux_x, flux_y))
    ]
    loads = [
        pltpu.make_async_copy(src, dst, load_sem.at[i])
        for i, (src, dst) in enumerate([(cos, cos_v), (coeff.at[me], coeff_v), (cos_t, cos_t_v)], pieces)
    ]
    strips = [
        pltpu.make_async_copy(cos.at[i, pl.ds(j * rows, rows)], cos_v.at[i, pl.ds(j * rows, rows)], load_sem.at[pieces])
        for i in range(2) for j in range(2)
    ]
    for load in feeds + strips:
        load.start()

    def settle(ref, size, sem):
        span = ref.at[pl.ds(0, size)]
        pltpu.make_async_copy(span, span, sem).wait()

    bits = [1 << i for i in range(total.bit_length() - 1)]
    flips = [bit * (1 - 2 * lax.rem(me // bit, 2)) for bit in bits]
    masks = sorted(range(total), key=lambda m: (-bin(m).count("1"), -m))
    chips = [me + sum(f for f, bit in zip(flips, bits) if m & bit) for m in masks]
    others = [chip for chip, m in zip(chips, masks) if m]

    def device(chip, core):
        return {"tm": base + chip, "space": core}

    def choose(options):
        for test, action in options:
            pl.when(test)(action)

    barrier = pltpu.get_barrier_semaphore()

    @pl.when(solving)
    def _():
        for core in (1, 0):
            for chip in others:
                pl.semaphore_signal(barrier, inc=1, device_id=device(chip, core), device_id_type=MESH)
        pl.semaphore_signal(barrier, inc=1, device_id=device(me, 0), device_id_type=MESH)

        @pl.when(half == 0)
        def _():
            pl.semaphore_signal(barrier, inc=1, device_id=mirror, device_id_type=MESH)

    for j in range(pieces):
        settle(inputs.at[j], 3, load_sem.at[j])
        span = slice(j * tile, (j + 1) * tile)
        rho[span], mx[span], my[span] = kinetic_prox(inputs[j, 0], inputs[j, 1], inputs[j, 2])

    for load in loads[1:]:
        load.start()
    row = lax.broadcasted_iota(jnp.int32, (rows, count), 0)
    col = lax.broadcasted_iota(jnp.int32, (rows, count), 1)
    bottom = side * rows + row == 2 * rows - 1
    wx = jnp.where(bottom, 0.0, mx[...])
    wy = jnp.where(col == count - 1, 0.0, my[...])
    div = flux_weight * (
        wx - jnp.where(row == 0, 0.0, pltpu.roll(wx, 1, 0)) + wy - pltpu.roll(wy, 1, 1))
    whole = rho[...] + div
    closing = jnp.full((rows, count), place, jnp.int32) == final
    pair = jnp.concatenate(
        [jnp.where(closing, 0.0, rho[...]), jnp.where(closing, whole, div)], axis=0)
    loads[0].wait()
    spread = table_by_t(cos_v, pair)
    crossing = by_table_t(jnp.broadcast_to(-flux_weight * wx[rows - 1:], (8, count)), cos_v)
    for k in chunks:
        for block in range(total):
            span = slice(block * full + k * group, block * full + (k + 1) * group)
            first = (k * total + block) * stride_rows
            for f in range(2):
                outgoing[first + f * group:first + (f + 1) * group] = spread[span, f * rows:(f + 1) * rows]
            part = block // per * rows
            outgoing[first + 2 * group:first + filled] = crossing[:1, part:part + rows]
    pl.semaphore_wait(barrier, total + side * (half - 1))

    def place_of(block, first, size):
        return pl.ds(pl.multiple_of(block * stride_rows + first, 8), size)

    def outward(k, chip, first, size):
        return pltpu.make_async_remote_copy(
            src_ref=outgoing.at[place_of(k * total + chip, first, size)],
            dst_ref=incoming.at[place_of(2 * k * total + own, first, size)],
            send_sem=out_sem.at[0], recv_sem=out_sem.at[1 + k],
            device_id=device(chip, 1), device_id_type=MESH)

    def out_kinds(chip, core, action):
        ending = chip == final
        inner = jnp.logical_not(ending)
        choose([
            (inner & (core == 0), lambda: action(0, filled)),
            (inner & (core == 1), lambda: action(0, 2 * group)),
            (ending & (core == 0), lambda: action(group, group + 1)),
            (ending & (core == 1), lambda: action(group, group)),
        ])

    def send_out(first, size):
        for k in chunks:
            for chip in others:
                outward(k, chip, first, size).start()

            @pl.when(side == 0)
            def _():
                outward(k, me, first, size).start()

    out_kinds(place, side, send_out)

    @pl.when(side == 0)
    def _():
        for chip in chips:
            pl.semaphore_signal(ready.at[0], inc=1, device_id=device(chip, 1), device_id_type=MESH)

    @pl.when(solving & (half == 1))
    def _():
        pl.semaphore_signal(ready.at[1], inc=1, device_id=mirror, device_id_type=MESH)

    row_halo = pltpu.make_async_remote_copy(
        src_ref=mx.at[pl.ds(rows - 8, 8)], dst_ref=halo, send_sem=halo_sem.at[0],
        recv_sem=halo_sem.at[1], device_id={"space": 1 - side}, device_id_type=MESH)

    @pl.when((place == 0) & (side == 0))
    def _():
        row_halo.start()

    @pl.when(half == 1)
    def _():
        for block in [2 * (k + 1) * total - 1 - core for k in chunks for core in range(2)]:
            incoming[pl.ds(block * stride_rows, group)] = jnp.zeros((group, rows), jnp.float32)

    small = (place == 0) | (place == final)

    @pl.when(small)
    def _():
        for block in range(CHUNKS * total):
            home[pl.ds(block * stride_rows, group)] = jnp.zeros((group, rows), jnp.float32)

    loads[1].wait()
    loads[2].wait()
    def swap(k):
        return pltpu.make_async_remote_copy(
            src_ref=cut.at[0, k], dst_ref=cut.at[1, k], send_sem=cut_sem.at[k],
            recv_sem=cut_sem.at[CHUNKS + k], device_id=mirror, device_id_type=MESH)

    def homeward(k, chip, core, first, size):
        return pltpu.make_async_remote_copy(
            src_ref=back.at[place_of((2 * k + core) * total + chip, first, size)],
            dst_ref=home.at[place_of(k * total + me, first, size)],
            send_sem=back_sem.at[0], recv_sem=back_sem.at[1],
            device_id=device(chip, core), device_id_type=MESH)

    def back_kinds(chip, core, action):
        ending = (chip == 0) | (chip == final)
        inner = jnp.logical_not(ending)
        choose([
            (ending, lambda: action(group, group + 1)),
            (inner & (core == 0), lambda: action(0, filled)),
            (inner & (core == 1), lambda: action(0, 2 * group)),
        ])

    @pl.when(place == 0)
    def _():
        pl.when(side == 0)(row_halo.wait_send)
        pl.when(solving)(row_halo.wait_recv)
        prior = jnp.where(jnp.full((1, count), side, jnp.int32) == 1, halo[7:], 0.0)
        first_source[...] = whole - jnp.where(row == 0, flux_weight * prior, 0.0)

    def solve():
        for k in chunks:
            incoming[place_of(2 * k * total + own, 0, stride_rows)] = outgoing[place_of(k * total + me, 0, stride_rows)]
        c = coeff_v[...]
        pivot = 1.0 / c
        pivots[0] = pivot
        for t in range(1, total):
            pivot = 1.0 / (c - pivot)
            pivots[t] = pivot
        inverse = 1.0 / (1.0 - pivot * pivot)
        start, stride = half * (total - 1), 1 - 2 * half
        gain = jnp.ones((full, count), jnp.float32)
        slope[start + stride * (total - 1)] = gain
        for i in reversed(range(total - 1)):
            gain = gain * pivots[i]
            slope[start + stride * i] = gain
        right = jnp.full((group, count), half, jnp.int32) == 1
        lanes = lax.broadcasted_iota(jnp.int32, (group, rows), 1)
        modes_at = lax.broadcasted_iota(jnp.int32, (group, rows), 0)
        everything = total * (filled + 2 * group)
        ends = []
        for k in chunks:
            span = slice(k * group, (k + 1) * group)
            pl.when(half == 0)(lambda: out_kinds(
                place, side, lambda first, size: settle(incoming, everything - size, out_sem.at[1 + k])))
            pl.when(half == 1)(lambda: out_kinds(
                place, side, lambda first, size: settle(incoming, everything - 2 * group - size, out_sem.at[1 + k])))
            zero = 2 * k * total

            def slices(t, f):
                firsts = [(zero + 2 * t + core) * stride_rows + f * group for core in range(2)]
                return [incoming[first:first + group] for first in firsts]

            shares = incoming[pl.ds(zero * stride_rows + 2 * group, total, stride=2 * stride_rows)]
            picked = lanes == lax.rem(me, per) * full + k * group + modes_at

            def beyond_halo(t):
                mine = jnp.where(picked, jnp.broadcast_to(shares[t:t + 1], (group, rows)), 0.0)
                return jnp.where(lanes == 0, jnp.sum(mine, axis=1, keepdims=True), 0.0)

            source = []
            for t in range(total):
                low, high = slices(t, 1)
                high = high + beyond_halo(t)
                now = slices(t, 0)
                if t > 0:
                    now = [x - y for x, y in zip(now, slices(t - 1, 0))]
                source.append(jnp.concatenate([low + now[0], high + now[1]], axis=1))
            source.append(jnp.concatenate(slices(total - 1, 0), axis=1))
            modal = by_table(jnp.concatenate(source, axis=0), cos_t_v)
            reach = sum(modal[t * group:(t + 1) * group] * slope[t, span] for t in range(total))
            last_rho = jnp.where(right, 0.0, modal[total * group:])
            cut[0, k] = pivots[total - 1, span] * reach - last_rho
            if k == 0:
                pl.when(half == 0)(lambda: pl.semaphore_wait(ready.at[1], 1))
            swap(k).start()
            steps[:, span] = modal[:total * group].reshape(total, group, count)
            ends.append(last_rho)

        value = jnp.zeros((full, count), jnp.float32)
        for i in range(total):
            value = (steps[start + stride * i] + value) * pivots[i]
            steps[start + stride * i] = value
        reached = value
        rest = jnp.zeros((full, count), jnp.float32)
        steps[start + stride * (total - 1)] = rest
        for i in reversed(range(total - 1)):
            rest = steps[start + stride * i] + pivots[i] * rest
            steps[start + stride * i] = rest

        out_kinds(place, side, lambda first, size: settle(outgoing, CHUNKS * (total - 1) * size, out_sem.at[0]))
        near_edge = cos_t_v[:, rows - 8:rows + 8]
        pl.semaphore_wait(ready.at[0], total)

        def put(k, t, block, brink):
            for core in range(2):
                piece = block[:, core * rows:(core + 1) * rows]
                zero = (2 * k + core) * total
                if t < total:
                    first = (zero + t) * stride_rows
                    back[first + group:first + 2 * group] = piece
                    back[first + 2 * group:first + filled] = brink[8 - core:9 - core]
                if t > 0:
                    first = (zero + t - 1) * stride_rows
                    back[first:first + group] = piece

        def send_back(k, chip, core):
            back_kinds(base + chip, core, lambda first, size: homeward(k, chip, core, first, size).start())

        for k in chunks:
            span = slice(k * group, (k + 1) * group)
            swap(k).wait()
            value, last_rho = reached[span], ends[k]
            pivot = pivots[total - 1, span]
            beyond = cut[1, k] - pivot * last_rho
            value = (value + pivot * beyond) * inverse[span]
            leading = steps[0, span] + slope[0, span] * value
            put(k, 0, by_table(leading, cos_v),
                table_by_t(near_edge, jnp.concatenate([leading] * total, axis=0)))

            @pl.when(half == 0)
            def _():
                homeward(k, 0, 0, group, group + 1).start()

                @pl.when(me != 0)
                def _():
                    homeward(k, 0, 1, group, group + 1).start()

            lines = [leading] + [steps[t, span] + slope[t, span] * value for t in range(1, total)]
            lines.append(jnp.where(right, 0.0, beyond + pivot * value))
            brink = table_by_t(near_edge, jnp.concatenate(lines[:total], axis=0))
            halfback = by_table(jnp.concatenate(lines[1:], axis=0), cos_v)
            for t in range(1, total + 1):
                put(k, t, halfback[(t - 1) * group:t * group], brink)
            for chip in others:
                @pl.when(base + chip != 0)
                def _():
                    send_back(k, chip, 0)
                    send_back(k, chip, 1)

            @pl.when(place != 0)
            def _():
                send_back(k, me, 0)

            mine = (2 * k + 1) * total + me
            home[place_of(k * total + me, group, group + 8)] = back[place_of(mine, group, group + 8)]

            @pl.when(jnp.logical_not(small))
            def _():
                home[place_of(k * total + me, 0, group)] = back[place_of(mine, 0, group)]

    pl.when(solving)(solve)
    returned = 2 * (group + 1) + (total - 1) * (filled + 2 * group)
    pl.when(side == 0)(lambda: back_kinds(
        place, side, lambda first, size: settle(home, CHUNKS * total * size, back_sem.at[1])))
    pl.when(solving)(lambda: back_kinds(
        place, side, lambda first, size: settle(home, CHUNKS * (total - 1) * size, back_sem.at[1])))

    def modes(first):
        spans = [(k * total + block) * stride_rows + first for block in range(total) for k in chunks]
        return jnp.concatenate([home[at:at + group] for at in spans], axis=0)

    here = modes(group)
    offset = lax.rem(total - me, total) * group
    row_at = lax.broadcasted_iota(jnp.int32, (per, rows), 0)
    lane_at = lax.broadcasted_iota(jnp.int32, (per, rows), 1)

    def find_edge():
        strip = []
        for part in range(count // rows):
            placed = jnp.zeros((per, rows), jnp.float32)
            for k in chunks:
                tail = home[pl.ds((k * total + part * per) * stride_rows + 2 * group, per, stride=stride_rows)]
                tail = jnp.where(lane_at < group, pltpu.roll(tail, offset, 1), 0.0)
                for d in range(per):
                    shift = d * full + k * group
                    placed = placed + jnp.where(row_at == d, pltpu.roll(tail, shift, 1) if shift else tail, 0.0)
            strip.append(jnp.broadcast_to(jnp.sum(placed, axis=0, keepdims=True), (8, rows)))
        return by_table(jnp.concatenate(strip, axis=1), cos_v)[:1]

    upper = jnp.full((1, count), side, jnp.int32) == 0

    @pl.when(place != 0)
    def _():
        values = by_table_tn(jnp.concatenate([here, here - modes(0)], axis=1), cos_v)
        edge = find_edge()
        pot = values[:rows]
        fields[0] = pot
        fields[1] = values[rows:]
        beyond_row[...] = jnp.broadcast_to(jnp.where(upper, edge, pot[rows - 1:]), beyond_row.shape)

    @pl.when(place == 0)
    def _():
        edge = find_edge()
        pot = by_table_tn(here, cos_v)
        fields[0] = pot
        before_first = jnp.where(upper, pot[:1], edge)
        after_last = jnp.where(upper, edge, pot[rows - 1:])
        beyond_row[...] = jnp.broadcast_to(after_last, beyond_row.shape)
        left_of = jnp.where(col == 0, pot, pltpu.roll(pot, 1, 1))
        right_of = jnp.where(col == count - 1, pot, pltpu.roll(pot, count - 1, 1))
        over = jnp.where(row == 0, before_first, pltpu.roll(pot, 1, 0))
        under = jnp.where(row == rows - 1, after_last, pltpu.roll(pot, rows - 1, 0))
        bend = (pot - left_of) + (pot - right_of) + (pot - over) + (pot - under)
        following = (2.0 + regular_shift) * pot + space_weight * bend - first_source[...]
        fields[1] = pot - following

    pl.when(solving)(lambda: back_kinds(
        place, side, lambda first, size: settle(back, CHUNKS * (returned - size), back_sem.at[0])))
    pl.when(side == 0)(lambda: out_kinds(
        place, side, lambda first, size: settle(outgoing, CHUNKS * total * size, out_sem.at[0])))


def finish_kernel(rho, mx, my, fields, beyond_row, out_d, out_x, out_y, res_d, res_x, res_y, store_sem):
    rows, count = rho.shape
    row = lax.broadcasted_iota(jnp.int32, (rows, count), 0)
    col = lax.broadcasted_iota(jnp.int32, (rows, count), 1)
    here = fields[0]
    after = jnp.where(row == rows - 1, beyond_row[0:1], pltpu.roll(here, rows - 1, 0))
    res_x[...] = mx[...] - flux_weight * (after - here)
    save_x = pltpu.make_async_copy(res_x, out_x.at[0], store_sem.at[0])
    save_x.start()
    grad = jnp.where(col == count - 1, 0.0, pltpu.roll(here, count - 1, 1) - here)
    res_y[...] = my[...] - flux_weight * grad
    save_y = pltpu.make_async_copy(res_y, out_y.at[0], store_sem.at[1])
    save_y.start()
    res_d[...] = rho[...] - fields[1]
    save_d = pltpu.make_async_copy(res_d, out_d.at[0], store_sem.at[2])
    save_d.start()
    for save in (save_x, save_y, save_d):
        save.wait()


def per_device_kernel(density, flux_x, flux_y):
    rows, count = density.shape[1:]
    total = lax.axis_size("tm") // 2
    group = count // total
    tables = host_tables(count, total)
    f32, bf16 = jnp.float32, jnp.bfloat16
    vm = pltpu.VMEM
    dma = pltpu.SemaphoreType.DMA
    slab = vm((rows, count), f32)
    tall = total * (2 * group + 8 * CHUNKS)
    scratch = [
        vm((2, 3, rows // 2, count), f32), vm((2, count, count), bf16), vm((2, count, count), bf16), vm((group, count), f32),
        slab, vm((8, count), f32), vm((tall, rows), f32), vm((2 * tall, rows), f32),
        vm((total, group, count), f32), vm((total, group, count), f32), vm((total, group, count), f32),
        vm((2, CHUNKS, group // CHUNKS, count), f32),
        vm((2 * tall, rows), f32), vm((tall, rows), f32),
        pltpu.SemaphoreType.REGULAR((2,)), dma((5,)), dma((2,)), dma((1 + CHUNKS,)), dma((2 * CHUNKS,)), dma((2,)),
    ]
    anywhere = pl.BlockSpec(memory_space=pl.ANY)

    def kernel(*refs):
        step_kernel(total, *refs)

    local = pl.BlockSpec(memory_space=pltpu.VMEM)
    held = pl.pallas_call(
        kernel,
        out_shape=[slab, slab, slab, vm((2, rows, count), f32), vm((8, count), f32)],
        in_specs=[anywhere] * 6,
        out_specs=[local] * 5,
        scratch_shapes=scratch,
        compiler_params=pltpu.CompilerParams(collective_id=0, has_side_effects=True),
    )(density, flux_x, flux_y, *tables)
    return pl.pallas_call(
        finish_kernel,
        out_shape=[jax.ShapeDtypeStruct(density.shape, f32)] * 3,
        in_specs=[local] * 5,
        out_specs=[anywhere] * 3,
        scratch_shapes=[slab, slab, slab, dma((3,))],
    )(*[pltpu.with_memory_space_constraint(x, pltpu.VMEM) for x in held])


def per_device(density, flux_x, flux_y):
    slabs, rows, count = density.shape
    size = lax.axis_size("tm")
    fits = (
        slabs == 1 and lax.axis_size("space") == 2 and size >= 2 and size & (size - 1) == 0
        and count % (8 * size) == 0 and rows == 128 and 2 * rows == count
    )
    return (per_device_kernel if fits else per_device_xla)(density, flux_x, flux_y)


def solution(mesh):
    return jax.shard_map(
        per_device,
        mesh=mesh,
        in_specs=(P("tm", "space", None), P("tm", "space", None), P("tm", "space", None)),
        out_specs=(P("tm", "space", None), P("tm", "space", None), P("tm", "space", None)),
        check_vma=False,
    )
```

```python
import jax
import jax.numpy as jnp
import numpy as np
from jax import lax
from jax.experimental import pallas as pl
from jax.experimental.pallas import tpu as pltpu
from jax.sharding import PartitionSpec as P

NEWTON = 4


prox_weight = 1.0
regular_shift = 0.0001
space_weight = 0.25
flux_weight = 0.5
highest = lax.Precision.HIGHEST


def swapped(block, axis, distance):
    count = lax.axis_size(axis)
    route = []
    for low in range(count):
        high = low | 1 << distance
        if high != low and high < count:
            route += [(low, high), (high, low)]
    return lax.ppermute(block, axis, route)


def shifted(array, axis, by):
    size = lax.axis_size(axis)
    pairs = [(i, i + by) for i in range(size) if 0 <= i + by < size]
    return lax.ppermute(array, axis, pairs)


def kinetic_prox(density, flux_x, flux_y):
    square = flux_x * flux_x + flux_y * flux_y
    target = density + prox_weight + jnp.sqrt(square)
    for step in range(NEWTON):
        above = target + prox_weight
        value = (target - density) * above * above - 0.5 * prox_weight * square
        slope = above * (3.0 * target + prox_weight - 2.0 * density)
        target = target - value / slope
    shrink = target / (target + prox_weight)
    return (target, shrink * flux_x, shrink * flux_y)


def cosine_table(count):
    modes = jnp.arange(count).astype(jnp.float32)[:, None]
    points = jnp.arange(count).astype(jnp.float32)[None, :]
    table = jnp.cos(jnp.pi * modes * (2.0 * points + 1.0) / (2.0 * count))
    scales = jnp.where(modes == 0, jnp.sqrt(1.0 / count), jnp.sqrt(2.0 / count))
    return scales * table


def eigen_values(count):
    modes = jnp.arange(count).astype(jnp.float32)
    return 4.0 * jnp.sin(jnp.pi * modes / (2.0 * count)) ** 2


def move_outward(stacked, bit):
    return swapped(stacked, "tm", bit)


def move_homeward(stacked, bit):
    return swapped(stacked, "tm", bit)


def butterfly(blocks, mover):
    total = lax.axis_size("tm")
    position = lax.axis_index("tm")
    bit_count = total.bit_length() - 1
    for bit in range(bit_count):
        higher = total >> bit + 1
        lowest = 1 << bit
        shaped = blocks.reshape((higher, 2, lowest) + blocks.shape[1:])
        own_bit = position >> bit & 1
        keeping = jnp.where(own_bit == 0, shaped[:, 0], shaped[:, 1])
        leaving = jnp.where(own_bit == 0, shaped[:, 1], shaped[:, 0])
        arrived = mover(leaving, bit)
        first_half = jnp.where(own_bit == 0, keeping, arrived)
        second_half = jnp.where(own_bit == 0, arrived, keeping)
        blocks = jnp.stack([first_half, second_half], axis=1).reshape(blocks.shape)
    return blocks


def per_device_xla(density, flux_x, flux_y):
    slabs = density.shape[0]
    rows_local = density.shape[1]
    count = density.shape[2]
    parts = lax.axis_size("space")
    modes_local = count // parts
    own_start = lax.axis_index("space") * rows_local
    mode_start = lax.axis_index("space") * modes_local
    rho, mom_x, mom_y = kinetic_prox(density, flux_x, flux_y)
    prior = shifted(rho[slabs - 1], "tm", 1)
    before = jnp.concatenate([prior[None], rho[:-1]], axis=0)
    zeroed = mom_y.at[:, :, count - 1].set(0.0)
    div_second = zeroed - jnp.concatenate(
        [jnp.zeros_like(zeroed[:, :, :1]), zeroed[:, :, :-1]], axis=2
    )
    partial_source = rho - before + flux_weight * div_second
    table = cosine_table(count)
    diff_table = jnp.concatenate(
        [table[:, :-1] - table[:, 1:], jnp.zeros_like(table[:, :1])], axis=1
    )
    stacked = jnp.concatenate([partial_source, flux_weight * mom_x], axis=1)
    column_modes = jnp.einsum("tij,kj->itk", stacked, table, precision=highest)
    left = lax.dynamic_slice(
        table, (0, own_start), (modes_local * lax.axis_size("space"), rows_local)
    )
    left_diff = lax.dynamic_slice(
        diff_table, (0, own_start), (modes_local * lax.axis_size("space"), rows_local)
    )
    both = jnp.concatenate([left, left_diff], axis=1)
    modal = lax.psum_scatter(
        jnp.einsum("ki,itj->ktj", both, column_modes, precision=highest),
        "space",
        scatter_dimension=0,
        tiled=True,
    )
    lam = eigen_values(count)
    lam_local = lax.dynamic_slice_in_dim(lam, mode_start, modes_local)
    coeff = 2.0 + regular_shift + space_weight * (lam_local[:, None] + lam[None, :])
    devices_tm = lax.axis_size("tm")
    position = lax.axis_index("tm")
    lines_local = modes_local * count
    line_group = lines_local // devices_tm
    steps_all = devices_tm * slabs
    outgoing = jnp.transpose(modal, (0, 2, 1)).reshape(devices_tm, line_group, slabs)
    incoming = butterfly(outgoing, move_outward)
    series = jnp.transpose(incoming, (1, 0, 2)).reshape(line_group, steps_all)
    line_coeff = lax.dynamic_slice_in_dim(
        coeff.reshape(lines_local), position * line_group, line_group
    )
    column = lax.broadcasted_iota(jnp.int32, (line_group, steps_all), 1)
    below_band = jnp.where(column == 0, 0.0, -1.0).astype(jnp.float32)
    above_band = jnp.where(column == steps_all - 1, 0.0, -1.0).astype(jnp.float32)
    middle_band = jnp.broadcast_to(line_coeff[:, None], (line_group, steps_all))
    solution = lax.linalg.tridiagonal_solve(
        below_band, middle_band, above_band, series[:, :, None]
    )[:, :, 0]
    blocked = solution.reshape(line_group, devices_tm, slabs)
    leading_next = jnp.concatenate(
        [solution[:, slabs::slabs], jnp.zeros((line_group, 1), jnp.float32)], axis=1
    )
    padded = jnp.concatenate([blocked, leading_next[:, :, None]], axis=2)
    returned = butterfly(jnp.transpose(padded, (1, 0, 2)), move_homeward)
    local_lines = returned.reshape(modes_local, count, slabs + 1)
    extended = jnp.transpose(local_lines, (0, 2, 1))
    phihat = extended[:, :slabs, :]
    left = lax.dynamic_slice(
        table, (mode_start, 0), (modes_local, rows_local * lax.axis_size("space"))
    )
    left_diff = lax.dynamic_slice(
        diff_table, (mode_start, 0), (modes_local, rows_local * lax.axis_size("space"))
    )
    values = jnp.einsum("ki,ktj->itj", left, extended, precision=highest)
    slopes = -jnp.einsum("ki,ktj->itj", left_diff, phihat, precision=highest)
    gathered = lax.psum_scatter(
        jnp.concatenate([values, slopes], axis=1), "space", scatter_dimension=0, tiled=True
    )
    physical = jnp.einsum("itk,kj->tij", gathered, table, precision=highest)
    potential = physical[: slabs + 1]
    grad_first = physical[slabs + 1 :]
    present = potential[:slabs]
    grad_second = jnp.concatenate(
        [present[:, :, 1:] - present[:, :, :-1], jnp.zeros_like(present[:, :, :1])], axis=2
    )
    density_out = rho - (present - potential[1:])
    flux_x_out = mom_x - flux_weight * grad_first
    flux_y_out = mom_y - flux_weight * grad_second
    return (density_out, flux_x_out, flux_y_out)


MESH = pl.DeviceIdType.MESH
CHUNKS = 2


def split_table(table):
    high = table.astype(jnp.bfloat16)
    low = (table - high.astype(np.float32)).astype(jnp.bfloat16)
    return np.stack([high, low], axis=-3)


def host_tables(count, solvers):
    modes = np.arange(count, dtype=np.float64)[:, None]
    points = np.arange(count, dtype=np.float64)[None, :]
    table = np.cos(np.pi * modes * (2.0 * points + 1.0) / (2.0 * count))
    table = table * np.where(modes == 0, np.sqrt(1.0 / count), np.sqrt(2.0 / count))
    lam = 4.0 * np.sin(np.pi * np.arange(count) / (2.0 * count)) ** 2
    coeff = 2.0 + regular_shift + space_weight * (lam[:, None] + lam[None, :])
    f32 = np.float32
    return (
        split_table(table.astype(f32)),
        split_table(table.T.astype(f32)),
        coeff.reshape(solvers, count // solvers, count).astype(f32),
    )


def parted(x):
    high = x.astype(jnp.bfloat16)
    return high, (x - high.astype(jnp.float32)).astype(jnp.bfloat16)


def mul(a, b):
    return jnp.dot(a, b, preferred_element_type=jnp.float32)


def mul_nt(a, b):
    return lax.dot_general(a, b, (((1,), (1,)), ((), ())), preferred_element_type=jnp.float32)


def by_table(x, table):
    high, low = parted(x)
    return mul(high, table[0]) + (mul(high, table[1]) + mul(low, table[0]))


def table_by(table, x):
    high, low = parted(x)
    return mul(table[0], high) + (mul(table[1], high) + mul(table[0], low))


def table_by_t(table, x):
    high, low = parted(x)
    return mul_nt(table[0], high) + (mul_nt(table[1], high) + mul_nt(table[0], low))


def by_table_t(x, table):
    high, low = parted(x)
    return mul_nt(high, table[0]) + (mul_nt(high, table[1]) + mul_nt(low, table[0]))


def mul_tn(a, b):
    return lax.dot_general(a, b, (((0,), (0,)), ((), ())), preferred_element_type=jnp.float32)


def by_table_tn(x, table):
    high, low = parted(x)
    return mul_tn(high, table[0]) + (mul_tn(high, table[1]) + mul_tn(low, table[0]))


def step_kernel(
    total, density, flux_x, flux_y, cos, cos_t, coeff,
    rho, mx, my, fields, beyond_row,
    inputs, cos_v, cos_t_v, coeff_v,
    first_source, halo, outgoing, incoming, pivots, slope, steps, cut, back, home,
    ready, load_sem, halo_sem, out_sem, cut_sem, back_sem,
):
    place = lax.axis_index("tm")
    half = place // total
    me = place - half * total
    base = half * total
    final = 2 * total - 1
    mirror = {"tm": lax.rem(place + total, 2 * total)}
    side = lax.axis_index("space")
    own = 2 * me + side
    rows, count = rho.shape
    full = coeff_v.shape[0]
    group = full // CHUNKS
    stride_rows, filled = 2 * group + 8, 2 * group + 1
    per = rows // full
    chunks = range(CHUNKS)
    solving = side == 1
    pieces = inputs.shape[0]
    tile = rows // pieces
    feeds = [
        pltpu.make_async_copy(src.at[0, pl.ds(j * tile, tile)], inputs.at[j, i], load_sem.at[j])
        for j in range(pieces) for i, src in enumerate((density, flux_x, flux_y))
    ]
    loads = [
        pltpu.make_async_copy(src, dst, load_sem.at[i])
        for i, (src, dst) in enumerate([(cos, cos_v), (coeff.at[me], coeff_v), (cos_t, cos_t_v)], pieces)
    ]
    strips = [
        pltpu.make_async_copy(cos.at[i, pl.ds(j * rows, rows)], cos_v.at[i, pl.ds(j * rows, rows)], load_sem.at[pieces])
        for i in range(2) for j in range(2)
    ]
    for load in feeds + strips:
        load.start()

    def settle(ref, size, sem):
        span = ref.at[pl.ds(0, size)]
        pltpu.make_async_copy(span, span, sem).wait()

    bits = [1 << i for i in range(total.bit_length() - 1)]
    flips = [bit * (1 - 2 * lax.rem(me // bit, 2)) for bit in bits]
    masks = sorted(range(total), key=lambda m: (-bin(m).count("1"), -m))
    chips = [me + sum(f for f, bit in zip(flips, bits) if m & bit) for m in masks]
    others = [chip for chip, m in zip(chips, masks) if m]

    def device(chip, core):
        return {"tm": base + chip, "space": core}

    def choose(options):
        for test, action in options:
            pl.when(test)(action)

    barrier = pltpu.get_barrier_semaphore()

    @pl.when(solving)
    def _():
        for core in (1, 0):
            for chip in others:
                pl.semaphore_signal(barrier, inc=1, device_id=device(chip, core), device_id_type=MESH)
        pl.semaphore_signal(barrier, inc=1, device_id=device(me, 0), device_id_type=MESH)

        @pl.when(half == 0)
        def _():
            pl.semaphore_signal(barrier, inc=1, device_id=mirror, device_id_type=MESH)

    for j in range(pieces):
        settle(inputs.at[j], 3, load_sem.at[j])
        span = slice(j * tile, (j + 1) * tile)
        rho[span], mx[span], my[span] = kinetic_prox(inputs[j, 0], inputs[j, 1], inputs[j, 2])

    for load in loads[1:]:
        load.start()
    row = lax.broadcasted_iota(jnp.int32, (rows, count), 0)
    col = lax.broadcasted_iota(jnp.int32, (rows, count), 1)
    bottom = side * rows + row == 2 * rows - 1
    wx = jnp.where(bottom, 0.0, mx[...])
    wy = jnp.where(col == count - 1, 0.0, my[...])
    div = flux_weight * (
        wx - jnp.where(row == 0, 0.0, pltpu.roll(wx, 1, 0)) + wy - pltpu.roll(wy, 1, 1))
    whole = rho[...] + div
    closing = jnp.full((rows, count), place, jnp.int32) == final
    pair = jnp.concatenate(
        [jnp.where(closing, 0.0, rho[...]), jnp.where(closing, whole, div)], axis=0)
    loads[0].wait()
    spread = table_by_t(cos_v, pair)
    crossing = by_table_t(jnp.broadcast_to(-flux_weight * wx[rows - 1:], (8, count)), cos_v)
    for k in chunks:
        for block in range(total):
            span = slice(block * full + k * group, block * full + (k + 1) * group)
            first = (k * total + block) * stride_rows
            for f in range(2):
                outgoing[first + f * group:first + (f + 1) * group] = spread[span, f * rows:(f + 1) * rows]
            part = block // per * rows
            outgoing[first + 2 * group:first + filled] = crossing[:1, part:part + rows]
    pl.semaphore_wait(barrier, total + side * (half - 1))

    def place_of(block, first, size):
        return pl.ds(pl.multiple_of(block * stride_rows + first, 8), size)

    def outward(k, chip, first, size):
        return pltpu.make_async_remote_copy(
            src_ref=outgoing.at[place_of(k * total + chip, first, size)],
            dst_ref=incoming.at[place_of(2 * k * total + own, first, size)],
            send_sem=out_sem.at[0], recv_sem=out_sem.at[1 + k],
            device_id=device(chip, 1), device_id_type=MESH)

    def out_kinds(chip, core, action):
        ending = chip == final
        inner = jnp.logical_not(ending)
        choose([
            (inner & (core == 0), lambda: action(0, filled)),
            (inner & (core == 1), lambda: action(0, 2 * group)),
            (ending & (core == 0), lambda: action(group, group + 1)),
            (ending & (core == 1), lambda: action(group, group)),
        ])

    def send_out(first, size):
        for k in chunks:
            for chip in others:
                outward(k, chip, first, size).start()

            @pl.when(side == 0)
            def _():
                outward(k, me, first, size).start()

    out_kinds(place, side, send_out)

    @pl.when(side == 0)
    def _():
        for chip in chips:
            pl.semaphore_signal(ready.at[0], inc=1, device_id=device(chip, 1), device_id_type=MESH)

    @pl.when(solving & (half == 1))
    def _():
        pl.semaphore_signal(ready.at[1], inc=1, device_id=mirror, device_id_type=MESH)

    row_halo = pltpu.make_async_remote_copy(
        src_ref=mx.at[pl.ds(rows - 8, 8)], dst_ref=halo, send_sem=halo_sem.at[0],
        recv_sem=halo_sem.at[1], device_id={"space": 1 - side}, device_id_type=MESH)

    @pl.when((place == 0) & (side == 0))
    def _():
        row_halo.start()

    @pl.when(half == 1)
    def _():
        for block in [2 * (k + 1) * total - 1 - core for k in chunks for core in range(2)]:
            incoming[pl.ds(block * stride_rows, group)] = jnp.zeros((group, rows), jnp.float32)

    small = (place == 0) | (place == final)

    @pl.when(small)
    def _():
        for block in range(CHUNKS * total):
            home[pl.ds(block * stride_rows, group)] = jnp.zeros((group, rows), jnp.float32)

    loads[1].wait()
    loads[2].wait()
    def swap(k):
        return pltpu.make_async_remote_copy(
            src_ref=cut.at[0, k], dst_ref=cut.at[1, k], send_sem=cut_sem.at[CHUNKS],
            recv_sem=cut_sem.at[k], device_id=mirror, device_id_type=MESH)

    def homeward(k, chip, core, first, size):
        return pltpu.make_async_remote_copy(
            src_ref=back.at[place_of((2 * k + core) * total + chip, first, size)],
            dst_ref=home.at[place_of(k * total + me, first, size)],
            send_sem=back_sem.at[0], recv_sem=back_sem.at[1],
            device_id=device(chip, core), device_id_type=MESH)

    def back_kinds(chip, core, action):
        ending = (chip == 0) | (chip == final)
        inner = jnp.logical_not(ending)
        choose([
            (ending, lambda: action(group, group + 1)),
            (inner & (core == 0), lambda: action(0, filled)),
            (inner & (core == 1), lambda: action(0, 2 * group)),
        ])

    @pl.when(place == 0)
    def _():
        pl.when(side == 0)(row_halo.wait_send)
        pl.when(solving)(row_halo.wait_recv)
        prior = jnp.where(jnp.full((1, count), side, jnp.int32) == 1, halo[7:], 0.0)
        first_source[...] = whole - jnp.where(row == 0, flux_weight * prior, 0.0)

    def solve():
        for k in chunks:
            incoming[place_of(2 * k * total + own, 0, stride_rows)] = outgoing[place_of(k * total + me, 0, stride_rows)]
        c = coeff_v[...]
        pivot = 1.0 / c
        pivots[0] = pivot
        for t in range(1, total):
            pivot = 1.0 / (c - pivot)
            pivots[t] = pivot
        inverse = 1.0 / (1.0 - pivot * pivot)
        start, stride = half * (total - 1), 1 - 2 * half
        gain = jnp.ones((full, count), jnp.float32)
        slope[start + stride * (total - 1)] = gain
        for i in reversed(range(total - 1)):
            gain = gain * pivots[i]
            slope[start + stride * i] = gain
        right = jnp.full((group, count), half, jnp.int32) == 1
        lanes = lax.broadcasted_iota(jnp.int32, (group, rows), 1)
        modes_at = lax.broadcasted_iota(jnp.int32, (group, rows), 0)
        everything = total * (filled + 2 * group)
        ends = []
        for k in chunks:
            span = slice(k * group, (k + 1) * group)
            pl.when(half == 0)(lambda: out_kinds(
                place, side, lambda first, size: settle(incoming, everything - size, out_sem.at[1 + k])))
            pl.when(half == 1)(lambda: out_kinds(
                place, side, lambda first, size: settle(incoming, everything - 2 * group - size, out_sem.at[1 + k])))
            zero = 2 * k * total

            def slices(t, f):
                firsts = [(zero + 2 * t + core) * stride_rows + f * group for core in range(2)]
                return [incoming[first:first + group] for first in firsts]

            shares = incoming[pl.ds(zero * stride_rows + 2 * group, total, stride=2 * stride_rows)]
            picked = lanes == lax.rem(me, per) * full + k * group + modes_at

            def beyond_halo(t):
                mine = jnp.where(picked, jnp.broadcast_to(shares[t:t + 1], (group, rows)), 0.0)
                return jnp.where(lanes == 0, jnp.sum(mine, axis=1, keepdims=True), 0.0)

            source = []
            for t in range(total):
                low, high = slices(t, 1)
                high = high + beyond_halo(t)
                now = slices(t, 0)
                if t > 0:
                    now = [x - y for x, y in zip(now, slices(t - 1, 0))]
                source.append(jnp.concatenate([low + now[0], high + now[1]], axis=1))
            source.append(jnp.concatenate(slices(total - 1, 0), axis=1))
            modal = by_table(jnp.concatenate(source, axis=0), cos_t_v)
            reach = sum(modal[t * group:(t + 1) * group] * slope[t, span] for t in range(total))
            last_rho = jnp.where(right, 0.0, modal[total * group:])
            cut[0, k] = pivots[total - 1, span] * reach - last_rho
            if k == 0:
                pl.when(half == 0)(lambda: pl.semaphore_wait(ready.at[1], 1))
            swap(k).start()
            steps[:, span] = modal[:total * group].reshape(total, group, count)
            ends.append(last_rho)

        value = jnp.zeros((full, count), jnp.float32)
        for i in range(total):
            value = (steps[start + stride * i] + value) * pivots[i]
            steps[start + stride * i] = value
        reached = value
        rest = jnp.zeros((full, count), jnp.float32)
        steps[start + stride * (total - 1)] = rest
        for i in reversed(range(total - 1)):
            rest = steps[start + stride * i] + pivots[i] * rest
            steps[start + stride * i] = rest

        out_kinds(place, side, lambda first, size: settle(outgoing, CHUNKS * (total - 1) * size, out_sem.at[0]))
        near_edge = cos_t_v[:, rows - 8:rows + 8]
        pl.semaphore_wait(ready.at[0], total)

        def put(k, t, block, brink):
            for core in range(2):
                piece = block[:, core * rows:(core + 1) * rows]
                zero = (2 * k + core) * total
                if t < total:
                    first = (zero + t) * stride_rows
                    back[first + group:first + 2 * group] = piece
                    back[first + 2 * group:first + filled] = brink[8 - core:9 - core]
                if t > 0:
                    first = (zero + t - 1) * stride_rows
                    back[first:first + group] = piece

        def send_back(k, chip, core):
            back_kinds(base + chip, core, lambda first, size: homeward(k, chip, core, first, size).start())

        for k in chunks:
            span = slice(k * group, (k + 1) * group)
            swap(k).wait_recv()
            value, last_rho = reached[span], ends[k]
            pivot = pivots[total - 1, span]
            beyond = cut[1, k] - pivot * last_rho
            value = (value + pivot * beyond) * inverse[span]
            leading = steps[0, span] + slope[0, span] * value
            put(k, 0, by_table(leading, cos_v),
                table_by_t(near_edge, jnp.concatenate([leading] * total, axis=0)))

            @pl.when(half == 0)
            def _():
                homeward(k, 0, 0, group, group + 1).start()

                @pl.when(me != 0)
                def _():
                    homeward(k, 0, 1, group, group + 1).start()

            lines = [leading] + [steps[t, span] + slope[t, span] * value for t in range(1, total)]
            lines.append(jnp.where(right, 0.0, beyond + pivot * value))
            brink = table_by_t(near_edge, jnp.concatenate(lines[:total], axis=0))
            halfback = by_table(jnp.concatenate(lines[1:], axis=0), cos_v)
            for t in range(1, total + 1):
                put(k, t, halfback[(t - 1) * group:t * group], brink)
            for chip in others:
                @pl.when(base + chip != 0)
                def _():
                    send_back(k, chip, 0)
                    send_back(k, chip, 1)

            @pl.when(place != 0)
            def _():
                send_back(k, me, 0)

            mine = (2 * k + 1) * total + me
            home[place_of(k * total + me, group, group + 8)] = back[place_of(mine, group, group + 8)]

            @pl.when(jnp.logical_not(small))
            def _():
                home[place_of(k * total + me, 0, group)] = back[place_of(mine, 0, group)]

    pl.when(solving)(solve)
    returned = 2 * (group + 1) + (total - 1) * (filled + 2 * group)
    pl.when(side == 0)(lambda: back_kinds(
        place, side, lambda first, size: settle(home, CHUNKS * total * size, back_sem.at[1])))
    pl.when(solving)(lambda: back_kinds(
        place, side, lambda first, size: settle(home, CHUNKS * (total - 1) * size, back_sem.at[1])))

    def modes(first):
        spans = [(k * total + block) * stride_rows + first for block in range(total) for k in chunks]
        return jnp.concatenate([home[at:at + group] for at in spans], axis=0)

    here = modes(group)
    offset = lax.rem(total - me, total) * group
    row_at = lax.broadcasted_iota(jnp.int32, (per, rows), 0)
    lane_at = lax.broadcasted_iota(jnp.int32, (per, rows), 1)

    def find_edge():
        strip = []
        for part in range(count // rows):
            placed = jnp.zeros((per, rows), jnp.float32)
            for k in chunks:
                tail = home[pl.ds((k * total + part * per) * stride_rows + 2 * group, per, stride=stride_rows)]
                tail = jnp.where(lane_at < group, pltpu.roll(tail, offset, 1), 0.0)
                for d in range(per):
                    shift = d * full + k * group
                    placed = placed + jnp.where(row_at == d, pltpu.roll(tail, shift, 1) if shift else tail, 0.0)
            strip.append(jnp.broadcast_to(jnp.sum(placed, axis=0, keepdims=True), (8, rows)))
        return by_table(jnp.concatenate(strip, axis=1), cos_v)[:1]

    upper = jnp.full((1, count), side, jnp.int32) == 0

    @pl.when(place != 0)
    def _():
        values = by_table_tn(jnp.concatenate([here, here - modes(0)], axis=1), cos_v)
        edge = find_edge()
        pot = values[:rows]
        fields[0] = pot
        fields[1] = values[rows:]
        beyond_row[...] = jnp.broadcast_to(jnp.where(upper, edge, pot[rows - 1:]), beyond_row.shape)

    @pl.when(place == 0)
    def _():
        edge = find_edge()
        pot = by_table_tn(here, cos_v)
        fields[0] = pot
        before_first = jnp.where(upper, pot[:1], edge)
        after_last = jnp.where(upper, edge, pot[rows - 1:])
        beyond_row[...] = jnp.broadcast_to(after_last, beyond_row.shape)
        left_of = jnp.where(col == 0, pot, pltpu.roll(pot, 1, 1))
        right_of = jnp.where(col == count - 1, pot, pltpu.roll(pot, count - 1, 1))
        over = jnp.where(row == 0, before_first, pltpu.roll(pot, 1, 0))
        under = jnp.where(row == rows - 1, after_last, pltpu.roll(pot, rows - 1, 0))
        bend = (pot - left_of) + (pot - right_of) + (pot - over) + (pot - under)
        following = (2.0 + regular_shift) * pot + space_weight * bend - first_source[...]
        fields[1] = pot - following

    pl.when(solving)(lambda: settle(cut.at[0], CHUNKS, cut_sem.at[CHUNKS]))
    pl.when(solving)(lambda: back_kinds(
        place, side, lambda first, size: settle(back, CHUNKS * (returned - size), back_sem.at[0])))
    pl.when(side == 0)(lambda: out_kinds(
        place, side, lambda first, size: settle(outgoing, CHUNKS * total * size, out_sem.at[0])))


def finish_kernel(rho, mx, my, fields, beyond_row, out_d, out_x, out_y, results, store_sem):
    rows, count = rho.shape
    row = lax.broadcasted_iota(jnp.int32, (rows, count), 0)
    col = lax.broadcasted_iota(jnp.int32, (rows, count), 1)
    saves = [
        pltpu.make_async_copy(results.at[i], out.at[0], store_sem.at[0])
        for i, out in enumerate((out_d, out_x, out_y))
    ]
    results[0] = rho[...] - fields[1]
    saves[0].start()
    here = fields[0]
    after = jnp.where(row == rows - 1, beyond_row[0:1], pltpu.roll(here, rows - 1, 0))
    results[1] = mx[...] - flux_weight * (after - here)
    saves[1].start()
    grad = jnp.where(col == count - 1, 0.0, pltpu.roll(here, count - 1, 1) - here)
    results[2] = my[...] - flux_weight * grad
    saves[2].start()
    pltpu.make_async_copy(results, results, store_sem.at[0]).wait()


def per_device_kernel(density, flux_x, flux_y):
    rows, count = density.shape[1:]
    total = lax.axis_size("tm") // 2
    group = count // total
    tables = host_tables(count, total)
    f32, bf16 = jnp.float32, jnp.bfloat16
    vm = pltpu.VMEM
    dma = pltpu.SemaphoreType.DMA
    slab = vm((rows, count), f32)
    tall = total * (2 * group + 8 * CHUNKS)
    scratch = [
        vm((1, 3, rows, count), f32), vm((2, count, count), bf16), vm((2, count, count), bf16), vm((group, count), f32),
        slab, vm((8, count), f32), vm((tall, rows), f32), vm((2 * tall, rows), f32),
        vm((total, group, count), f32), vm((total, group, count), f32), vm((total, group, count), f32),
        vm((2, CHUNKS, group // CHUNKS, count), f32),
        vm((2 * tall, rows), f32), vm((tall, rows), f32),
        pltpu.SemaphoreType.REGULAR((2,)), dma((4,)), dma((2,)), dma((1 + CHUNKS,)), dma((1 + CHUNKS,)), dma((2,)),
    ]
    anywhere = pl.BlockSpec(memory_space=pl.ANY)

    def kernel(*refs):
        step_kernel(total, *refs)

    local = pl.BlockSpec(memory_space=pltpu.VMEM)
    held = pl.pallas_call(
        kernel,
        out_shape=[slab, slab, slab, vm((2, rows, count), f32), vm((8, count), f32)],
        in_specs=[anywhere] * 6,
        out_specs=[local] * 5,
        scratch_shapes=scratch,
        compiler_params=pltpu.CompilerParams(collective_id=0, has_side_effects=True),
    )(density, flux_x, flux_y, *tables)
    return pl.pallas_call(
        finish_kernel,
        out_shape=[jax.ShapeDtypeStruct(density.shape, f32)] * 3,
        in_specs=[local] * 5,
        out_specs=[anywhere] * 3,
        scratch_shapes=[vm((3, rows, count), f32), dma((1,))],
    )(*[pltpu.with_memory_space_constraint(x, pltpu.VMEM) for x in held])


def per_device(density, flux_x, flux_y):
    slabs, rows, count = density.shape
    size = lax.axis_size("tm")
    fits = (
        slabs == 1 and lax.axis_size("space") == 2 and size >= 2 and size & (size - 1) == 0
        and count % (8 * size) == 0 and rows == 128 and 2 * rows == count
    )
    return (per_device_kernel if fits else per_device_xla)(density, flux_x, flux_y)


def solution(mesh):
    return jax.shard_map(
        per_device,
        mesh=mesh,
        in_specs=(P("tm", "space", None), P("tm", "space", None), P("tm", "space", None)),
        out_specs=(P("tm", "space", None), P("tm", "space", None), P("tm", "space", None)),
        check_vma=False,
    )
```

```python
import jax
import jax.numpy as jnp
import numpy as np
from jax import lax
from jax.experimental import pallas as pl
from jax.experimental.pallas import tpu as pltpu
from jax.sharding import PartitionSpec as P

NEWTON = 4


prox_weight = 1.0
regular_shift = 0.0001
space_weight = 0.25
flux_weight = 0.5
highest = lax.Precision.HIGHEST


def swapped(block, axis, distance):
    count = lax.axis_size(axis)
    route = []
    for low in range(count):
        high = low | 1 << distance
        if high != low and high < count:
            route += [(low, high), (high, low)]
    return lax.ppermute(block, axis, route)


def shifted(array, axis, by):
    size = lax.axis_size(axis)
    pairs = [(i, i + by) for i in range(size) if 0 <= i + by < size]
    return lax.ppermute(array, axis, pairs)


def kinetic_prox(density, flux_x, flux_y):
    square = flux_x * flux_x + flux_y * flux_y
    target = density + prox_weight + jnp.sqrt(square)
    for step in range(NEWTON):
        above = target + prox_weight
        value = (target - density) * above * above - 0.5 * prox_weight * square
        slope = above * (3.0 * target + prox_weight - 2.0 * density)
        target = target - value / slope
    shrink = target / (target + prox_weight)
    return (target, shrink * flux_x, shrink * flux_y)


def cosine_table(count):
    modes = jnp.arange(count).astype(jnp.float32)[:, None]
    points = jnp.arange(count).astype(jnp.float32)[None, :]
    table = jnp.cos(jnp.pi * modes * (2.0 * points + 1.0) / (2.0 * count))
    scales = jnp.where(modes == 0, jnp.sqrt(1.0 / count), jnp.sqrt(2.0 / count))
    return scales * table


def eigen_values(count):
    modes = jnp.arange(count).astype(jnp.float32)
    return 4.0 * jnp.sin(jnp.pi * modes / (2.0 * count)) ** 2


def move_outward(stacked, bit):
    return swapped(stacked, "tm", bit)


def move_homeward(stacked, bit):
    return swapped(stacked, "tm", bit)


def butterfly(blocks, mover):
    total = lax.axis_size("tm")
    position = lax.axis_index("tm")
    bit_count = total.bit_length() - 1
    for bit in range(bit_count):
        higher = total >> bit + 1
        lowest = 1 << bit
        shaped = blocks.reshape((higher, 2, lowest) + blocks.shape[1:])
        own_bit = position >> bit & 1
        keeping = jnp.where(own_bit == 0, shaped[:, 0], shaped[:, 1])
        leaving = jnp.where(own_bit == 0, shaped[:, 1], shaped[:, 0])
        arrived = mover(leaving, bit)
        first_half = jnp.where(own_bit == 0, keeping, arrived)
        second_half = jnp.where(own_bit == 0, arrived, keeping)
        blocks = jnp.stack([first_half, second_half], axis=1).reshape(blocks.shape)
    return blocks


def per_device_xla(density, flux_x, flux_y):
    slabs = density.shape[0]
    rows_local = density.shape[1]
    count = density.shape[2]
    parts = lax.axis_size("space")
    modes_local = count // parts
    own_start = lax.axis_index("space") * rows_local
    mode_start = lax.axis_index("space") * modes_local
    rho, mom_x, mom_y = kinetic_prox(density, flux_x, flux_y)
    prior = shifted(rho[slabs - 1], "tm", 1)
    before = jnp.concatenate([prior[None], rho[:-1]], axis=0)
    zeroed = mom_y.at[:, :, count - 1].set(0.0)
    div_second = zeroed - jnp.concatenate(
        [jnp.zeros_like(zeroed[:, :, :1]), zeroed[:, :, :-1]], axis=2
    )
    partial_source = rho - before + flux_weight * div_second
    table = cosine_table(count)
    diff_table = jnp.concatenate(
        [table[:, :-1] - table[:, 1:], jnp.zeros_like(table[:, :1])], axis=1
    )
    stacked = jnp.concatenate([partial_source, flux_weight * mom_x], axis=1)
    column_modes = jnp.einsum("tij,kj->itk", stacked, table, precision=highest)
    left = lax.dynamic_slice(
        table, (0, own_start), (modes_local * lax.axis_size("space"), rows_local)
    )
    left_diff = lax.dynamic_slice(
        diff_table, (0, own_start), (modes_local * lax.axis_size("space"), rows_local)
    )
    both = jnp.concatenate([left, left_diff], axis=1)
    modal = lax.psum_scatter(
        jnp.einsum("ki,itj->ktj", both, column_modes, precision=highest),
        "space",
        scatter_dimension=0,
        tiled=True,
    )
    lam = eigen_values(count)
    lam_local = lax.dynamic_slice_in_dim(lam, mode_start, modes_local)
    coeff = 2.0 + regular_shift + space_weight * (lam_local[:, None] + lam[None, :])
    devices_tm = lax.axis_size("tm")
    position = lax.axis_index("tm")
    lines_local = modes_local * count
    line_group = lines_local // devices_tm
    steps_all = devices_tm * slabs
    outgoing = jnp.transpose(modal, (0, 2, 1)).reshape(devices_tm, line_group, slabs)
    incoming = butterfly(outgoing, move_outward)
    series = jnp.transpose(incoming, (1, 0, 2)).reshape(line_group, steps_all)
    line_coeff = lax.dynamic_slice_in_dim(
        coeff.reshape(lines_local), position * line_group, line_group
    )
    column = lax.broadcasted_iota(jnp.int32, (line_group, steps_all), 1)
    below_band = jnp.where(column == 0, 0.0, -1.0).astype(jnp.float32)
    above_band = jnp.where(column == steps_all - 1, 0.0, -1.0).astype(jnp.float32)
    middle_band = jnp.broadcast_to(line_coeff[:, None], (line_group, steps_all))
    solution = lax.linalg.tridiagonal_solve(
        below_band, middle_band, above_band, series[:, :, None]
    )[:, :, 0]
    blocked = solution.reshape(line_group, devices_tm, slabs)
    leading_next = jnp.concatenate(
        [solution[:, slabs::slabs], jnp.zeros((line_group, 1), jnp.float32)], axis=1
    )
    padded = jnp.concatenate([blocked, leading_next[:, :, None]], axis=2)
    returned = butterfly(jnp.transpose(padded, (1, 0, 2)), move_homeward)
    local_lines = returned.reshape(modes_local, count, slabs + 1)
    extended = jnp.transpose(local_lines, (0, 2, 1))
    phihat = extended[:, :slabs, :]
    left = lax.dynamic_slice(
        table, (mode_start, 0), (modes_local, rows_local * lax.axis_size("space"))
    )
    left_diff = lax.dynamic_slice(
        diff_table, (mode_start, 0), (modes_local, rows_local * lax.axis_size("space"))
    )
    values = jnp.einsum("ki,ktj->itj", left, extended, precision=highest)
    slopes = -jnp.einsum("ki,ktj->itj", left_diff, phihat, precision=highest)
    gathered = lax.psum_scatter(
        jnp.concatenate([values, slopes], axis=1), "space", scatter_dimension=0, tiled=True
    )
    physical = jnp.einsum("itk,kj->tij", gathered, table, precision=highest)
    potential = physical[: slabs + 1]
    grad_first = physical[slabs + 1 :]
    present = potential[:slabs]
    grad_second = jnp.concatenate(
        [present[:, :, 1:] - present[:, :, :-1], jnp.zeros_like(present[:, :, :1])], axis=2
    )
    density_out = rho - (present - potential[1:])
    flux_x_out = mom_x - flux_weight * grad_first
    flux_y_out = mom_y - flux_weight * grad_second
    return (density_out, flux_x_out, flux_y_out)


MESH = pl.DeviceIdType.MESH
CHUNKS = 2


def split_table(table):
    high = table.astype(jnp.bfloat16)
    low = (table - high.astype(np.float32)).astype(jnp.bfloat16)
    return np.stack([high, low], axis=-3)


def host_tables(count, solvers):
    modes = np.arange(count, dtype=np.float64)[:, None]
    points = np.arange(count, dtype=np.float64)[None, :]
    table = np.cos(np.pi * modes * (2.0 * points + 1.0) / (2.0 * count))
    table = table * np.where(modes == 0, np.sqrt(1.0 / count), np.sqrt(2.0 / count))
    lam = 4.0 * np.sin(np.pi * np.arange(count) / (2.0 * count)) ** 2
    coeff = 2.0 + regular_shift + space_weight * (lam[:, None] + lam[None, :])
    f32 = np.float32
    return (
        split_table(table.astype(f32)),
        split_table(table.T.astype(f32)),
        coeff.reshape(solvers, count // solvers, count).astype(f32),
    )


def parted(x):
    high = x.astype(jnp.bfloat16)
    return high, (x - high.astype(jnp.float32)).astype(jnp.bfloat16)


def mul(a, b):
    return jnp.dot(a, b, preferred_element_type=jnp.float32)


def mul_nt(a, b):
    return lax.dot_general(a, b, (((1,), (1,)), ((), ())), preferred_element_type=jnp.float32)


def by_table(x, table):
    high, low = parted(x)
    return mul(high, table[0]) + (mul(high, table[1]) + mul(low, table[0]))


def table_by(table, x):
    high, low = parted(x)
    return mul(table[0], high) + (mul(table[1], high) + mul(table[0], low))


def table_by_t(table, x):
    high, low = parted(x)
    return mul_nt(table[0], high) + (mul_nt(table[1], high) + mul_nt(table[0], low))


def by_table_t(x, table):
    high, low = parted(x)
    return mul_nt(high, table[0]) + (mul_nt(high, table[1]) + mul_nt(low, table[0]))


def mul_tn(a, b):
    return lax.dot_general(a, b, (((0,), (0,)), ((), ())), preferred_element_type=jnp.float32)


def by_table_tn(x, table):
    high, low = parted(x)
    return mul_tn(high, table[0]) + (mul_tn(high, table[1]) + mul_tn(low, table[0]))


def step_kernel(
    total, density, flux_x, flux_y, cos, cos_t, coeff,
    rho, mx, my, fields, beyond_row,
    inputs, cos_v, cos_t_v, coeff_v,
    first_source, halo, outgoing, incoming, pivots, slope, steps, cut, back, home,
    ready, load_sem, halo_sem, out_sem, cut_sem, back_sem,
):
    place = lax.axis_index("tm")
    half = place // total
    me = place - half * total
    base = half * total
    final = 2 * total - 1
    mirror = {"tm": lax.rem(place + total, 2 * total)}
    side = lax.axis_index("space")
    own = 2 * me + side
    rows, count = rho.shape
    full = coeff_v.shape[0]
    group = full // CHUNKS
    stride_rows, filled = 2 * group + 8, 2 * group + 1
    per = rows // full
    chunks = range(CHUNKS)
    solving = side == 1
    pieces = inputs.shape[0]
    tile = rows // pieces
    feeds = [
        pltpu.make_async_copy(src.at[0, pl.ds(j * tile, tile)], inputs.at[j, i], load_sem.at[j])
        for j in range(pieces) for i, src in enumerate((density, flux_x, flux_y))
    ]
    loads = [
        pltpu.make_async_copy(src, dst, load_sem.at[i])
        for i, (src, dst) in enumerate([(cos, cos_v), (coeff.at[me], coeff_v), (cos_t, cos_t_v)], pieces)
    ]
    strips = [
        pltpu.make_async_copy(cos.at[i, pl.ds(j * rows, rows)], cos_v.at[i, pl.ds(j * rows, rows)], load_sem.at[pieces])
        for i in range(2) for j in range(2)
    ]
    for load in feeds + strips:
        load.start()

    def settle(ref, size, sem):
        span = ref.at[pl.ds(0, size)]
        pltpu.make_async_copy(span, span, sem).wait()

    bits = [1 << i for i in range(total.bit_length() - 1)]
    flips = [bit * (1 - 2 * lax.rem(me // bit, 2)) for bit in bits]
    masks = sorted(range(total), key=lambda m: (-bin(m).count("1"), -m))
    chips = [me + sum(f for f, bit in zip(flips, bits) if m & bit) for m in masks]
    others = [chip for chip, m in zip(chips, masks) if m]

    def device(chip, core):
        return {"tm": base + chip, "space": core}

    def choose(options):
        for test, action in options:
            pl.when(test)(action)

    barrier = pltpu.get_barrier_semaphore()

    @pl.when(solving)
    def _():
        for core in (1, 0):
            for chip in others:
                pl.semaphore_signal(barrier, inc=1, device_id=device(chip, core), device_id_type=MESH)
        pl.semaphore_signal(barrier, inc=1, device_id=device(me, 0), device_id_type=MESH)

        @pl.when(half == 0)
        def _():
            pl.semaphore_signal(barrier, inc=1, device_id=mirror, device_id_type=MESH)

    for j in range(pieces):
        settle(inputs.at[j], 3, load_sem.at[j])
        span = slice(j * tile, (j + 1) * tile)
        rho[span], mx[span], my[span] = kinetic_prox(inputs[j, 0], inputs[j, 1], inputs[j, 2])

    for load in loads[1:]:
        load.start()
    row = lax.broadcasted_iota(jnp.int32, (rows, count), 0)
    col = lax.broadcasted_iota(jnp.int32, (rows, count), 1)
    bottom = side * rows + row == 2 * rows - 1
    wx = jnp.where(bottom, 0.0, mx[...])
    wy = jnp.where(col == count - 1, 0.0, my[...])
    div = flux_weight * (
        wx - jnp.where(row == 0, 0.0, pltpu.roll(wx, 1, 0)) + wy - pltpu.roll(wy, 1, 1))
    whole = rho[...] + div
    closing = jnp.full((rows, count), place, jnp.int32) == final
    pair = jnp.concatenate(
        [jnp.where(closing, 0.0, rho[...]), jnp.where(closing, whole, div)], axis=0)
    loads[0].wait()
    spread = table_by_t(cos_v, pair)
    crossing = by_table_t(jnp.broadcast_to(-flux_weight * wx[rows - 1:], (8, count)), cos_v)
    for k in chunks:
        for block in range(total):
            span = slice(block * full + k * group, block * full + (k + 1) * group)
            first = (k * total + block) * stride_rows
            for f in range(2):
                outgoing[first + f * group:first + (f + 1) * group] = spread[span, f * rows:(f + 1) * rows]
            part = block // per * rows
            outgoing[first + 2 * group:first + filled] = crossing[:1, part:part + rows]
    pl.semaphore_wait(barrier, total + side * (half - 1))

    def place_of(block, first, size):
        return pl.ds(pl.multiple_of(block * stride_rows + first, 8), size)

    def outward(k, chip, first, size):
        return pltpu.make_async_remote_copy(
            src_ref=outgoing.at[place_of(k * total + chip, first, size)],
            dst_ref=incoming.at[place_of(2 * k * total + own, first, size)],
            send_sem=out_sem.at[0], recv_sem=out_sem.at[1 + k],
            device_id=device(chip, 1), device_id_type=MESH)

    def out_kinds(chip, core, action):
        ending = chip == final
        inner = jnp.logical_not(ending)
        choose([
            (inner & (core == 0), lambda: action(0, filled)),
            (inner & (core == 1), lambda: action(0, 2 * group)),
            (ending & (core == 0), lambda: action(group, group + 1)),
            (ending & (core == 1), lambda: action(group, group)),
        ])

    def send_out(first, size):
        for k in chunks:
            for chip in others:
                outward(k, chip, first, size).start()

            @pl.when(side == 0)
            def _():
                outward(k, me, first, size).start()

    out_kinds(place, side, send_out)

    @pl.when(side == 0)
    def _():
        for chip in chips:
            pl.semaphore_signal(ready.at[0], inc=1, device_id=device(chip, 1), device_id_type=MESH)

    @pl.when(solving & (half == 1))
    def _():
        pl.semaphore_signal(ready.at[1], inc=1, device_id=mirror, device_id_type=MESH)

    row_halo = pltpu.make_async_remote_copy(
        src_ref=mx.at[pl.ds(rows - 8, 8)], dst_ref=halo, send_sem=halo_sem.at[0],
        recv_sem=halo_sem.at[1], device_id={"space": 1 - side}, device_id_type=MESH)

    @pl.when((place == 0) & (side == 0))
    def _():
        row_halo.start()

    @pl.when(half == 1)
    def _():
        for block in [2 * (k + 1) * total - 1 - core for k in chunks for core in range(2)]:
            incoming[pl.ds(block * stride_rows, group)] = jnp.zeros((group, rows), jnp.float32)

    small = (place == 0) | (place == final)

    @pl.when(small)
    def _():
        for block in range(CHUNKS * total):
            home[pl.ds(block * stride_rows, group)] = jnp.zeros((group, rows), jnp.float32)

    loads[1].wait()
    loads[2].wait()
    def swap(k):
        return pltpu.make_async_remote_copy(
            src_ref=cut.at[0, k], dst_ref=cut.at[1, k], send_sem=cut_sem.at[CHUNKS],
            recv_sem=cut_sem.at[k], device_id=mirror, device_id_type=MESH)

    def homeward(k, chip, core, first, size):
        return pltpu.make_async_remote_copy(
            src_ref=back.at[place_of((2 * k + core) * total + chip, first, size)],
            dst_ref=home.at[place_of(k * total + me, first, size)],
            send_sem=back_sem.at[0], recv_sem=back_sem.at[1],
            device_id=device(chip, core), device_id_type=MESH)

    def back_kinds(chip, core, action):
        ending = (chip == 0) | (chip == final)
        inner = jnp.logical_not(ending)
        choose([
            (ending, lambda: action(group, group + 1)),
            (inner & (core == 0), lambda: action(0, filled)),
            (inner & (core == 1), lambda: action(0, 2 * group)),
        ])

    @pl.when(place == 0)
    def _():
        pl.when(side == 0)(row_halo.wait_send)
        pl.when(solving)(row_halo.wait_recv)
        prior = jnp.where(jnp.full((1, count), side, jnp.int32) == 1, halo[7:], 0.0)
        first_source[...] = whole - jnp.where(row == 0, flux_weight * prior, 0.0)

    def solve():
        for k in chunks:
            incoming[place_of(2 * k * total + own, 0, stride_rows)] = outgoing[place_of(k * total + me, 0, stride_rows)]
        c = coeff_v[...]
        pivot = 1.0 / c
        pivots[0] = pivot
        for t in range(1, total):
            pivot = 1.0 / (c - pivot)
            pivots[t] = pivot
        inverse = 1.0 / (1.0 - pivot * pivot)
        start, stride = half * (total - 1), 1 - 2 * half
        gain = jnp.ones((full, count), jnp.float32)
        slope[start + stride * (total - 1)] = gain
        for i in reversed(range(total - 1)):
            gain = gain * pivots[i]
            slope[start + stride * i] = gain
        right = jnp.full((group, count), half, jnp.int32) == 1
        lanes = lax.broadcasted_iota(jnp.int32, (group, rows), 1)
        modes_at = lax.broadcasted_iota(jnp.int32, (group, rows), 0)
        everything = total * (filled + 2 * group)
        ends = []
        for k in chunks:
            span = slice(k * group, (k + 1) * group)
            pl.when(half == 0)(lambda: out_kinds(
                place, side, lambda first, size: settle(incoming, everything - size, out_sem.at[1 + k])))
            pl.when(half == 1)(lambda: out_kinds(
                place, side, lambda first, size: settle(incoming, everything - 2 * group - size, out_sem.at[1 + k])))
            zero = 2 * k * total

            def slices(t, f):
                firsts = [(zero + 2 * t + core) * stride_rows + f * group for core in range(2)]
                return [incoming[first:first + group] for first in firsts]

            shares = incoming[pl.ds(zero * stride_rows + 2 * group, total, stride=2 * stride_rows)]
            picked = lanes == lax.rem(me, per) * full + k * group + modes_at

            def beyond_halo(t):
                mine = jnp.where(picked, jnp.broadcast_to(shares[t:t + 1], (group, rows)), 0.0)
                return jnp.where(lanes == 0, jnp.sum(mine, axis=1, keepdims=True), 0.0)

            source = []
            for t in range(total):
                low, high = slices(t, 1)
                high = high + beyond_halo(t)
                now = slices(t, 0)
                if t > 0:
                    now = [x - y for x, y in zip(now, slices(t - 1, 0))]
                source.append(jnp.concatenate([low + now[0], high + now[1]], axis=1))
            source.append(jnp.concatenate(slices(total - 1, 0), axis=1))
            modal = by_table(jnp.concatenate(source, axis=0), cos_t_v)
            reach = sum(modal[t * group:(t + 1) * group] * slope[t, span] for t in range(total))
            last_rho = jnp.where(right, 0.0, modal[total * group:])
            cut[0, k] = pivots[total - 1, span] * reach - last_rho
            if k == 0:
                pl.when(half == 0)(lambda: pl.semaphore_wait(ready.at[1], 1))
            swap(k).start()
            steps[:, span] = modal[:total * group].reshape(total, group, count)
            ends.append(last_rho)

        value = jnp.zeros((full, count), jnp.float32)
        for i in range(total):
            value = (steps[start + stride * i] + value) * pivots[i]
            steps[start + stride * i] = value
        reached = value
        rest = jnp.zeros((full, count), jnp.float32)
        steps[start + stride * (total - 1)] = rest
        for i in reversed(range(total - 1)):
            rest = steps[start + stride * i] + pivots[i] * rest
            steps[start + stride * i] = rest

        out_kinds(place, side, lambda first, size: settle(outgoing, CHUNKS * (total - 1) * size, out_sem.at[0]))
        near_edge = cos_t_v[:, rows - 8:rows + 8]
        pl.semaphore_wait(ready.at[0], total)

        def put(k, t, block, brink):
            for core in range(2):
                piece = block[:, core * rows:(core + 1) * rows]
                zero = (2 * k + core) * total
                if t < total:
                    first = (zero + t) * stride_rows
                    back[first + group:first + 2 * group] = piece
                    back[first + 2 * group:first + filled] = brink[8 - core:9 - core]
                if t > 0:
                    first = (zero + t - 1) * stride_rows
                    back[first:first + group] = piece

        def send_back(k, chip, core):
            back_kinds(base + chip, core, lambda first, size: homeward(k, chip, core, first, size).start())

        for k in chunks:
            span = slice(k * group, (k + 1) * group)
            swap(k).wait_recv()
            value, last_rho = reached[span], ends[k]
            pivot = pivots[total - 1, span]
            beyond = cut[1, k] - pivot * last_rho
            value = (value + pivot * beyond) * inverse[span]
            leading = steps[0, span] + slope[0, span] * value
            put(k, 0, by_table(leading, cos_v),
                table_by_t(near_edge, jnp.concatenate([leading] * total, axis=0)))

            @pl.when(half == 0)
            def _():
                homeward(k, 0, 0, group, group + 1).start()

                @pl.when(me != 0)
                def _():
                    homeward(k, 0, 1, group, group + 1).start()

            lines = [leading] + [steps[t, span] + slope[t, span] * value for t in range(1, total)]
            lines.append(jnp.where(right, 0.0, beyond + pivot * value))
            brink = table_by_t(near_edge, jnp.concatenate(lines[:total], axis=0))
            halfback = by_table(jnp.concatenate(lines[1:], axis=0), cos_v)
            for t in range(1, total + 1):
                put(k, t, halfback[(t - 1) * group:t * group], brink)
            for chip in others:
                @pl.when(base + chip != 0)
                def _():
                    send_back(k, chip, 0)
                    send_back(k, chip, 1)

            @pl.when(place != 0)
            def _():
                send_back(k, me, 0)

            mine = (2 * k + 1) * total + me
            home[place_of(k * total + me, group, group + 8)] = back[place_of(mine, group, group + 8)]

            @pl.when(jnp.logical_not(small))
            def _():
                home[place_of(k * total + me, 0, group)] = back[place_of(mine, 0, group)]

    pl.when(solving)(solve)
    returned = 2 * (group + 1) + (total - 1) * (filled + 2 * group)
    pl.when(side == 0)(lambda: back_kinds(
        place, side, lambda first, size: settle(home, CHUNKS * total * size, back_sem.at[1])))
    pl.when(solving)(lambda: back_kinds(
        place, side, lambda first, size: settle(home, CHUNKS * (total - 1) * size, back_sem.at[1])))

    def modes(first):
        spans = [(k * total + block) * stride_rows + first for block in range(total) for k in chunks]
        return jnp.concatenate([home[at:at + group] for at in spans], axis=0)

    here = modes(group)
    offset = lax.rem(total - me, total) * group
    row_at = lax.broadcasted_iota(jnp.int32, (per, rows), 0)
    lane_at = lax.broadcasted_iota(jnp.int32, (per, rows), 1)

    def find_edge():
        strip = []
        for part in range(count // rows):
            placed = jnp.zeros((per, rows), jnp.float32)
            for k in chunks:
                tail = home[pl.ds((k * total + part * per) * stride_rows + 2 * group, per, stride=stride_rows)]
                tail = jnp.where(lane_at < group, pltpu.roll(tail, offset, 1), 0.0)
                for d in range(per):
                    shift = d * full + k * group
                    placed = placed + jnp.where(row_at == d, pltpu.roll(tail, shift, 1) if shift else tail, 0.0)
            strip.append(jnp.broadcast_to(jnp.sum(placed, axis=0, keepdims=True), (8, rows)))
        return by_table(jnp.concatenate(strip, axis=1), cos_v)[:1]

    upper = jnp.full((1, count), side, jnp.int32) == 0

    @pl.when(place != 0)
    def _():
        values = by_table_tn(jnp.concatenate([here, here - modes(0)], axis=1), cos_v)
        edge = find_edge()
        pot = values[:rows]
        fields[0] = pot
        fields[1] = values[rows:]
        beyond_row[...] = jnp.broadcast_to(jnp.where(upper, edge, pot[rows - 1:]), beyond_row.shape)

    @pl.when(place == 0)
    def _():
        edge = find_edge()
        pot = by_table_tn(here, cos_v)
        fields[0] = pot
        before_first = jnp.where(upper, pot[:1], edge)
        after_last = jnp.where(upper, edge, pot[rows - 1:])
        beyond_row[...] = jnp.broadcast_to(after_last, beyond_row.shape)
        left_of = jnp.where(col == 0, pot, pltpu.roll(pot, 1, 1))
        right_of = jnp.where(col == count - 1, pot, pltpu.roll(pot, count - 1, 1))
        over = jnp.where(row == 0, before_first, pltpu.roll(pot, 1, 0))
        under = jnp.where(row == rows - 1, after_last, pltpu.roll(pot, rows - 1, 0))
        bend = (pot - left_of) + (pot - right_of) + (pot - over) + (pot - under)
        following = (2.0 + regular_shift) * pot + space_weight * bend - first_source[...]
        fields[1] = pot - following

    pl.when(solving)(lambda: settle(cut.at[0], CHUNKS, cut_sem.at[CHUNKS]))
    pl.when(solving)(lambda: back_kinds(
        place, side, lambda first, size: settle(back, CHUNKS * (returned - size), back_sem.at[0])))
    pl.when(side == 0)(lambda: out_kinds(
        place, side, lambda first, size: settle(outgoing, CHUNKS * total * size, out_sem.at[0])))


def finish_kernel(rho, mx, my, fields, beyond_row, out_d, out_x, out_y, results, store_sem):
    rows, count = rho.shape
    row = lax.broadcasted_iota(jnp.int32, (rows, count), 0)
    col = lax.broadcasted_iota(jnp.int32, (rows, count), 1)
    saves = [
        pltpu.make_async_copy(results.at[i], out.at[0], store_sem.at[0])
        for i, out in enumerate((out_d, out_x, out_y))
    ]
    results[0] = rho[...] - fields[1]
    saves[0].start()
    here = fields[0]
    after = jnp.where(row == rows - 1, beyond_row[0:1], pltpu.roll(here, rows - 1, 0))
    results[1] = mx[...] - flux_weight * (after - here)
    saves[1].start()
    grad = jnp.where(col == count - 1, 0.0, pltpu.roll(here, count - 1, 1) - here)
    results[2] = my[...] - flux_weight * grad
    saves[2].start()
    pltpu.make_async_copy(results, results, store_sem.at[0]).wait()


def per_device_kernel(density, flux_x, flux_y):
    rows, count = density.shape[1:]
    total = lax.axis_size("tm") // 2
    group = count // total
    tables = host_tables(count, total)
    f32, bf16 = jnp.float32, jnp.bfloat16
    vm = pltpu.VMEM
    dma = pltpu.SemaphoreType.DMA
    slab = vm((rows, count), f32)
    tall = total * (2 * group + 8 * CHUNKS)
    spare = 2 * group // CHUNKS + 8
    scratch = [
        vm((1, 3, rows, count), f32), vm((2, count, count), bf16), vm((2, count, count), bf16), vm((group, count), f32),
        slab, vm((8, count), f32), vm((tall, rows), f32), vm((2 * tall + 2 * spare, rows), f32),
        vm((total, group, count), f32), vm((total, group, count), f32), vm((total, group, count), f32),
        vm((2, CHUNKS, group // CHUNKS, count), f32),
        vm((2 * tall, rows), f32), vm((tall + spare, rows), f32),
        pltpu.SemaphoreType.REGULAR((2,)), dma((4,)), dma((2,)), dma((1 + CHUNKS,)), dma((1 + CHUNKS,)), dma((2,)),
    ]
    anywhere = pl.BlockSpec(memory_space=pl.ANY)

    def kernel(*refs):
        step_kernel(total, *refs)

    local = pl.BlockSpec(memory_space=pltpu.VMEM)
    held = pl.pallas_call(
        kernel,
        out_shape=[slab, slab, slab, vm((2, rows, count), f32), vm((8, count), f32)],
        in_specs=[anywhere] * 6,
        out_specs=[local] * 5,
        scratch_shapes=scratch,
        compiler_params=pltpu.CompilerParams(collective_id=0, has_side_effects=True),
    )(density, flux_x, flux_y, *tables)
    return pl.pallas_call(
        finish_kernel,
        out_shape=[jax.ShapeDtypeStruct(density.shape, f32)] * 3,
        in_specs=[local] * 5,
        out_specs=[anywhere] * 3,
        scratch_shapes=[vm((3, rows, count), f32), dma((1,))],
    )(*[pltpu.with_memory_space_constraint(x, pltpu.VMEM) for x in held])


def per_device(density, flux_x, flux_y):
    slabs, rows, count = density.shape
    size = lax.axis_size("tm")
    fits = (
        slabs == 1 and lax.axis_size("space") == 2 and size >= 2 and size & (size - 1) == 0
        and count % (8 * size) == 0 and rows == 128 and 2 * rows == count
    )
    return (per_device_kernel if fits else per_device_xla)(density, flux_x, flux_y)


def solution(mesh):
    return jax.shard_map(
        per_device,
        mesh=mesh,
        in_specs=(P("tm", "space", None), P("tm", "space", None), P("tm", "space", None)),
        out_specs=(P("tm", "space", None), P("tm", "space", None), P("tm", "space", None)),
        check_vma=False,
    )
```
